1024 devices in a mesh: gx: 8 (over y), gy: 4 (over x), gz: 32 (over z, core).
Axes of the slice: x: 4, y: 8, z: 16, core: 2. Of those that a mesh axis runs over, the one named last changes fastest.
Arguments:
- adjoint_state: float32 [3, 64, 64, 4096], P(None, 'gx', 'gy', 'gz'), may hold values from -20 to 20
- base_flow: bfloat16 [3, 64, 64, 4096], P(None, 'gx', 'gy', 'gz'), may hold values from -4 to 4
- base_grads: bfloat16 [9, 64, 64, 4096], P(None, 'gx', 'gy', 'gz'), may hold values from -3 to 3
- sponge: float32 [64, 64, 4096], P('gx', 'gy', 'gz'), may hold values from 0.5 to 8
Outputs:
- solution: float32 [3, 64, 64, 4096], P(None, 'gx', 'gy', 'gz')
The draws below stay inside these ranges and needn't reach their ends.
All inputs are finite; a program needn't handle non-finite values.
Results may differ from the reference program's by a relative error of at most 0.0004.
Values sent between devices are 32-bit elements; how exact they have to be, the bound alone decides.
No kernel may reach another device: no remote copies, remote signals or barrier semaphores. Data moves between devices by JAX's collectives and lax.ppermute only.
A program may use at most 32 MiB of HBM per device.

```python
import math
import jax
import jax.numpy as jnp
import numpy as np
from jax import lax

ITERS = 2
NX = 64
NY = 64
NZ = 4096


def draw_adjoint_state(key, part):
    zpos = jnp.arange(NZ, dtype=jnp.float32) / (NZ - 1)
    zramp = jnp.exp(jnp.log(3.0) * zpos)[None, None, None, :]
    rough = jnp.clip(jax.random.normal(key, (3, NX, NY, NZ), jnp.float32), -4.0, 4.0)
    return rough * zramp


def block_levels(stream_key, extent, cuts, low, high):
    gain = 1.0
    for axis_at, blocks in cuts:
        draws = jax.random.uniform(jax.random.fold_in(jax.random.fold_in(stream_key, 6), axis_at), (blocks,), jnp.float32, low / len(cuts), high / len(cuts))
        gain = gain * jnp.repeat(jnp.exp(draws), extent[axis_at] // blocks).reshape((-1,) + (1,) * (len(extent) - 1 - axis_at))
    return gain


def scatter_about(own_key, extent, deviation, reach, cuts=(), kind=jnp.bfloat16):
    loudness = block_levels(own_key, extent, cuts, -0.22, 0.18) if cuts else 1.0
    drawn = jax.random.normal(own_key, extent, jnp.float32) * deviation * loudness
    return jnp.minimum(jnp.maximum(drawn, -reach), reach).astype(kind)


def setup_inputs(seed: int = 0) -> dict:
    splits = jax.random.split(jax.random.key(seed), 5)
    adjoint_state = draw_adjoint_state(jax.random.fold_in(splits[4], 71), 0)
    base_flow = scatter_about(splits[1], (3, NX, NY, NZ), 1.0, 4.0, ((1, 8), (2, 4), (3, 32)))
    base_grads = scatter_about(splits[2], (9, NX, NY, NZ), 0.5, 3.0, ((1, 8), (2, 4), (3, 32)))
    sponge = jnp.clip(jnp.exp(math.log(8.0) - 2.7725887 * jax.random.uniform(splits[3], (NX, NY, NZ), jnp.float32) ** block_levels(splits[3], (NX, NY, NZ), ((0, 8), (1, 4), (2, 32)), -0.2, 0.2)), 0.5, 8.0)
    return {"adjoint_state": adjoint_state, "base_flow": base_flow, "base_grads": base_grads, "sponge": sponge}


inverse_step = 2.0
viscosity = 0.05


def gll_tables():
    degree = 7
    interior = np.array([-0.8717401485096066, -0.5917001814331423, -0.2092992179024789, 0.2092992179024789, 0.5917001814331423, 0.8717401485096066])
    points = np.concatenate([[-1.0], interior, [1.0]])
    previous = np.ones(8)
    current = points * 1.0
    for degree_now in range(1, degree):
        following = ((2 * degree_now + 1) * points * current - degree_now * previous) / (degree_now + 1)
        previous = current
        current = following
    end_poly = current
    weights = 2.0 / (degree * (degree + 1) * end_poly ** 2)
    matrix = np.zeros((8, 8))
    for row_idx in range(8):
        for col_idx in range(8):
            if row_idx != col_idx:
                matrix[row_idx, col_idx] = end_poly[row_idx] / (end_poly[col_idx] * (points[row_idx] - points[col_idx]))
    matrix[0, 0] = -degree * (degree + 1) / 4.0
    matrix[7, 7] = degree * (degree + 1) / 4.0
    return weights, matrix


def grad_x(field, matrix):
    dims_all = field.shape
    lead = dims_all[:-3]
    blocks = field.reshape(lead + (dims_all[-3] // 8, 8, dims_all[-2], dims_all[-1]))
    return jnp.einsum('ab,...ebyz->...eayz', matrix, blocks, precision=lax.Precision.HIGHEST).reshape(dims_all)


def grad_y(field, matrix):
    dims_all = field.shape
    lead = dims_all[:-3]
    blocks = field.reshape(lead + (dims_all[-3], dims_all[-2] // 8, 8, dims_all[-1]))
    return jnp.einsum('ab,...xebz->...xeaz', matrix, blocks, precision=lax.Precision.HIGHEST).reshape(dims_all)


def grad_z(field, matrix):
    dims_all = field.shape
    lead = dims_all[:-3]
    blocks = field.reshape(lead + (dims_all[-3], dims_all[-2], dims_all[-1] // 8, 8))
    return jnp.einsum('ab,...xyeb->...xyea', matrix, blocks, precision=lax.Precision.HIGHEST).reshape(dims_all)


def twin_pass(extended, axis):
    count = extended.shape[axis] - 2
    middle = lax.slice_in_dim(extended, 1, count + 1, axis=axis)
    after = lax.slice_in_dim(extended, 2, count + 2, axis=axis)
    before = lax.slice_in_dim(extended, 0, count, axis=axis)
    position = jnp.arange(count) % 8
    bshape = (count,) + (1,) * (-axis - 1)
    upper = (position == 7).reshape(bshape)
    lower = (position == 0).reshape(bshape)
    return middle + jnp.where(upper, after, 0.0) + jnp.where(lower, before, 0.0)


def dim_factors(count, start, total):
    global_pos = start + jnp.arange(count)
    position = jnp.arange(count) % 8
    border = (global_pos == 0) | (global_pos == total - 1)
    keep_dim = jnp.where(border, 0.0, 1.0).astype(jnp.float32)
    twin = ((position == 0) | (position == 7)) & jnp.logical_not(border)
    share = jnp.where(twin, 0.5, 1.0).astype(jnp.float32)
    return keep_dim, share


def node_masks(sizes_xyz, starts, totals):
    keep_x, share_x = dim_factors(sizes_xyz[0], starts[0], totals[0])
    keep_y, share_y = dim_factors(sizes_xyz[1], starts[1], totals[1])
    keep_z, share_z = dim_factors(sizes_xyz[2], starts[2], totals[2])
    keep = keep_x[:, None, None] * keep_y[None, :, None] * keep_z[None, None, :]
    weight = keep * (share_x[:, None, None] * share_y[None, :, None] * share_z[None, None, :])
    return keep, weight


def mass_nodes(sizes_xyz, weights):
    mass_x = jnp.tile(weights, sizes_xyz[0] // 8)
    mass_y = jnp.tile(weights, sizes_xyz[1] // 8)
    mass_z = jnp.tile(weights, sizes_xyz[2] // 8)
    return mass_x[:, None, None] * mass_y[None, :, None] * mass_z[None, None, :]


def assemble_whole(field):
    for axis in (-3, -2, -1):
        padding = [(0, 0)] * field.ndim
        padding[field.ndim + axis] = (1, 1)
        field = twin_pass(jnp.pad(field, padding), axis)
    return field


def reference(adjoint_state, base_flow, base_grads, sponge):
    weights_np, matrix_np = gll_tables()
    weights = jnp.asarray(weights_np, jnp.float32)
    deriv = jnp.asarray(matrix_np, jnp.float32)
    deriv_t = jnp.asarray(matrix_np.T, jnp.float32)
    sizes_xyz = adjoint_state.shape[1:]
    mass3 = mass_nodes(sizes_xyz, weights)
    keep, weight = node_masks(sizes_xyz, (0, 0, 0), sizes_xyz)
    flow = base_flow.astype(jnp.float32)
    grads = base_grads.astype(jnp.float32)
    sponge_term = mass3 * (inverse_step + sponge)

    def forcing_comp(comp):
        velocity = adjoint_state[comp]
        transport = flow[0] * grad_x(velocity, deriv) + flow[1] * grad_y(velocity, deriv) + flow[2] * grad_z(velocity, deriv)
        coupling = grads[3 * comp] * adjoint_state[0] + grads[3 * comp + 1] * adjoint_state[1] + grads[3 * comp + 2] * adjoint_state[2]
        local = mass3 * (inverse_step * velocity + transport - coupling)
        return keep * assemble_whole(local)

    forcing = jnp.stack([forcing_comp(comp) for comp in range(3)])

    def helm_one(field):
        stiff = grad_x(mass3 * grad_x(field, deriv), deriv_t) + grad_y(mass3 * grad_y(field, deriv), deriv_t)
        stiff = stiff + grad_z(mass3 * grad_z(field, deriv), deriv_t)
        local = sponge_term * field + viscosity * stiff
        return keep * assemble_whole(local)

    def helmholtz(field):
        return lax.map(helm_one, field)

    def inner(left, right):
        return jnp.sum(weight * left * right)

    solution = jnp.zeros_like(forcing)
    residual = forcing
    direction = forcing
    norm_now = inner(residual, residual)
    for step in range(ITERS):
        image = helmholtz(direction)
        alpha = norm_now / inner(direction, image)
        solution = solution + alpha * direction
        if step + 1 < ITERS:
            residual = residual - alpha * image
            norm_next = inner(residual, residual)
            direction = residual + (norm_next / norm_now) * direction
            norm_now = norm_next
    return solution
```

```python
import functools

import jax
import jax.numpy as jnp
import numpy as np
from jax import lax
from jax.experimental import pallas as pl
from jax.experimental.pallas import tpu as pltpu
from jax.sharding import PartitionSpec as P

inverse_step = 2.0
viscosity = 0.05
F32 = jnp.float32
BF16 = jnp.bfloat16
NODES = 8


def gll_tables():
    degree = 7
    interior = np.array(
        [
            -0.8717401485096066,
            -0.5917001814331423,
            -0.2092992179024789,
            0.2092992179024789,
            0.5917001814331423,
            0.8717401485096066,
        ]
    )
    points = np.concatenate([[-1.0], interior, [1.0]])
    previous = np.ones(8)
    current = points * 1.0
    for degree_now in range(1, degree):
        following = ((2 * degree_now + 1) * points * current - degree_now * previous) / (
            degree_now + 1
        )
        previous = current
        current = following
    weights = 2.0 / (degree * (degree + 1) * current**2)
    matrix = np.zeros((8, 8))
    for row_idx in range(8):
        for col_idx in range(8):
            if row_idx != col_idx:
                matrix[row_idx, col_idx] = current[row_idx] / (
                    current[col_idx] * (points[row_idx] - points[col_idx])
                )
    matrix[0, 0] = -degree * (degree + 1) / 4.0
    matrix[7, 7] = degree * (degree + 1) / 4.0
    return (weights, matrix)


W1, D1 = gll_tables()
W1 = W1.astype(np.float32).astype(np.float64)
D1 = D1.astype(np.float32).astype(np.float64)
K1 = D1.T @ (W1[:, None] * D1)


def block_diag(small, count):
    return np.kron(np.eye(count), small)


def twin_matrix(length):
    out = np.eye(length)
    for i in range(NODES - 1, length - 1, NODES):
        out[i, i + 1] = 1.0
        out[i + 1, i] = 1.0
    return out


def assembled_stiffness(length):
    out = twin_matrix(length) @ block_diag(K1, length // NODES)
    out[0, 0] += K1[7, 7]
    out[-1, -1] += K1[0, 0]
    return out


def assembled_weights(length):
    out = np.tile(W1, length // NODES)
    out[0::NODES] *= 2.0
    out[NODES - 1 :: NODES] *= 2.0
    return out


def halves(matrix):
    high = matrix.astype(np.float32).astype(BF16)
    low = (matrix - high.astype(np.float64)).astype(np.float32).astype(BF16)
    return np.asarray(high), np.asarray(low)


def left_operand(matrix):
    high, low = halves(matrix)
    zero = np.zeros_like(low)
    return np.concatenate(
        [np.concatenate([high, high], 1), np.concatenate([low, zero], 1)], 0
    )


def right_operand(matrix):
    high, low = halves(matrix)
    zero = np.zeros_like(low)
    return np.concatenate(
        [np.concatenate([high, low], 1), np.concatenate([high, zero], 1)], 0
    )


def split(x):
    high = x.astype(BF16)
    low = (x - high.astype(F32)).astype(BF16)
    return high, low


def mul_left(operand, x):
    rows = operand.shape[0] // 2
    high, low = split(x)
    out = jnp.dot(operand, jnp.concatenate([high, low], 0), preferred_element_type=F32)
    return out[:rows] + out[rows:]


def mul_right(x, operand):
    cols = operand.shape[1] // 2
    high, low = split(x)
    out = jnp.dot(jnp.concatenate([high, low], 1), operand, preferred_element_type=F32)
    return out[:, :cols] + out[:, cols:]


def twin_z(x):
    length = x.shape[-1]
    lane = lax.broadcasted_iota(jnp.int32, x.shape, 1)
    after = pltpu.roll(x, length - 1, 1)
    before = pltpu.roll(x, 1, 1)
    spot = lane & (NODES - 1)
    upper = (spot == NODES - 1) & (lane != length - 1)
    lower = (spot == 0) & (lane != 0)
    return x + jnp.where(upper, after, 0.0) + jnp.where(lower, before, 0.0)


def twin_y(x):
    first, second = x[:, :8], x[:, 8:]
    row = lax.broadcasted_iota(jnp.int32, first.shape, 1)
    one = first + jnp.where(row == 7, second[:, 0:1], 0.0)
    two = second + jnp.where(row == 0, first[:, 7:8], 0.0)
    return jnp.concatenate([one, two], 1)


def forcing_kernel(
    nx, adj, flow, grads, sponge, mass, dy, dz, field, drag, right, left, right2, left2
):
    ix = lax.axis_index("gx")
    a = adj[...]
    _, sx, sy, sz = a.shape
    rows = sx * sy
    m = mass[...]
    grad_z = mul_right(a.reshape(3 * rows, sz), dz[...]).reshape(3, rows, sz)
    s_local = m * (inverse_step + sponge[...].reshape(rows, sz))
    s_asm = twin_z(twin_y(s_local.reshape(sx, sy, sz)).reshape(rows, sz))
    drag[...] = s_asm
    right[6] = s_asm[(sx - 1) * sy :]
    left[6] = s_asm[:sy]
    fl = [flow[j].astype(F32).reshape(rows, sz) for j in range(3)]
    flat = a.reshape(3, rows, sz)
    low_edge = jnp.where(ix == 0, 0.0, float(K1[7, 0])).astype(F32)
    high_edge = jnp.where(ix == nx - 1, 0.0, float(K1[0, 7])).astype(F32)
    for c in range(3):
        grad_y = mul_left(dy[...], flat[c])
        planes = [a[c, i] for i in range(sx)]
        grad_x = []
        for i in range(sx):
            total = float(D1[i, 0]) * planes[0]
            for k in range(1, sx):
                total = total + float(D1[i, k]) * planes[k]
            grad_x.append(total)
        grad_x = jnp.concatenate(grad_x, 0)
        local = inverse_step * flat[c]
        local = local + fl[0] * grad_x + fl[1] * grad_y + fl[2] * grad_z[c]
        for j in range(3):
            local = local - grads[3 * c + j].astype(F32).reshape(rows, sz) * flat[j]
        local = m * local
        out = twin_z(twin_y(local.reshape(sx, sy, sz)).reshape(rows, sz))
        field[c] = out
        plane = [out[i * sy : (i + 1) * sy] for i in range(sx)]
        up = low_edge * plane[0]
        for i in range(1, sx - 1):
            up = up + float(K1[7, i]) * plane[i]
        down = high_edge * plane[sx - 1]
        for i in range(1, sx - 1):
            down = down + float(K1[0, i]) * plane[i]
        right[c] = plane[sx - 1]
        right[3 + c] = up
        left[c] = plane[0]
        left[3 + c] = down
        right2[c] = plane[sx - 1]
        left2[c] = plane[0]


def x_stage_kernel(
    field, drag, from_low, from_high, from_low2, from_high2, ext, drag_out, up, down
):
    sy, sz = from_low.shape[1:]
    rows = field.shape[1]
    sx = rows // sy
    drag_out[...] = drag[...]
    drag_out[:sy] = drag[:sy] + from_low[6]
    drag_out[rows - sy :] = drag[rows - sy :] + from_high[6]
    count = 2 * sx
    for c in range(3):
        ext[c, :rows] = field[c]
        ext[c, :sy] = field[c, :sy] + from_low[c]
        ext[c, rows - sy : rows] = field[c, rows - sy :] + from_high[c]
        ext[c, rows : rows + sy] = from_low[3 + c] + float(K1[7, 0]) * from_low2[c]
        ext[c, rows + sy : rows + 2 * sy] = (
            from_high[3 + c] + float(K1[0, 7]) * from_high2[c]
        )

        def row(y):
            return ext[c, pl.ds(y, sx, stride=sy), :]

        up[c * count : c * count + sx] = row(sy - 1)
        total = float(K1[7, 0]) * row(sy - 8)
        for k in range(1, 7):
            total = total + float(K1[7, k]) * row(sy - 8 + k)
        up[c * count + sx : (c + 1) * count] = total
        down[c * count : c * count + sx] = row(0)
        total = float(K1[0, 7]) * row(7)
        for k in range(1, 7):
            total = total + float(K1[0, k]) * row(k)
        down[c * count + sx : (c + 1) * count] = total
    base = 3 * count
    up[base : base + sx] = drag_out[pl.ds(sy - 1, sx, stride=sy), :]
    down[base : base + sx] = drag_out[pl.ds(0, sx, stride=sy), :]
    base += sx
    up[base : base + 8] = jnp.zeros((8, sz), F32)
    down[base : base + 8] = jnp.zeros((8, sz), F32)
    for c in range(3):
        for side in range(2):
            spot = rows + side * sy
            at = base + 2 * c + side
            up[at : at + 1] = ext[c, spot + sy - 1 : spot + sy]
            down[at : at + 1] = ext[c, spot : spot + 1]


def y_stage_kernel(ext, drag, from_low, from_high, pick, ext_out, drag_out, message):
    rows, sz = drag.shape
    sy = (ext.shape[1] - rows) // 2
    sx = rows // sy
    count = 2 * sx
    base = 3 * count
    drag_out[...] = drag[...]
    drag_out[pl.ds(0, sx, stride=sy), :] = (
        drag[pl.ds(0, sx, stride=sy), :] + from_low[base : base + sx]
    )
    drag_out[pl.ds(sy - 1, sx, stride=sy), :] = (
        drag[pl.ds(sy - 1, sx, stride=sy), :] + from_high[base : base + sx]
    )
    base += sx
    used = rows + 2 * sy
    size = ext_out.shape[1]
    for c in range(3):
        ext_out[c, :used] = ext[c]
        ext_out[c, pl.ds(0, sx, stride=sy), :] = (
            ext[c, pl.ds(0, sx, stride=sy), :] + from_low[c * count : c * count + sx]
        )
        ext_out[c, pl.ds(sy - 1, sx, stride=sy), :] = (
            ext[c, pl.ds(sy - 1, sx, stride=sy), :]
            + from_high[c * count : c * count + sx]
        )
        for side in range(2):
            spot = rows + side * sy
            at = base + 2 * c + side
            ext_out[c, spot : spot + 1] = ext[c, spot : spot + 1] + from_low[at : at + 1]
            ext_out[c, spot + sy - 1 : spot + sy] = (
                ext[c, spot + sy - 1 : spot + sy] + from_high[at : at + 1]
            )
        ext_out[c, used : used + sx] = from_low[c * count + sx : (c + 1) * count]
        ext_out[c, used + sx : used + 2 * sx] = from_high[c * count + sx : (c + 1) * count]
        ext_out[c, used + 2 * sx :] = jnp.zeros((size - used - 2 * sx, sz), F32)
    for c in range(3):
        message[:, c * size : (c + 1) * size] = lax.dot_general(
            pick[...],
            ext_out[c],
            (((1,), (1,)), ((), ())),
            precision=lax.Precision.HIGHEST,
            preferred_element_type=F32,
        )
    message[:, 3 * size :] = lax.dot_general(
        pick[...],
        drag_out[...],
        (((1,), (1,)), ((), ())),
        precision=lax.Precision.HIGHEST,
        preferred_element_type=F32,
    )


def keep_mask(shape, sy, counts):
    row = lax.broadcasted_iota(jnp.int32, shape, 0)
    z = lax.broadcasted_iota(jnp.int32, shape, 1)
    shift = sy.bit_length() - 1
    x = lax.shift_right_logical(row, shift)
    y = row & (sy - 1)
    sx = shape[0] // sy
    mask = None
    for axis, spot, size in (("gx", x, sx), ("gy", y, sy), ("gz", z, shape[1])):
        here = spot + lax.axis_index(axis) * size
        inside = (here != 0) & (here != counts[axis] * size - 1)
        mask = inside if mask is None else mask & inside
    return mask


def moments_kernel(
    counts,
    sy,
    ext,
    drag,
    sponge,
    from_low,
    from_high,
    place,
    plane_asm,
    line_asm,
    plane_own,
    line_own,
    mass,
    share,
    plane_weight_asm,
    line_weight_asm,
    plane_weight,
    line_weight,
    base,
    image,
    sums,
):
    rows, sz = drag.shape
    size = ext.shape[1]
    keep = keep_mask((rows, sz), sy, counts)
    lane = lax.broadcasted_iota(jnp.int32, from_low.shape, 0)
    both = jnp.where(lane < 2, from_low[...], from_high[...])
    high = both.astype(BF16)
    rest = both - high.astype(F32)
    mid = rest.astype(BF16)
    low = (rest - mid.astype(F32)).astype(BF16)
    parts = jnp.concatenate([high, mid, low], 0)
    add = lax.dot_general(
        parts, place[...], (((0,), (0,)), ((), ())), preferred_element_type=F32
    )
    s_asm = drag[...] + add[3 * size :, :sz]
    s_own = mass[...] * (inverse_step + sponge[...].reshape(rows, sz))
    halves_of = mass.shape[1]
    total = [jnp.zeros((1, sz), F32) for _ in range(4)]
    for c in range(3):
        whole = ext[c] + add[c * size : (c + 1) * size, :sz]
        v = jnp.where(keep, whole[:rows], 0.0)
        plane = mul_left(plane_asm[...], jnp.concatenate([v, whole[rows:]], 0))
        line = mul_right(v, line_asm[...]) + add[c * size : c * size + rows, sz:]
        stiff = plane * line_weight_asm[...] + line * plane_weight_asm[...]
        u = jnp.where(keep, s_asm * v + viscosity * stiff, 0.0)
        stiff = (
            mul_left(plane_own[...], u) * line_weight[...]
            + mul_right(u, line_own[...]) * plane_weight[...]
        )
        own = s_own * u + viscosity * stiff
        base[c] = v
        image[c] = u
        sv = share[...] * v
        su = share[...] * u
        for k, term in enumerate((sv * v, sv * u, su * u, u * own)):
            total[k] = total[k] + jnp.sum(term, axis=0, keepdims=True)
    spot = lax.broadcasted_iota(jnp.int32, (1, sz), 1)
    out = jnp.zeros((1, sz), F32)
    for k in range(4):
        out = jnp.where(spot == k, jnp.sum(total[k], axis=1, keepdims=True), out)
    sums[...] = jnp.broadcast_to(out, sums.shape)


def combine_kernel(base, image, sums, out):
    total = jnp.sum(sums[...], axis=0, keepdims=True)
    m0, m1, m2, m3 = (total[:, k : k + 1] for k in range(4))
    alpha = m0 / m1
    norm = m0 - 2.0 * alpha * m1 + alpha * alpha * m2
    grow = 1.0 + norm / m0
    bend = grow * grow * m1 - 2.0 * grow * alpha * m2 + alpha * alpha * m3
    alpha2 = norm / bend
    one = alpha + alpha2 * grow
    two = alpha * alpha2
    for c in range(3):
        out[c] = one * base[c] - two * image[c]


VMEM = pl.BlockSpec(memory_space=pltpu.VMEM)


def call(kernel, operands, outs, flops=1_000_000):
    shapes = [jax.ShapeDtypeStruct(s, F32) for s in outs]
    size = sum(4 * int(np.prod(s)) for s in outs) + sum(
        o.dtype.itemsize * o.size for o in operands
    )
    return pl.pallas_call(
        kernel,
        out_shape=shapes,
        in_specs=[VMEM] * len(operands),
        out_specs=[VMEM] * len(outs),
        compiler_params=pltpu.CompilerParams(vmem_limit_bytes=16 * 1024 * 1024),
        cost_estimate=pl.CostEstimate(
            flops=flops, bytes_accessed=size, transcendentals=0
        ),
    )(*operands)


def shift(x, axis, step):
    count = lax.axis_size(axis)
    pairs = [(i, i + step) for i in range(count) if 0 <= i + step < count]
    return lax.ppermute(x, axis, pairs)


def body(adjoint_state, base_flow, base_grads, sponge):
    _, sx, sy, sz = adjoint_state.shape
    rows = sx * sy
    size = 2 * rows
    used = rows + 2 * sy
    counts = {axis: lax.axis_size(axis) for axis in ("gx", "gy", "gz")}
    wx, wy, wz = W1, np.tile(W1, sy // NODES), np.tile(W1, sz // NODES)
    ax, ay, az = (assembled_weights(n) for n in (sx, sy, sz))

    def f32(x):
        return jnp.asarray(x.astype(np.float32))

    def over_plane(x, y):
        return f32(np.broadcast_to(np.kron(x, y)[:, None], (rows, sz)))

    mass = f32(np.kron(wx, wy)[:, None] * wz[None, :])
    ends = np.ones(NODES)
    ends[0] = ends[-1] = 0.5
    share = f32(
        np.kron(ends, np.tile(ends, sy // NODES))[:, None]
        * np.tile(ends, sz // NODES)[None, :]
    )
    dy = jnp.asarray(left_operand(block_diag(D1, rows // NODES)))
    dz = jnp.asarray(right_operand(block_diag(D1, sz // NODES).T))
    field, drag, right, left, right2, left2 = call(
        functools.partial(forcing_kernel, counts["gx"]),
        (adjoint_state, base_flow, base_grads, sponge, mass, dy, dz),
        [(3, rows, sz), (rows, sz)] + [(7, sy, sz)] * 2 + [(3, sy, sz)] * 2,
    )
    x_low2 = shift(right2, "gx", 2)
    x_high2 = shift(left2, "gx", -2)
    x_low = shift(right, "gx", 1)
    x_high = shift(left, "gx", -1)
    message_rows = 7 * sx + 8
    ext, drag, up, down = call(
        x_stage_kernel,
        (field, drag, x_low, x_high, x_low2, x_high2),
        [(3, used, sz), (rows, sz), (message_rows, sz), (message_rows, sz)],
    )
    y_low = shift(up, "gy", 1)
    y_high = shift(down, "gy", -1)
    pick = np.zeros((8, sz))
    pick[0, sz - 1] = 1.0
    pick[1, sz - 8 : sz - 1] = K1[7, :7]
    pick[2, 0] = 1.0
    pick[3, 1:8] = K1[0, 1:]
    ext, drag, message = call(
        y_stage_kernel,
        (ext, drag, y_low, y_high, f32(pick)),
        [(3, size, sz), (rows, sz), (8, 3 * size + rows)],
    )
    z_low = shift(message, "gz", 1)
    z_high = shift(message, "gz", -1)

    place = np.zeros((8, 2 * sz))
    place[0, 0] = place[1, sz] = place[2, sz - 1] = place[3, 2 * sz - 1] = 1.0
    place = jnp.asarray(np.tile(place, (3, 1)).astype(np.float32).astype(BF16))
    plane_asm = np.zeros((rows, size))
    plane_asm[:, :rows] = np.kron(assembled_stiffness(sx), np.diag(ay)) + np.kron(
        np.diag(ax), assembled_stiffness(sy)
    )
    for y in range(sy):
        plane_asm[y, rows + y] = ay[y]
        plane_asm[rows - sy + y, rows + sy + y] = ay[y]
    for x in range(sx):
        plane_asm[x * sy, used + x] = ax[x]
        plane_asm[x * sy + sy - 1, used + sx + x] = ax[x]
    plane_own = np.kron(K1, np.diag(wy)) + np.kron(
        np.diag(wx), block_diag(K1, sy // NODES)
    )
    slots = counts["gz"]
    base, image, sums = call(
        functools.partial(moments_kernel, counts, sy),
        (
            ext,
            drag,
            sponge,
            z_low,
            z_high,
            place,
            jnp.asarray(left_operand(plane_asm)),
            jnp.asarray(right_operand(assembled_stiffness(sz).T)),
            jnp.asarray(left_operand(plane_own)),
            jnp.asarray(right_operand(block_diag(K1, sz // NODES).T)),
            mass,
            share,
            over_plane(ax, ay),
            f32(az[None, :]),
            over_plane(wx, wy),
            f32(wz[None, :]),
        ),
        [(3, rows, sz), (3, rows, sz), (slots, sz)],
    )
    sums = lax.all_to_all(sums, "gz", 0, 0, tiled=True)
    sums = jnp.sum(sums, axis=0, keepdims=True)
    slots = counts["gx"] * counts["gy"]
    sums = jnp.broadcast_to(sums, (slots, sz))
    sums = lax.all_to_all(sums, ("gx", "gy"), 0, 0, tiled=True)
    (out,) = call(combine_kernel, (base, image, sums), [(3, rows, sz)])
    return out.reshape(3, sx, sy, sz)


def solution(mesh):
    placed = (
        P(None, "gx", "gy", "gz"),
        P(None, "gx", "gy", "gz"),
        P(None, "gx", "gy", "gz"),
        P("gx", "gy", "gz"),
    )
    return jax.shard_map(
        body, mesh=mesh, in_specs=placed, out_specs=P(None, "gx", "gy", "gz"), check_vma=False
    )
```

```python
import functools

import jax
import jax.numpy as jnp
import numpy as np
from jax import lax
from jax.experimental import pallas as pl
from jax.experimental.pallas import tpu as pltpu
from jax.sharding import PartitionSpec as P

inverse_step = 2.0
viscosity = 0.05
F32 = jnp.float32
BF16 = jnp.bfloat16
NODES = 8


def gll_tables():
    degree = 7
    interior = np.array(
        [
            -0.8717401485096066,
            -0.5917001814331423,
            -0.2092992179024789,
            0.2092992179024789,
            0.5917001814331423,
            0.8717401485096066,
        ]
    )
    points = np.concatenate([[-1.0], interior, [1.0]])
    previous = np.ones(8)
    current = points * 1.0
    for degree_now in range(1, degree):
        following = ((2 * degree_now + 1) * points * current - degree_now * previous) / (
            degree_now + 1
        )
        previous = current
        current = following
    weights = 2.0 / (degree * (degree + 1) * current**2)
    matrix = np.zeros((8, 8))
    for row_idx in range(8):
        for col_idx in range(8):
            if row_idx != col_idx:
                matrix[row_idx, col_idx] = current[row_idx] / (
                    current[col_idx] * (points[row_idx] - points[col_idx])
                )
    matrix[0, 0] = -degree * (degree + 1) / 4.0
    matrix[7, 7] = degree * (degree + 1) / 4.0
    return (weights, matrix)


W1, D1 = gll_tables()
W1 = W1.astype(np.float32).astype(np.float64)
D1 = D1.astype(np.float32).astype(np.float64)
K1 = D1.T @ (W1[:, None] * D1)


def block_diag(small, count):
    return np.kron(np.eye(count), small)


def twin_matrix(length):
    out = np.eye(length)
    for i in range(NODES - 1, length - 1, NODES):
        out[i, i + 1] = 1.0
        out[i + 1, i] = 1.0
    return out


def assembled_stiffness(length):
    out = twin_matrix(length) @ block_diag(K1, length // NODES)
    out[0, 0] += K1[7, 7]
    out[-1, -1] += K1[0, 0]
    return out


def assembled_weights(length):
    out = np.tile(W1, length // NODES)
    out[0::NODES] *= 2.0
    out[NODES - 1 :: NODES] *= 2.0
    return out


def halves(matrix):
    high = matrix.astype(np.float32).astype(BF16)
    low = (matrix - high.astype(np.float64)).astype(np.float32).astype(BF16)
    return np.asarray(high), np.asarray(low)


def left_operand(matrix):
    high, low = halves(matrix)
    zero = np.zeros_like(low)
    return np.concatenate(
        [np.concatenate([high, high], 1), np.concatenate([low, zero], 1)], 0
    )


def right_operand(matrix):
    high, low = halves(matrix)
    zero = np.zeros_like(low)
    return np.concatenate(
        [np.concatenate([high, low], 1), np.concatenate([high, zero], 1)], 0
    )


def split(x):
    high = x.astype(BF16)
    low = (x - high.astype(F32)).astype(BF16)
    return high, low


def mul_left(operand, x):
    rows = operand.shape[0] // 2
    high, low = split(x)
    out = jnp.dot(operand, jnp.concatenate([high, low], 0), preferred_element_type=F32)
    return out[:rows] + out[rows:]


def mul_right(x, operand):
    cols = operand.shape[1] // 2
    high, low = split(x)
    out = jnp.dot(jnp.concatenate([high, low], 1), operand, preferred_element_type=F32)
    return out[:, :cols] + out[:, cols:]


def twin_z(x):
    length = x.shape[-1]
    lane = lax.broadcasted_iota(jnp.int32, x.shape, 1)
    after = pltpu.roll(x, length - 1, 1)
    before = pltpu.roll(x, 1, 1)
    spot = lane & (NODES - 1)
    upper = (spot == NODES - 1) & (lane != length - 1)
    lower = (spot == 0) & (lane != 0)
    return x + jnp.where(upper, after, 0.0) + jnp.where(lower, before, 0.0)


def twin_y(x):
    first, second = x[:, :8], x[:, 8:]
    row = lax.broadcasted_iota(jnp.int32, first.shape, 1)
    one = first + jnp.where(row == 7, second[:, 0:1], 0.0)
    two = second + jnp.where(row == 0, first[:, 7:8], 0.0)
    return jnp.concatenate([one, two], 1)


def forcing_kernel(
    nx,
    adj_hbm,
    flow_hbm,
    grads_hbm,
    sponge_hbm,
    mass_hbm,
    dy_hbm,
    dz_hbm,
    field,
    drag,
    right,
    left,
    right2,
    left2,
    adj,
    flow,
    grads,
    sponge,
    mass,
    dy,
    dz,
    sems,
):
    copies = [
        pltpu.make_async_copy(src, dst, sems.at[k])
        for k, (src, dst) in enumerate(
            (
                (adj_hbm, adj),
                (dz_hbm, dz),
                (mass_hbm, mass),
                (sponge_hbm, sponge),
                (dy_hbm, dy),
                (flow_hbm, flow),
                (grads_hbm, grads),
            )
        )
    ]
    for copy in copies:
        copy.start()
    ix = lax.axis_index("gx")
    for copy in copies:
        copy.wait()
    a = adj[...]
    _, sx, sy, sz = a.shape
    rows = sx * sy
    m = mass[...]
    grad_z = mul_right(a.reshape(3 * rows, sz), dz[...]).reshape(3, rows, sz)
    s_local = m * (inverse_step + sponge[...].reshape(rows, sz))
    s_asm = twin_z(twin_y(s_local.reshape(sx, sy, sz)).reshape(rows, sz))
    drag[...] = s_asm
    right[6] = s_asm[(sx - 1) * sy :]
    left[6] = s_asm[:sy]
    fl = [flow[j].astype(F32).reshape(rows, sz) for j in range(3)]
    flat = a.reshape(3, rows, sz)
    low_edge = jnp.where(ix == 0, 0.0, float(K1[7, 0])).astype(F32)
    high_edge = jnp.where(ix == nx - 1, 0.0, float(K1[0, 7])).astype(F32)
    for c in range(3):
        grad_y = mul_left(dy[...], flat[c])
        planes = [a[c, i] for i in range(sx)]
        grad_x = []
        for i in range(sx):
            total = float(D1[i, 0]) * planes[0]
            for k in range(1, sx):
                total = total + float(D1[i, k]) * planes[k]
            grad_x.append(total)
        grad_x = jnp.concatenate(grad_x, 0)
        local = inverse_step * flat[c]
        local = local + fl[0] * grad_x + fl[1] * grad_y + fl[2] * grad_z[c]
        for j in range(3):
            local = local - grads[3 * c + j].astype(F32).reshape(rows, sz) * flat[j]
        local = m * local
        out = twin_z(twin_y(local.reshape(sx, sy, sz)).reshape(rows, sz))
        field[c] = out
        plane = [out[i * sy : (i + 1) * sy] for i in range(sx)]
        up = low_edge * plane[0]
        for i in range(1, sx - 1):
            up = up + float(K1[7, i]) * plane[i]
        down = high_edge * plane[sx - 1]
        for i in range(1, sx - 1):
            down = down + float(K1[0, i]) * plane[i]
        right[c] = plane[sx - 1]
        right[3 + c] = up
        left[c] = plane[0]
        left[3 + c] = down
        right2[c] = plane[sx - 1]
        left2[c] = plane[0]


def x_stage_kernel(
    field, drag, from_low, from_high, from_low2, from_high2, ext, drag_out, up, down
):
    sy, sz = from_low.shape[1:]
    rows = field.shape[1]
    sx = rows // sy
    drag_out[...] = drag[...]
    drag_out[:sy] = drag[:sy] + from_low[6]
    drag_out[rows - sy :] = drag[rows - sy :] + from_high[6]
    count = 2 * sx
    for c in range(3):
        ext[c, :rows] = field[c]
        ext[c, :sy] = field[c, :sy] + from_low[c]
        ext[c, rows - sy : rows] = field[c, rows - sy :] + from_high[c]
        ext[c, rows : rows + sy] = from_low[3 + c] + float(K1[7, 0]) * from_low2[c]
        ext[c, rows + sy : rows + 2 * sy] = (
            from_high[3 + c] + float(K1[0, 7]) * from_high2[c]
        )

        def row(y):
            return ext[c, pl.ds(y, sx, stride=sy), :]

        up[c * count : c * count + sx] = row(sy - 1)
        total = float(K1[7, 0]) * row(sy - 8)
        for k in range(1, 7):
            total = total + float(K1[7, k]) * row(sy - 8 + k)
        up[c * count + sx : (c + 1) * count] = total
        down[c * count : c * count + sx] = row(0)
        total = float(K1[0, 7]) * row(7)
        for k in range(1, 7):
            total = total + float(K1[0, k]) * row(k)
        down[c * count + sx : (c + 1) * count] = total
    base = 3 * count
    up[base : base + sx] = drag_out[pl.ds(sy - 1, sx, stride=sy), :]
    down[base : base + sx] = drag_out[pl.ds(0, sx, stride=sy), :]
    base += sx
    up[base : base + 8] = jnp.zeros((8, sz), F32)
    down[base : base + 8] = jnp.zeros((8, sz), F32)
    for c in range(3):
        for side in range(2):
            spot = rows + side * sy
            at = base + 2 * c + side
            up[at : at + 1] = ext[c, spot + sy - 1 : spot + sy]
            down[at : at + 1] = ext[c, spot : spot + 1]


def y_stage_kernel(ext, drag, from_low, from_high, pick, ext_out, drag_out, message):
    rows, sz = drag.shape
    sy = (ext.shape[1] - rows) // 2
    sx = rows // sy
    count = 2 * sx
    base = 3 * count
    drag_out[...] = drag[...]
    drag_out[pl.ds(0, sx, stride=sy), :] = (
        drag[pl.ds(0, sx, stride=sy), :] + from_low[base : base + sx]
    )
    drag_out[pl.ds(sy - 1, sx, stride=sy), :] = (
        drag[pl.ds(sy - 1, sx, stride=sy), :] + from_high[base : base + sx]
    )
    base += sx
    used = rows + 2 * sy
    size = ext_out.shape[1]
    for c in range(3):
        ext_out[c, :used] = ext[c]
        ext_out[c, pl.ds(0, sx, stride=sy), :] = (
            ext[c, pl.ds(0, sx, stride=sy), :] + from_low[c * count : c * count + sx]
        )
        ext_out[c, pl.ds(sy - 1, sx, stride=sy), :] = (
            ext[c, pl.ds(sy - 1, sx, stride=sy), :]
            + from_high[c * count : c * count + sx]
        )
        for side in range(2):
            spot = rows + side * sy
            at = base + 2 * c + side
            ext_out[c, spot : spot + 1] = ext[c, spot : spot + 1] + from_low[at : at + 1]
            ext_out[c, spot + sy - 1 : spot + sy] = (
                ext[c, spot + sy - 1 : spot + sy] + from_high[at : at + 1]
            )
        ext_out[c, used : used + sx] = from_low[c * count + sx : (c + 1) * count]
        ext_out[c, used + sx : used + 2 * sx] = from_high[c * count + sx : (c + 1) * count]
        ext_out[c, used + 2 * sx :] = jnp.zeros((size - used - 2 * sx, sz), F32)
    for c in range(3):
        message[:, c * size : (c + 1) * size] = lax.dot_general(
            pick[...],
            ext_out[c],
            (((1,), (1,)), ((), ())),
            precision=lax.Precision.HIGHEST,
            preferred_element_type=F32,
        )
    message[:, 3 * size :] = lax.dot_general(
        pick[...],
        drag_out[...],
        (((1,), (1,)), ((), ())),
        precision=lax.Precision.HIGHEST,
        preferred_element_type=F32,
    )


def keep_mask(shape, sy, counts):
    row = lax.broadcasted_iota(jnp.int32, shape, 0)
    z = lax.broadcasted_iota(jnp.int32, shape, 1)
    shift = sy.bit_length() - 1
    x = lax.shift_right_logical(row, shift)
    y = row & (sy - 1)
    sx = shape[0] // sy
    mask = None
    for axis, spot, size in (("gx", x, sx), ("gy", y, sy), ("gz", z, shape[1])):
        here = spot + lax.axis_index(axis) * size
        inside = (here != 0) & (here != counts[axis] * size - 1)
        mask = inside if mask is None else mask & inside
    return mask


def line_pattern(values, shape):
    spot = lax.broadcasted_iota(jnp.int32, shape, 1) & (NODES - 1)
    out = jnp.full(shape, float(values[0]), F32)
    for k in range(1, NODES):
        out = jnp.where(spot == k, float(values[k]), out)
    return out


def moments_kernel(
    counts,
    sy,
    ext,
    drag,
    sponge,
    from_low,
    from_high,
    place,
    plane_asm,
    line_asm,
    plane_own,
    line_own,
    mass,
    share,
    plane_weight_asm,
    plane_weight,
    base,
    image,
    sums,
):
    rows, sz = drag.shape
    size = ext.shape[1]
    keep = keep_mask((rows, sz), sy, counts)
    lane = lax.broadcasted_iota(jnp.int32, from_low.shape, 0)
    both = jnp.where(lane < 2, from_low[...], from_high[...])
    high = both.astype(BF16)
    rest = both - high.astype(F32)
    mid = rest.astype(BF16)
    low = (rest - mid.astype(F32)).astype(BF16)
    parts = jnp.concatenate([high, mid, low], 0)
    add = lax.dot_general(
        parts, place[...], (((0,), (0,)), ((), ())), preferred_element_type=F32
    )
    s_asm = drag[...] + add[3 * size :, :sz]
    s_own = mass[...] * (inverse_step + sponge[...].reshape(rows, sz))
    line_weight = line_pattern(W1, (1, sz))
    line_weight_asm = line_pattern(assembled_weights(NODES), (1, sz))
    total = [jnp.zeros((1, sz), F32) for _ in range(4)]
    for c in range(3):
        whole = ext[c] + add[c * size : (c + 1) * size, :sz]
        v = jnp.where(keep, whole[:rows], 0.0)
        plane = mul_left(plane_asm[...], jnp.concatenate([v, whole[rows:]], 0))
        line = mul_right(v, line_asm[...]) + add[c * size : c * size + rows, sz:]
        stiff = plane * line_weight_asm + line * plane_weight_asm[...]
        u = jnp.where(keep, s_asm * v + viscosity * stiff, 0.0)
        stiff = (
            mul_left(plane_own[...], u) * line_weight
            + mul_right(u, line_own[...]) * plane_weight[...]
        )
        own = s_own * u + viscosity * stiff
        base[c] = v
        image[c] = u
        sv = share[...] * v
        su = share[...] * u
        for k, term in enumerate((sv * v, sv * u, su * u, u * own)):
            total[k] = total[k] + jnp.sum(term, axis=0, keepdims=True)
    spot = lax.broadcasted_iota(jnp.int32, (1, sz), 1)
    out = jnp.zeros((1, sz), F32)
    for k in range(4):
        out = jnp.where(spot == k, jnp.sum(total[k], axis=1, keepdims=True), out)
    sums[...] = jnp.broadcast_to(out, sums.shape)


def combine_kernel(base, image, sums, out):
    total = jnp.sum(sums[...], axis=0, keepdims=True)
    m0, m1, m2, m3 = (total[:, k : k + 1] for k in range(4))
    alpha = m0 / m1
    norm = m0 - 2.0 * alpha * m1 + alpha * alpha * m2
    grow = 1.0 + norm / m0
    bend = grow * grow * m1 - 2.0 * grow * alpha * m2 + alpha * alpha * m3
    alpha2 = norm / bend
    one = alpha + alpha2 * grow
    two = alpha * alpha2
    for c in range(3):
        out[c] = one * base[c] - two * image[c]


VMEM = pl.BlockSpec(memory_space=pltpu.VMEM)
HBM = pl.BlockSpec(memory_space=pltpu.HBM)


def call(kernel, operands, outs, fetch=False):
    shapes = [jax.ShapeDtypeStruct(s, F32) for s in outs]
    size = sum(4 * int(np.prod(s)) for s in outs) + sum(
        o.dtype.itemsize * o.size for o in operands
    )
    return pl.pallas_call(
        kernel,
        out_shape=shapes,
        in_specs=[HBM if fetch else VMEM] * len(operands),
        out_specs=[VMEM] * len(outs),
        scratch_shapes=[pltpu.VMEM(o.shape, o.dtype) for o in operands]
        + [pltpu.SemaphoreType.DMA((len(operands),))]
        if fetch
        else [],
        compiler_params=pltpu.CompilerParams(vmem_limit_bytes=16 * 1024 * 1024),
        cost_estimate=pl.CostEstimate(
            flops=1_000_000, bytes_accessed=size, transcendentals=0
        ),
    )(*operands)


def shift(x, axis, step):
    count = lax.axis_size(axis)
    pairs = [(i, i + step) for i in range(count) if 0 <= i + step < count]
    return lax.ppermute(x, axis, pairs)


def body(adjoint_state, base_flow, base_grads, sponge):
    _, sx, sy, sz = adjoint_state.shape
    rows = sx * sy
    size = 2 * rows
    used = rows + 2 * sy
    counts = {axis: lax.axis_size(axis) for axis in ("gx", "gy", "gz")}
    wx, wy, wz = W1, np.tile(W1, sy // NODES), np.tile(W1, sz // NODES)
    ax, ay = assembled_weights(sx), assembled_weights(sy)

    def f32(x):
        return jnp.asarray(x.astype(np.float32))

    def over_plane(x, y):
        return f32(np.broadcast_to(np.kron(x, y)[:, None], (rows, sz)))

    mass = f32(np.kron(wx, wy)[:, None] * wz[None, :])
    ends = np.ones(NODES)
    ends[0] = ends[-1] = 0.5
    share = f32(
        np.kron(ends, np.tile(ends, sy // NODES))[:, None]
        * np.tile(ends, sz // NODES)[None, :]
    )
    dy = jnp.asarray(left_operand(block_diag(D1, rows // NODES)))
    dz = jnp.asarray(right_operand(block_diag(D1, sz // NODES).T))
    field, drag, right, left, right2, left2 = call(
        functools.partial(forcing_kernel, counts["gx"]),
        (adjoint_state, base_flow, base_grads, sponge, mass, dy, dz),
        [(3, rows, sz), (rows, sz)] + [(7, sy, sz)] * 2 + [(3, sy, sz)] * 2,
        fetch=True,
    )
    x_low2 = shift(right2, "gx", 2)
    x_high2 = shift(left2, "gx", -2)
    x_low = shift(right, "gx", 1)
    x_high = shift(left, "gx", -1)
    message_rows = 7 * sx + 8
    ext, drag, up, down = call(
        x_stage_kernel,
        (field, drag, x_low, x_high, x_low2, x_high2),
        [(3, used, sz), (rows, sz), (message_rows, sz), (message_rows, sz)],
    )
    y_low = shift(up, "gy", 1)
    y_high = shift(down, "gy", -1)
    pick = np.zeros((8, sz))
    pick[0, sz - 1] = 1.0
    pick[1, sz - 8 : sz - 1] = K1[7, :7]
    pick[2, 0] = 1.0
    pick[3, 1:8] = K1[0, 1:]
    ext, drag, message = call(
        y_stage_kernel,
        (ext, drag, y_low, y_high, f32(pick)),
        [(3, size, sz), (rows, sz), (8, 3 * size + rows)],
    )
    z_low = shift(message, "gz", 1)
    z_high = shift(message, "gz", -1)

    place = np.zeros((8, 2 * sz))
    place[0, 0] = place[1, sz] = place[2, sz - 1] = place[3, 2 * sz - 1] = 1.0
    place = jnp.asarray(np.tile(place, (3, 1)).astype(np.float32).astype(BF16))
    plane_asm = np.zeros((rows, size))
    plane_asm[:, :rows] = np.kron(assembled_stiffness(sx), np.diag(ay)) + np.kron(
        np.diag(ax), assembled_stiffness(sy)
    )
    for y in range(sy):
        plane_asm[y, rows + y] = ay[y]
        plane_asm[rows - sy + y, rows + sy + y] = ay[y]
    for x in range(sx):
        plane_asm[x * sy, used + x] = ax[x]
        plane_asm[x * sy + sy - 1, used + sx + x] = ax[x]
    plane_own = np.kron(K1, np.diag(wy)) + np.kron(
        np.diag(wx), block_diag(K1, sy // NODES)
    )
    slots = counts["gz"]
    base, image, sums = call(
        functools.partial(moments_kernel, counts, sy),
        (
            ext,
            drag,
            sponge,
            z_low,
            z_high,
            place,
            jnp.asarray(left_operand(plane_asm)),
            jnp.asarray(right_operand(assembled_stiffness(sz).T)),
            jnp.asarray(left_operand(plane_own)),
            jnp.asarray(right_operand(block_diag(K1, sz // NODES).T)),
            mass,
            share,
            over_plane(ax, ay),
            over_plane(wx, wy),
        ),
        [(3, rows, sz), (3, rows, sz), (slots, sz)],
    )
    sums = lax.all_to_all(sums, "gz", 0, 0, tiled=True)
    sums = jnp.sum(sums, axis=0, keepdims=True)
    slots = counts["gx"] * counts["gy"]
    sums = jnp.broadcast_to(sums, (slots, sz))
    sums = lax.all_to_all(sums, ("gx", "gy"), 0, 0, tiled=True)
    (out,) = call(combine_kernel, (base, image, sums), [(3, rows, sz)])
    return out.reshape(3, sx, sy, sz)


def solution(mesh):
    placed = (
        P(None, "gx", "gy", "gz"),
        P(None, "gx", "gy", "gz"),
        P(None, "gx", "gy", "gz"),
        P("gx", "gy", "gz"),
    )
    return jax.shard_map(
        body, mesh=mesh, in_specs=placed, out_specs=P(None, "gx", "gy", "gz"), check_vma=False
    )
```

```python
import functools

import jax
import jax.numpy as jnp
import numpy as np
from jax import lax
from jax.experimental import pallas as pl
from jax.experimental.pallas import tpu as pltpu
from jax.sharding import PartitionSpec as P

inverse_step = 2.0
viscosity = 0.05
F32 = jnp.float32
BF16 = jnp.bfloat16
NODES = 8


def gll_tables():
    degree = 7
    interior = np.array(
        [
            -0.8717401485096066,
            -0.5917001814331423,
            -0.2092992179024789,
            0.2092992179024789,
            0.5917001814331423,
            0.8717401485096066,
        ]
    )
    points = np.concatenate([[-1.0], interior, [1.0]])
    previous = np.ones(8)
    current = points * 1.0
    for degree_now in range(1, degree):
        following = ((2 * degree_now + 1) * points * current - degree_now * previous) / (
            degree_now + 1
        )
        previous = current
        current = following
    weights = 2.0 / (degree * (degree + 1) * current**2)
    matrix = np.zeros((8, 8))
    for row_idx in range(8):
        for col_idx in range(8):
            if row_idx != col_idx:
                matrix[row_idx, col_idx] = current[row_idx] / (
                    current[col_idx] * (points[row_idx] - points[col_idx])
                )
    matrix[0, 0] = -degree * (degree + 1) / 4.0
    matrix[7, 7] = degree * (degree + 1) / 4.0
    return (weights, matrix)


W1, D1 = gll_tables()
W1 = W1.astype(np.float32).astype(np.float64)
D1 = D1.astype(np.float32).astype(np.float64)
K1 = D1.T @ (W1[:, None] * D1)


def block_diag(small, count):
    return np.kron(np.eye(count), small)


def twin_matrix(length):
    out = np.eye(length)
    for i in range(NODES - 1, length - 1, NODES):
        out[i, i + 1] = 1.0
        out[i + 1, i] = 1.0
    return out


def assembled_stiffness(length):
    out = twin_matrix(length) @ block_diag(K1, length // NODES)
    out[0, 0] += K1[7, 7]
    out[-1, -1] += K1[0, 0]
    return out


def assembled_weights(length):
    out = np.tile(W1, length // NODES)
    out[0::NODES] *= 2.0
    out[NODES - 1 :: NODES] *= 2.0
    return out


def halves(matrix):
    high = matrix.astype(np.float32).astype(BF16)
    low = (matrix - high.astype(np.float64)).astype(np.float32).astype(BF16)
    return np.asarray(high), np.asarray(low)


def left_operand(matrix):
    high, low = halves(matrix)
    zero = np.zeros_like(low)
    return np.concatenate(
        [np.concatenate([high, high], 1), np.concatenate([low, zero], 1)], 0
    )


def right_operand(matrix):
    high, low = halves(matrix)
    zero = np.zeros_like(low)
    return np.concatenate(
        [np.concatenate([high, low], 1), np.concatenate([high, zero], 1)], 0
    )


def split(x):
    high = x.astype(BF16)
    low = (x - high.astype(F32)).astype(BF16)
    return high, low


def mul_left(operand, x):
    rows = operand.shape[0] // 2
    high, low = split(x)
    out = jnp.dot(operand, jnp.concatenate([high, low], 0), preferred_element_type=F32)
    return out[:rows] + out[rows:]


def mul_right(x, operand):
    cols = operand.shape[1] // 2
    high, low = split(x)
    out = jnp.dot(jnp.concatenate([high, low], 1), operand, preferred_element_type=F32)
    return out[:, :cols] + out[:, cols:]


def twin_z(x):
    length = x.shape[-1]
    lane = lax.broadcasted_iota(jnp.int32, x.shape, 1)
    after = pltpu.roll(x, length - 1, 1)
    before = pltpu.roll(x, 1, 1)
    spot = lane & (NODES - 1)
    upper = (spot == NODES - 1) & (lane != length - 1)
    lower = (spot == 0) & (lane != 0)
    return x + jnp.where(upper, after, 0.0) + jnp.where(lower, before, 0.0)


def twin_y(x):
    first, second = x[:, :8], x[:, 8:]
    row = lax.broadcasted_iota(jnp.int32, first.shape, 1)
    one = first + jnp.where(row == 7, second[:, 0:1], 0.0)
    two = second + jnp.where(row == 0, first[:, 7:8], 0.0)
    return jnp.concatenate([one, two], 1)


def forcing_kernel(
    nx,
    adj_hbm,
    flow_hbm,
    grads_hbm,
    sponge_hbm,
    mass_hbm,
    dy_hbm,
    dz_hbm,
    field,
    drag,
    right,
    left,
    right2,
    left2,
    adj,
    flow,
    grads,
    sponge,
    mass,
    dy,
    dz,
    sems,
):
    copies = [
        pltpu.make_async_copy(src, dst, sems.at[k])
        for k, (src, dst) in enumerate(
            (
                (adj_hbm, adj),
                (dz_hbm, dz),
                (mass_hbm, mass),
                (sponge_hbm, sponge),
                (dy_hbm, dy),
                (flow_hbm, flow),
                (grads_hbm, grads),
            )
        )
    ]
    for copy in copies:
        copy.start()
    ix = lax.axis_index("gx")
    for copy in copies:
        copy.wait()
    a = adj[...]
    _, sx, sy, sz = a.shape
    rows = sx * sy
    m = mass[...]
    grad_z = mul_right(a.reshape(3 * rows, sz), dz[...]).reshape(3, rows, sz)
    s_local = m * (inverse_step + sponge[...].reshape(rows, sz))
    s_asm = twin_z(twin_y(s_local.reshape(sx, sy, sz)).reshape(rows, sz))
    drag[...] = s_asm
    right[6] = s_asm[(sx - 1) * sy :]
    left[6] = s_asm[:sy]
    fl = [flow[j].astype(F32).reshape(rows, sz) for j in range(3)]
    flat = a.reshape(3, rows, sz)
    low_edge = jnp.where(ix == 0, 0.0, float(K1[7, 0])).astype(F32)
    high_edge = jnp.where(ix == nx - 1, 0.0, float(K1[0, 7])).astype(F32)
    for c in range(3):
        grad_y = mul_left(dy[...], flat[c])
        planes = [a[c, i] for i in range(sx)]
        grad_x = []
        for i in range(sx):
            total = float(D1[i, 0]) * planes[0]
            for k in range(1, sx):
                total = total + float(D1[i, k]) * planes[k]
            grad_x.append(total)
        grad_x = jnp.concatenate(grad_x, 0)
        local = inverse_step * flat[c]
        local = local + fl[0] * grad_x + fl[1] * grad_y + fl[2] * grad_z[c]
        for j in range(3):
            local = local - grads[3 * c + j].astype(F32).reshape(rows, sz) * flat[j]
        local = m * local
        out = twin_z(twin_y(local.reshape(sx, sy, sz)).reshape(rows, sz))
        field[c] = out
        plane = [out[i * sy : (i + 1) * sy] for i in range(sx)]
        up = low_edge * plane[0]
        for i in range(1, sx - 1):
            up = up + float(K1[7, i]) * plane[i]
        down = high_edge * plane[sx - 1]
        for i in range(1, sx - 1):
            down = down + float(K1[0, i]) * plane[i]
        right[c] = plane[sx - 1]
        right[3 + c] = up
        left[c] = plane[0]
        left[3 + c] = down
        right2[c] = plane[sx - 1]
        left2[c] = plane[0]


def x_stage_kernel(
    field, drag, from_low, from_high, from_low2, from_high2, ext, drag_out, up, down
):
    sy, sz = from_low.shape[1:]
    rows = field.shape[1]
    sx = rows // sy
    drag_out[...] = drag[...]
    drag_out[:sy] = drag[:sy] + from_low[6]
    drag_out[rows - sy :] = drag[rows - sy :] + from_high[6]
    count = 2 * sx
    for c in range(3):
        ext[c, :rows] = field[c]
        ext[c, :sy] = field[c, :sy] + from_low[c]
        ext[c, rows - sy : rows] = field[c, rows - sy :] + from_high[c]
        ext[c, rows : rows + sy] = from_low[3 + c] + float(K1[7, 0]) * from_low2[c]
        ext[c, rows + sy : rows + 2 * sy] = (
            from_high[3 + c] + float(K1[0, 7]) * from_high2[c]
        )

        def row(y):
            return ext[c, pl.ds(y, sx, stride=sy), :]

        up[c * count : c * count + sx] = row(sy - 1)
        total = float(K1[7, 0]) * row(sy - 8)
        for k in range(1, 7):
            total = total + float(K1[7, k]) * row(sy - 8 + k)
        up[c * count + sx : (c + 1) * count] = total
        down[c * count : c * count + sx] = row(0)
        total = float(K1[0, 7]) * row(7)
        for k in range(1, 7):
            total = total + float(K1[0, k]) * row(k)
        down[c * count + sx : (c + 1) * count] = total
    base = 3 * count
    up[base : base + sx] = drag_out[pl.ds(sy - 1, sx, stride=sy), :]
    down[base : base + sx] = drag_out[pl.ds(0, sx, stride=sy), :]
    base += sx
    up[base : base + 8] = jnp.zeros((8, sz), F32)
    down[base : base + 8] = jnp.zeros((8, sz), F32)
    for c in range(3):
        for side in range(2):
            spot = rows + side * sy
            at = base + 2 * c + side
            up[at : at + 1] = ext[c, spot + sy - 1 : spot + sy]
            down[at : at + 1] = ext[c, spot : spot + 1]


def y_stage_kernel(ext, drag, from_low, from_high, pick, ext_out, drag_out, message):
    rows, sz = drag.shape
    sy = (ext.shape[1] - rows) // 2
    sx = rows // sy
    count = 2 * sx
    base = 3 * count
    drag_out[...] = drag[...]
    drag_out[pl.ds(0, sx, stride=sy), :] = (
        drag[pl.ds(0, sx, stride=sy), :] + from_low[base : base + sx]
    )
    drag_out[pl.ds(sy - 1, sx, stride=sy), :] = (
        drag[pl.ds(sy - 1, sx, stride=sy), :] + from_high[base : base + sx]
    )
    base += sx
    used = rows + 2 * sy
    size = ext_out.shape[1]
    for c in range(3):
        ext_out[c, :used] = ext[c]
        ext_out[c, pl.ds(0, sx, stride=sy), :] = (
            ext[c, pl.ds(0, sx, stride=sy), :] + from_low[c * count : c * count + sx]
        )
        ext_out[c, pl.ds(sy - 1, sx, stride=sy), :] = (
            ext[c, pl.ds(sy - 1, sx, stride=sy), :]
            + from_high[c * count : c * count + sx]
        )
        for side in range(2):
            spot = rows + side * sy
            at = base + 2 * c + side
            ext_out[c, spot : spot + 1] = ext[c, spot : spot + 1] + from_low[at : at + 1]
            ext_out[c, spot + sy - 1 : spot + sy] = (
                ext[c, spot + sy - 1 : spot + sy] + from_high[at : at + 1]
            )
        ext_out[c, used : used + sx] = from_low[c * count + sx : (c + 1) * count]
        ext_out[c, used + sx : used + 2 * sx] = from_high[c * count + sx : (c + 1) * count]
        ext_out[c, used + 2 * sx :] = jnp.zeros((size - used - 2 * sx, sz), F32)
    for c in range(3):
        message[:, c * size : (c + 1) * size] = lax.dot_general(
            pick[...],
            ext_out[c],
            (((1,), (1,)), ((), ())),
            precision=lax.Precision.HIGHEST,
            preferred_element_type=F32,
        )
    message[:, 3 * size :] = lax.dot_general(
        pick[...],
        drag_out[...],
        (((1,), (1,)), ((), ())),
        precision=lax.Precision.HIGHEST,
        preferred_element_type=F32,
    )


def keep_mask(shape, sy, counts):
    row = lax.broadcasted_iota(jnp.int32, shape, 0)
    z = lax.broadcasted_iota(jnp.int32, shape, 1)
    shift = sy.bit_length() - 1
    x = lax.shift_right_logical(row, shift)
    y = row & (sy - 1)
    sx = shape[0] // sy
    mask = None
    for axis, spot, size in (("gx", x, sx), ("gy", y, sy), ("gz", z, shape[1])):
        here = spot + lax.axis_index(axis) * size
        inside = (here != 0) & (here != counts[axis] * size - 1)
        mask = inside if mask is None else mask & inside
    return mask


def line_pattern(values, shape):
    spot = lax.broadcasted_iota(jnp.int32, shape, 1) & (NODES - 1)
    out = jnp.full(shape, float(values[0]), F32)
    for k in range(1, NODES):
        out = jnp.where(spot == k, float(values[k]), out)
    return out


def moments_kernel(
    counts,
    sy,
    ext,
    drag,
    sponge,
    from_low,
    from_high,
    place,
    plane_asm,
    line_asm,
    plane_own,
    line_own,
    mass,
    share,
    plane_weight_asm,
    plane_weight,
    base,
    image,
    sums,
):
    rows, sz = drag.shape
    size = ext.shape[1]
    keep = keep_mask((rows, sz), sy, counts)
    lane = lax.broadcasted_iota(jnp.int32, from_low.shape, 0)
    both = jnp.where(lane < 2, from_low[...], from_high[...])
    high = both.astype(BF16)
    rest = both - high.astype(F32)
    mid = rest.astype(BF16)
    low = (rest - mid.astype(F32)).astype(BF16)
    parts = jnp.concatenate([high, mid, low], 0)
    add = lax.dot_general(
        parts, place[...], (((0,), (0,)), ((), ())), preferred_element_type=F32
    )
    s_asm = drag[...] + add[3 * size :, :sz]
    s_own = mass[...] * (inverse_step + sponge[...].reshape(rows, sz))
    line_weight = line_pattern(W1, (1, sz))
    line_weight_asm = line_pattern(assembled_weights(NODES), (1, sz))
    total = [jnp.zeros((1, sz), F32) for _ in range(4)]
    for c in range(3):
        whole = ext[c] + add[c * size : (c + 1) * size, :sz]
        v = jnp.where(keep, whole[:rows], 0.0)
        plane = mul_left(plane_asm[...], jnp.concatenate([v, whole[rows:]], 0))
        line = mul_right(v, line_asm[...]) + add[c * size : c * size + rows, sz:]
        stiff = plane * line_weight_asm + line * plane_weight_asm[...]
        u = jnp.where(keep, s_asm * v + viscosity * stiff, 0.0)
        stiff = (
            mul_left(plane_own[...], u) * line_weight
            + mul_right(u, line_own[...]) * plane_weight[...]
        )
        own = s_own * u + viscosity * stiff
        base[c] = v
        image[c] = u
        sv = share[...] * v
        su = share[...] * u
        for k, term in enumerate((sv * v, sv * u, su * u, u * own)):
            total[k] = total[k] + jnp.sum(term, axis=0, keepdims=True)
    spot = lax.broadcasted_iota(jnp.int32, (1, sz), 1)
    out = jnp.zeros((1, sz), F32)
    for k in range(4):
        out = jnp.where(spot == k, jnp.sum(total[k], axis=1, keepdims=True), out)
    sums[...] = jnp.broadcast_to(out, sums.shape)


def combine_kernel(base, image, sums, out):
    total = jnp.sum(sums[...], axis=0, keepdims=True)
    m0, m1, m2, m3 = (total[:, k : k + 1] for k in range(4))
    alpha = m0 / m1
    norm = m0 - 2.0 * alpha * m1 + alpha * alpha * m2
    grow = 1.0 + norm / m0
    bend = grow * grow * m1 - 2.0 * grow * alpha * m2 + alpha * alpha * m3
    alpha2 = norm / bend
    one = alpha + alpha2 * grow
    two = alpha * alpha2
    for c in range(3):
        out[c] = one * base[c] - two * image[c]


VMEM = pl.BlockSpec(memory_space=pltpu.VMEM)
HBM = pl.BlockSpec(memory_space=pltpu.HBM)


def call(kernel, operands, outs, fetch=False):
    shapes = [jax.ShapeDtypeStruct(s, F32) for s in outs]
    size = sum(4 * int(np.prod(s)) for s in outs) + sum(
        o.dtype.itemsize * o.size for o in operands
    )
    if fetch:
        operands = [pltpu.with_memory_space_constraint(o, pltpu.HBM) for o in operands]
    return pl.pallas_call(
        kernel,
        out_shape=shapes,
        in_specs=[HBM if fetch else VMEM] * len(operands),
        out_specs=[VMEM] * len(outs),
        scratch_shapes=[pltpu.VMEM(o.shape, o.dtype) for o in operands]
        + [pltpu.SemaphoreType.DMA((len(operands),))]
        if fetch
        else [],
        compiler_params=pltpu.CompilerParams(vmem_limit_bytes=16 * 1024 * 1024),
        cost_estimate=pl.CostEstimate(
            flops=1_000_000, bytes_accessed=size, transcendentals=0
        ),
    )(*operands)


def shift(x, axis, step):
    count = lax.axis_size(axis)
    pairs = [(i, i + step) for i in range(count) if 0 <= i + step < count]
    return lax.ppermute(x, axis, pairs)


def body(adjoint_state, base_flow, base_grads, sponge):
    _, sx, sy, sz = adjoint_state.shape
    rows = sx * sy
    size = 2 * rows
    used = rows + 2 * sy
    counts = {axis: lax.axis_size(axis) for axis in ("gx", "gy", "gz")}
    wx, wy, wz = W1, np.tile(W1, sy // NODES), np.tile(W1, sz // NODES)
    ax, ay = assembled_weights(sx), assembled_weights(sy)

    def f32(x):
        return jnp.asarray(x.astype(np.float32))

    def over_plane(x, y):
        return f32(np.broadcast_to(np.kron(x, y)[:, None], (rows, sz)))

    mass = f32(np.kron(wx, wy)[:, None] * wz[None, :])
    ends = np.ones(NODES)
    ends[0] = ends[-1] = 0.5
    share = f32(
        np.kron(ends, np.tile(ends, sy // NODES))[:, None]
        * np.tile(ends, sz // NODES)[None, :]
    )
    dy = jnp.asarray(left_operand(block_diag(D1, rows // NODES)))
    dz = jnp.asarray(right_operand(block_diag(D1, sz // NODES).T))
    field, drag, right, left, right2, left2 = call(
        functools.partial(forcing_kernel, counts["gx"]),
        (adjoint_state, base_flow, base_grads, sponge, mass, dy, dz),
        [(3, rows, sz), (rows, sz)] + [(7, sy, sz)] * 2 + [(3, sy, sz)] * 2,
        fetch=True,
    )
    x_low2 = shift(right2, "gx", 2)
    x_high2 = shift(left2, "gx", -2)
    x_low = shift(right, "gx", 1)
    x_high = shift(left, "gx", -1)
    message_rows = 7 * sx + 8
    ext, drag, up, down = call(
        x_stage_kernel,
        (field, drag, x_low, x_high, x_low2, x_high2),
        [(3, used, sz), (rows, sz), (message_rows, sz), (message_rows, sz)],
    )
    y_low = shift(up, "gy", 1)
    y_high = shift(down, "gy", -1)
    pick = np.zeros((8, sz))
    pick[0, sz - 1] = 1.0
    pick[1, sz - 8 : sz - 1] = K1[7, :7]
    pick[2, 0] = 1.0
    pick[3, 1:8] = K1[0, 1:]
    ext, drag, message = call(
        y_stage_kernel,
        (ext, drag, y_low, y_high, f32(pick)),
        [(3, size, sz), (rows, sz), (8, 3 * size + rows)],
    )
    z_low = shift(message, "gz", 1)
    z_high = shift(message, "gz", -1)

    place = np.zeros((8, 2 * sz))
    place[0, 0] = place[1, sz] = place[2, sz - 1] = place[3, 2 * sz - 1] = 1.0
    place = jnp.asarray(np.tile(place, (3, 1)).astype(np.float32).astype(BF16))
    plane_asm = np.zeros((rows, size))
    plane_asm[:, :rows] = np.kron(assembled_stiffness(sx), np.diag(ay)) + np.kron(
        np.diag(ax), assembled_stiffness(sy)
    )
    for y in range(sy):
        plane_asm[y, rows + y] = ay[y]
        plane_asm[rows - sy + y, rows + sy + y] = ay[y]
    for x in range(sx):
        plane_asm[x * sy, used + x] = ax[x]
        plane_asm[x * sy + sy - 1, used + sx + x] = ax[x]
    plane_own = np.kron(K1, np.diag(wy)) + np.kron(
        np.diag(wx), block_diag(K1, sy // NODES)
    )
    slots = counts["gz"]
    base, image, sums = call(
        functools.partial(moments_kernel, counts, sy),
        (
            ext,
            drag,
            sponge,
            z_low,
            z_high,
            place,
            jnp.asarray(left_operand(plane_asm)),
            jnp.asarray(right_operand(assembled_stiffness(sz).T)),
            jnp.asarray(left_operand(plane_own)),
            jnp.asarray(right_operand(block_diag(K1, sz // NODES).T)),
            mass,
            share,
            over_plane(ax, ay),
            over_plane(wx, wy),
        ),
        [(3, rows, sz), (3, rows, sz), (slots, sz)],
    )
    sums = lax.all_to_all(sums, "gz", 0, 0, tiled=True)
    sums = jnp.sum(sums, axis=0, keepdims=True)
    slots = counts["gx"] * counts["gy"]
    sums = jnp.broadcast_to(sums, (slots, sz))
    sums = lax.all_to_all(sums, ("gx", "gy"), 0, 0, tiled=True)
    (out,) = call(combine_kernel, (base, image, sums), [(3, rows, sz)])
    return out.reshape(3, sx, sy, sz)


def solution(mesh):
    placed = (
        P(None, "gx", "gy", "gz"),
        P(None, "gx", "gy", "gz"),
        P(None, "gx", "gy", "gz"),
        P("gx", "gy", "gz"),
    )
    return jax.shard_map(
        body, mesh=mesh, in_specs=placed, out_specs=P(None, "gx", "gy", "gz"), check_vma=False
    )
```

```python
import functools

import jax
import jax.numpy as jnp
import numpy as np
from jax import lax
from jax.experimental import pallas as pl
from jax.experimental.pallas import tpu as pltpu
from jax.sharding import PartitionSpec as P

inverse_step = 2.0
viscosity = 0.05
F32 = jnp.float32
BF16 = jnp.bfloat16
NODES = 8


def gll_tables():
    degree = 7
    interior = np.array(
        [
            -0.8717401485096066,
            -0.5917001814331423,
            -0.2092992179024789,
            0.2092992179024789,
            0.5917001814331423,
            0.8717401485096066,
        ]
    )
    points = np.concatenate([[-1.0], interior, [1.0]])
    previous = np.ones(8)
    current = points * 1.0
    for degree_now in range(1, degree):
        following = ((2 * degree_now + 1) * points * current - degree_now * previous) / (
            degree_now + 1
        )
        previous = current
        current = following
    weights = 2.0 / (degree * (degree + 1) * current**2)
    matrix = np.zeros((8, 8))
    for row_idx in range(8):
        for col_idx in range(8):
            if row_idx != col_idx:
                matrix[row_idx, col_idx] = current[row_idx] / (
                    current[col_idx] * (points[row_idx] - points[col_idx])
                )
    matrix[0, 0] = -degree * (degree + 1) / 4.0
    matrix[7, 7] = degree * (degree + 1) / 4.0
    return (weights, matrix)


W1, D1 = gll_tables()
W1 = W1.astype(np.float32).astype(np.float64)
D1 = D1.astype(np.float32).astype(np.float64)
K1 = D1.T @ (W1[:, None] * D1)


def block_diag(small, count):
    return np.kron(np.eye(count), small)


def twin_matrix(length):
    out = np.eye(length)
    for i in range(NODES - 1, length - 1, NODES):
        out[i, i + 1] = 1.0
        out[i + 1, i] = 1.0
    return out


def assembled_stiffness(length):
    out = twin_matrix(length) @ block_diag(K1, length // NODES)
    out[0, 0] += K1[7, 7]
    out[-1, -1] += K1[0, 0]
    return out


def assembled_weights(length):
    out = np.tile(W1, length // NODES)
    out[0::NODES] *= 2.0
    out[NODES - 1 :: NODES] *= 2.0
    return out


def halves(matrix):
    high = matrix.astype(np.float32).astype(BF16)
    low = (matrix - high.astype(np.float64)).astype(np.float32).astype(BF16)
    return np.asarray(high), np.asarray(low)


def left_operand(matrix):
    high, low = halves(matrix)
    zero = np.zeros_like(low)
    return np.concatenate(
        [np.concatenate([high, high], 1), np.concatenate([low, zero], 1)], 0
    )


def right_operand(matrix):
    high, low = halves(matrix)
    zero = np.zeros_like(low)
    return np.concatenate(
        [np.concatenate([high, low], 1), np.concatenate([high, zero], 1)], 0
    )


def split(x):
    high = x.astype(BF16)
    low = (x - high.astype(F32)).astype(BF16)
    return high, low


def mul_left(operand, x):
    rows = operand.shape[0] // 2
    high, low = split(x)
    out = jnp.dot(operand, jnp.concatenate([high, low], 0), preferred_element_type=F32)
    return out[:rows] + out[rows:]


def mul_right(x, operand):
    cols = operand.shape[1] // 2
    high, low = split(x)
    out = jnp.dot(jnp.concatenate([high, low], 1), operand, preferred_element_type=F32)
    return out[:, :cols] + out[:, cols:]


def twin_z(x):
    length = x.shape[-1]
    lane = lax.broadcasted_iota(jnp.int32, x.shape, 1)
    after = pltpu.roll(x, length - 1, 1)
    before = pltpu.roll(x, 1, 1)
    spot = lane & (NODES - 1)
    upper = (spot == NODES - 1) & (lane != length - 1)
    lower = (spot == 0) & (lane != 0)
    return x + jnp.where(upper, after, 0.0) + jnp.where(lower, before, 0.0)


def twin_y(x):
    first, second = x[:, :8], x[:, 8:]
    row = lax.broadcasted_iota(jnp.int32, first.shape, 1)
    one = first + jnp.where(row == 7, second[:, 0:1], 0.0)
    two = second + jnp.where(row == 0, first[:, 7:8], 0.0)
    return jnp.concatenate([one, two], 1)


def forcing_kernel(
    nx,
    adj_hbm,
    flow_hbm,
    grads_hbm,
    sponge_hbm,
    mass_hbm,
    dy_hbm,
    dz_hbm,
    field,
    drag,
    right,
    left,
    adj,
    flow,
    grads,
    sponge,
    mass,
    dy,
    dz,
    sems,
):
    copies = [
        pltpu.make_async_copy(src, dst, sems.at[k])
        for k, (src, dst) in enumerate(
            (
                (adj_hbm, adj),
                (dz_hbm, dz),
                (mass_hbm, mass),
                (sponge_hbm, sponge),
                (dy_hbm, dy),
                (flow_hbm, flow),
                (grads_hbm, grads),
            )
        )
    ]
    for copy in copies:
        copy.start()
    ix = lax.axis_index("gx")
    copies[0].wait()
    a = adj[...]
    _, sx, sy, sz = a.shape
    rows = sx * sy
    copies[1].wait()
    grad_z = mul_right(a.reshape(3 * rows, sz), dz[...]).reshape(3, rows, sz)
    copies[2].wait()
    copies[3].wait()
    m = mass[...]
    s_local = m * (inverse_step + sponge[...].reshape(rows, sz))
    s_asm = twin_z(twin_y(s_local.reshape(sx, sy, sz)).reshape(rows, sz))
    drag[...] = s_asm
    right[6] = s_asm[(sx - 1) * sy :]
    left[6] = s_asm[:sy]
    for copy in copies[4:]:
        copy.wait()
    fl = [flow[j].astype(F32).reshape(rows, sz) for j in range(3)]
    flat = a.reshape(3, rows, sz)
    low_edge = jnp.where(ix == 0, 0.0, float(K1[7, 0])).astype(F32)
    high_edge = jnp.where(ix == nx - 1, 0.0, float(K1[0, 7])).astype(F32)
    for c in range(3):
        grad_y = mul_left(dy[...], flat[c])
        planes = [a[c, i] for i in range(sx)]
        grad_x = []
        for i in range(sx):
            total = float(D1[i, 0]) * planes[0]
            for k in range(1, sx):
                total = total + float(D1[i, k]) * planes[k]
            grad_x.append(total)
        grad_x = jnp.concatenate(grad_x, 0)
        local = inverse_step * flat[c]
        local = local + fl[0] * grad_x + fl[1] * grad_y + fl[2] * grad_z[c]
        for j in range(3):
            local = local - grads[3 * c + j].astype(F32).reshape(rows, sz) * flat[j]
        local = m * local
        out = twin_z(twin_y(local.reshape(sx, sy, sz)).reshape(rows, sz))
        field[c] = out
        plane = [out[i * sy : (i + 1) * sy] for i in range(sx)]
        up = low_edge * plane[0]
        for i in range(1, sx - 1):
            up = up + float(K1[7, i]) * plane[i]
        down = high_edge * plane[sx - 1]
        for i in range(1, sx - 1):
            down = down + float(K1[0, i]) * plane[i]
        right[c] = plane[sx - 1]
        right[3 + c] = up
        left[c] = plane[0]
        left[3 + c] = down


def x_stage_kernel(
    field, drag, from_low, from_high, from_low2, from_high2, ext, drag_out, up, down
):
    sy, sz = from_low.shape[1:]
    rows = field.shape[1]
    sx = rows // sy
    drag_out[...] = drag[...]
    drag_out[:sy] = drag[:sy] + from_low[6]
    drag_out[rows - sy :] = drag[rows - sy :] + from_high[6]
    count = 2 * sx
    for c in range(3):
        ext[c, :rows] = field[c]
        ext[c, :sy] = field[c, :sy] + from_low[c]
        ext[c, rows - sy : rows] = field[c, rows - sy :] + from_high[c]
        ext[c, rows : rows + sy] = from_low[3 + c] + float(K1[7, 0]) * from_low2[c]
        ext[c, rows + sy : rows + 2 * sy] = (
            from_high[3 + c] + float(K1[0, 7]) * from_high2[c]
        )

        def row(y):
            return ext[c, pl.ds(y, sx, stride=sy), :]

        up[c * count : c * count + sx] = row(sy - 1)
        total = float(K1[7, 0]) * row(sy - 8)
        for k in range(1, 7):
            total = total + float(K1[7, k]) * row(sy - 8 + k)
        up[c * count + sx : (c + 1) * count] = total
        down[c * count : c * count + sx] = row(0)
        total = float(K1[0, 7]) * row(7)
        for k in range(1, 7):
            total = total + float(K1[0, k]) * row(k)
        down[c * count + sx : (c + 1) * count] = total
    base = 3 * count
    up[base : base + sx] = drag_out[pl.ds(sy - 1, sx, stride=sy), :]
    down[base : base + sx] = drag_out[pl.ds(0, sx, stride=sy), :]
    base += sx
    up[base : base + 8] = jnp.zeros((8, sz), F32)
    down[base : base + 8] = jnp.zeros((8, sz), F32)
    for c in range(3):
        for side in range(2):
            spot = rows + side * sy
            at = base + 2 * c + side
            up[at : at + 1] = ext[c, spot + sy - 1 : spot + sy]
            down[at : at + 1] = ext[c, spot : spot + 1]


def y_stage_kernel(ext, drag, from_low, from_high, pick, ext_out, drag_out, message):
    rows, sz = drag.shape
    sy = (ext.shape[1] - rows) // 2
    sx = rows // sy
    count = 2 * sx
    base = 3 * count
    drag_out[...] = drag[...]
    drag_out[pl.ds(0, sx, stride=sy), :] = (
        drag[pl.ds(0, sx, stride=sy), :] + from_low[base : base + sx]
    )
    drag_out[pl.ds(sy - 1, sx, stride=sy), :] = (
        drag[pl.ds(sy - 1, sx, stride=sy), :] + from_high[base : base + sx]
    )
    base += sx
    used = rows + 2 * sy
    size = ext_out.shape[1]
    for c in range(3):
        ext_out[c, :used] = ext[c]
        ext_out[c, pl.ds(0, sx, stride=sy), :] = (
            ext[c, pl.ds(0, sx, stride=sy), :] + from_low[c * count : c * count + sx]
        )
        ext_out[c, pl.ds(sy - 1, sx, stride=sy), :] = (
            ext[c, pl.ds(sy - 1, sx, stride=sy), :]
            + from_high[c * count : c * count + sx]
        )
        for side in range(2):
            spot = rows + side * sy
            at = base + 2 * c + side
            ext_out[c, spot : spot + 1] = ext[c, spot : spot + 1] + from_low[at : at + 1]
            ext_out[c, spot + sy - 1 : spot + sy] = (
                ext[c, spot + sy - 1 : spot + sy] + from_high[at : at + 1]
            )
        ext_out[c, used : used + sx] = from_low[c * count + sx : (c + 1) * count]
        ext_out[c, used + sx : used + 2 * sx] = from_high[c * count + sx : (c + 1) * count]
        ext_out[c, used + 2 * sx :] = jnp.zeros((size - used - 2 * sx, sz), F32)
    for c in range(3):
        message[:, c * size : (c + 1) * size] = lax.dot_general(
            pick[...],
            ext_out[c],
            (((1,), (1,)), ((), ())),
            precision=lax.Precision.HIGHEST,
            preferred_element_type=F32,
        )
    message[:, 3 * size :] = lax.dot_general(
        pick[...],
        drag_out[...],
        (((1,), (1,)), ((), ())),
        precision=lax.Precision.HIGHEST,
        preferred_element_type=F32,
    )


def keep_mask(shape, sy, counts):
    row = lax.broadcasted_iota(jnp.int32, shape, 0)
    z = lax.broadcasted_iota(jnp.int32, shape, 1)
    shift = sy.bit_length() - 1
    x = lax.shift_right_logical(row, shift)
    y = row & (sy - 1)
    sx = shape[0] // sy
    mask = None
    for axis, spot, size in (("gx", x, sx), ("gy", y, sy), ("gz", z, shape[1])):
        here = spot + lax.axis_index(axis) * size
        inside = (here != 0) & (here != counts[axis] * size - 1)
        mask = inside if mask is None else mask & inside
    return mask


def line_pattern(values, shape):
    spot = lax.broadcasted_iota(jnp.int32, shape, 1) & (NODES - 1)
    out = jnp.full(shape, float(values[0]), F32)
    for k in range(1, NODES):
        out = jnp.where(spot == k, float(values[k]), out)
    return out


def moments_kernel(
    counts,
    sy,
    ext,
    drag,
    sponge,
    from_low,
    from_high,
    place,
    plane_asm,
    line_asm,
    plane_own,
    line_own,
    mass,
    share,
    plane_weight_asm,
    plane_weight,
    base,
    image,
    sums,
):
    rows, sz = drag.shape
    size = ext.shape[1]
    keep = keep_mask((rows, sz), sy, counts)
    lane = lax.broadcasted_iota(jnp.int32, from_low.shape, 0)
    both = jnp.where(lane < 2, from_low[...], from_high[...])
    high = both.astype(BF16)
    rest = both - high.astype(F32)
    mid = rest.astype(BF16)
    low = (rest - mid.astype(F32)).astype(BF16)
    parts = jnp.concatenate([high, mid, low], 0)
    add = lax.dot_general(
        parts, place[...], (((0,), (0,)), ((), ())), preferred_element_type=F32
    )
    s_asm = drag[...] + add[3 * size :, :sz]
    s_own = mass[...] * (inverse_step + sponge[...].reshape(rows, sz))
    line_weight = line_pattern(W1, (1, sz))
    line_weight_asm = line_pattern(assembled_weights(NODES), (1, sz))
    total = [jnp.zeros((1, sz), F32) for _ in range(4)]
    for c in range(3):
        whole = ext[c] + add[c * size : (c + 1) * size, :sz]
        v = jnp.where(keep, whole[:rows], 0.0)
        plane = mul_left(plane_asm[...], jnp.concatenate([v, whole[rows:]], 0))
        line = mul_right(v, line_asm[...]) + add[c * size : c * size + rows, sz:]
        stiff = plane * line_weight_asm + line * plane_weight_asm[...]
        u = jnp.where(keep, s_asm * v + viscosity * stiff, 0.0)
        stiff = (
            mul_left(plane_own[...], u) * line_weight
            + mul_right(u, line_own[...]) * plane_weight[...]
        )
        own = s_own * u + viscosity * stiff
        base[c] = v
        image[c] = u
        sv = share[...] * v
        su = share[...] * u
        for k, term in enumerate((sv * v, sv * u, su * u, u * own)):
            total[k] = total[k] + jnp.sum(term, axis=0, keepdims=True)
    spot = lax.broadcasted_iota(jnp.int32, (1, sz), 1)
    out = jnp.zeros((1, sz), F32)
    for k in range(4):
        out = jnp.where(spot == k, jnp.sum(total[k], axis=1, keepdims=True), out)
    sums[...] = jnp.broadcast_to(out, sums.shape)


def combine_kernel(base, image, sums, out):
    total = jnp.sum(sums[...], axis=0, keepdims=True)
    m0, m1, m2, m3 = (total[:, k : k + 1] for k in range(4))
    alpha = m0 / m1
    norm = m0 - 2.0 * alpha * m1 + alpha * alpha * m2
    grow = 1.0 + norm / m0
    bend = grow * grow * m1 - 2.0 * grow * alpha * m2 + alpha * alpha * m3
    alpha2 = norm / bend
    one = alpha + alpha2 * grow
    two = alpha * alpha2
    for c in range(3):
        out[c] = one * base[c] - two * image[c]


VMEM = pl.BlockSpec(memory_space=pltpu.VMEM)
HBM = pl.BlockSpec(memory_space=pltpu.HBM)


def call(kernel, operands, outs, fetch=False):
    shapes = [jax.ShapeDtypeStruct(s, F32) for s in outs]
    size = sum(4 * int(np.prod(s)) for s in outs) + sum(
        o.dtype.itemsize * o.size for o in operands
    )
    if fetch:
        operands = [pltpu.with_memory_space_constraint(o, pltpu.HBM) for o in operands]
    return pl.pallas_call(
        kernel,
        out_shape=shapes,
        in_specs=[HBM if fetch else VMEM] * len(operands),
        out_specs=[VMEM] * len(outs),
        scratch_shapes=[pltpu.VMEM(o.shape, o.dtype) for o in operands]
        + [pltpu.SemaphoreType.DMA((len(operands),))]
        if fetch
        else [],
        compiler_params=pltpu.CompilerParams(vmem_limit_bytes=16 * 1024 * 1024),
        cost_estimate=pl.CostEstimate(
            flops=1_000_000, bytes_accessed=size, transcendentals=0
        ),
    )(*operands)


def shift(x, axis, step):
    count = lax.axis_size(axis)
    pairs = [(i, i + step) for i in range(count) if 0 <= i + step < count]
    return lax.ppermute(x, axis, pairs)


def body(adjoint_state, base_flow, base_grads, sponge):
    _, sx, sy, sz = adjoint_state.shape
    rows = sx * sy
    size = 2 * rows
    used = rows + 2 * sy
    counts = {axis: lax.axis_size(axis) for axis in ("gx", "gy", "gz")}
    wx, wy, wz = W1, np.tile(W1, sy // NODES), np.tile(W1, sz // NODES)
    ax, ay = assembled_weights(sx), assembled_weights(sy)

    def f32(x):
        return jnp.asarray(x.astype(np.float32))

    def over_plane(x, y):
        return f32(np.broadcast_to(np.kron(x, y)[:, None], (rows, sz)))

    mass = f32(np.kron(wx, wy)[:, None] * wz[None, :])
    ends = np.ones(NODES)
    ends[0] = ends[-1] = 0.5
    share = f32(
        np.kron(ends, np.tile(ends, sy // NODES))[:, None]
        * np.tile(ends, sz // NODES)[None, :]
    )
    dy = jnp.asarray(left_operand(block_diag(D1, rows // NODES)))
    dz = jnp.asarray(right_operand(block_diag(D1, sz // NODES).T))
    field, drag, right, left = call(
        functools.partial(forcing_kernel, counts["gx"]),
        (adjoint_state, base_flow, base_grads, sponge, mass, dy, dz),
        [(3, rows, sz), (rows, sz)] + [(7, sy, sz)] * 2,
        fetch=True,
    )
    x_low = shift(right, "gx", 1)
    x_low2 = shift(right, "gx", 2)
    x_high = shift(left, "gx", -1)
    x_high2 = shift(left, "gx", -2)
    message_rows = 7 * sx + 8
    ext, drag, up, down = call(
        x_stage_kernel,
        (field, drag, x_low, x_high, x_low2, x_high2),
        [(3, used, sz), (rows, sz), (message_rows, sz), (message_rows, sz)],
    )
    y_low = shift(up, "gy", 1)
    y_high = shift(down, "gy", -1)
    pick = np.zeros((8, sz))
    pick[0, sz - 1] = 1.0
    pick[1, sz - 8 : sz - 1] = K1[7, :7]
    pick[2, 0] = 1.0
    pick[3, 1:8] = K1[0, 1:]
    ext, drag, message = call(
        y_stage_kernel,
        (ext, drag, y_low, y_high, f32(pick)),
        [(3, size, sz), (rows, sz), (8, 3 * size + rows)],
    )
    z_low = shift(message, "gz", 1)
    z_high = shift(message, "gz", -1)

    place = np.zeros((8, 2 * sz))
    place[0, 0] = place[1, sz] = place[2, sz - 1] = place[3, 2 * sz - 1] = 1.0
    place = jnp.asarray(np.tile(place, (3, 1)).astype(np.float32).astype(BF16))
    plane_asm = np.zeros((rows, size))
    plane_asm[:, :rows] = np.kron(assembled_stiffness(sx), np.diag(ay)) + np.kron(
        np.diag(ax), assembled_stiffness(sy)
    )
    for y in range(sy):
        plane_asm[y, rows + y] = ay[y]
        plane_asm[rows - sy + y, rows + sy + y] = ay[y]
    for x in range(sx):
        plane_asm[x * sy, used + x] = ax[x]
        plane_asm[x * sy + sy - 1, used + sx + x] = ax[x]
    plane_own = np.kron(K1, np.diag(wy)) + np.kron(
        np.diag(wx), block_diag(K1, sy // NODES)
    )
    slots = counts["gz"]
    base, image, sums = call(
        functools.partial(moments_kernel, counts, sy),
        (
            ext,
            drag,
            sponge,
            z_low,
            z_high,
            place,
            jnp.asarray(left_operand(plane_asm)),
            jnp.asarray(right_operand(assembled_stiffness(sz).T)),
            jnp.asarray(left_operand(plane_own)),
            jnp.asarray(right_operand(block_diag(K1, sz // NODES).T)),
            mass,
            share,
            over_plane(ax, ay),
            over_plane(wx, wy),
        ),
        [(3, rows, sz), (3, rows, sz), (slots, sz)],
    )
    sums = lax.all_to_all(sums, "gz", 0, 0, tiled=True)
    sums = jnp.sum(sums, axis=0, keepdims=True)
    slots = counts["gx"] * counts["gy"]
    sums = jnp.broadcast_to(sums, (slots, sz))
    sums = lax.all_to_all(sums, ("gx", "gy"), 0, 0, tiled=True)
    (out,) = call(combine_kernel, (base, image, sums), [(3, rows, sz)])
    return out.reshape(3, sx, sy, sz)


def solution(mesh):
    placed = (
        P(None, "gx", "gy", "gz"),
        P(None, "gx", "gy", "gz"),
        P(None, "gx", "gy", "gz"),
        P("gx", "gy", "gz"),
    )
    return jax.shard_map(
        body, mesh=mesh, in_specs=placed, out_specs=P(None, "gx", "gy", "gz"), check_vma=False
    )
```

```python
import functools

import jax
import jax.numpy as jnp
import numpy as np
from jax import lax
from jax.experimental import pallas as pl
from jax.experimental.pallas import tpu as pltpu
from jax.sharding import PartitionSpec as P

inverse_step = 2.0
viscosity = 0.05
F32 = jnp.float32
BF16 = jnp.bfloat16
NODES = 8


def gll_tables():
    degree = 7
    interior = np.array(
        [
            -0.8717401485096066,
            -0.5917001814331423,
            -0.2092992179024789,
            0.2092992179024789,
            0.5917001814331423,
            0.8717401485096066,
        ]
    )
    points = np.concatenate([[-1.0], interior, [1.0]])
    previous = np.ones(8)
    current = points * 1.0
    for degree_now in range(1, degree):
        following = ((2 * degree_now + 1) * points * current - degree_now * previous) / (
            degree_now + 1
        )
        previous = current
        current = following
    weights = 2.0 / (degree * (degree + 1) * current**2)
    matrix = np.zeros((8, 8))
    for row_idx in range(8):
        for col_idx in range(8):
            if row_idx != col_idx:
                matrix[row_idx, col_idx] = current[row_idx] / (
                    current[col_idx] * (points[row_idx] - points[col_idx])
                )
    matrix[0, 0] = -degree * (degree + 1) / 4.0
    matrix[7, 7] = degree * (degree + 1) / 4.0
    return (weights, matrix)


W1, D1 = gll_tables()
W1 = W1.astype(np.float32).astype(np.float64)
D1 = D1.astype(np.float32).astype(np.float64)
K1 = D1.T @ (W1[:, None] * D1)


def block_diag(small, count):
    return np.kron(np.eye(count), small)


def twin_matrix(length):
    out = np.eye(length)
    for i in range(NODES - 1, length - 1, NODES):
        out[i, i + 1] = 1.0
        out[i + 1, i] = 1.0
    return out


def assembled_stiffness(length):
    out = twin_matrix(length) @ block_diag(K1, length // NODES)
    out[0, 0] += K1[7, 7]
    out[-1, -1] += K1[0, 0]
    return out


def assembled_weights(length):
    out = np.tile(W1, length // NODES)
    out[0::NODES] *= 2.0
    out[NODES - 1 :: NODES] *= 2.0
    return out


def halves(matrix):
    high = matrix.astype(np.float32).astype(BF16)
    low = (matrix - high.astype(np.float64)).astype(np.float32).astype(BF16)
    return np.asarray(high), np.asarray(low)


def left_operand(matrix):
    high, low = halves(matrix)
    zero = np.zeros_like(low)
    return np.concatenate(
        [np.concatenate([high, high], 1), np.concatenate([low, zero], 1)], 0
    )


def right_operand(matrix):
    high, low = halves(matrix)
    zero = np.zeros_like(low)
    return np.concatenate(
        [np.concatenate([high, low], 1), np.concatenate([high, zero], 1)], 0
    )


def split(x):
    high = x.astype(BF16)
    low = (x - high.astype(F32)).astype(BF16)
    return high, low


def mul_left(operand, x):
    rows = operand.shape[0] // 2
    high, low = split(x)
    out = jnp.dot(operand, jnp.concatenate([high, low], 0), preferred_element_type=F32)
    return out[:rows] + out[rows:]


def mul_right(x, operand):
    cols = operand.shape[1] // 2
    high, low = split(x)
    out = jnp.dot(jnp.concatenate([high, low], 1), operand, preferred_element_type=F32)
    return out[:, :cols] + out[:, cols:]


def twin_z(x):
    length = x.shape[-1]
    lane = lax.broadcasted_iota(jnp.int32, x.shape, 1)
    after = pltpu.roll(x, length - 1, 1)
    before = pltpu.roll(x, 1, 1)
    spot = lane & (NODES - 1)
    upper = (spot == NODES - 1) & (lane != length - 1)
    lower = (spot == 0) & (lane != 0)
    return x + jnp.where(upper, after, 0.0) + jnp.where(lower, before, 0.0)


def twin_y(x):
    first, second = x[:, :8], x[:, 8:]
    row = lax.broadcasted_iota(jnp.int32, first.shape, 1)
    one = first + jnp.where(row == 7, second[:, 0:1], 0.0)
    two = second + jnp.where(row == 0, first[:, 7:8], 0.0)
    return jnp.concatenate([one, two], 1)


def member(axis):
    return (lax.axis_index(axis) & 1) == 0


def has_neighbour(axis, high, count):
    here = lax.axis_index(axis)
    return jnp.where(high, here < count - 1, here > 0)


def slot_of(x, z):
    return 2 * x + z


def as_number(flag):
    return jnp.where(flag, 1, 0)


def turned(pick, tile):
    return lax.dot_general(
        pick,
        tile,
        (((1,), (1,)), ((), ())),
        precision=lax.Precision.HIGHEST,
        preferred_element_type=F32,
    )


def spread(tiles, place):
    both = jnp.concatenate(tiles, 1)
    high = both.astype(BF16)
    rest = both - high.astype(F32)
    mid = rest.astype(BF16)
    low = (rest - mid.astype(F32)).astype(BF16)
    parts = jnp.concatenate([high, mid, low], 0)
    return lax.dot_general(
        parts, place, (((0,), (0,)), ((), ())), preferred_element_type=F32
    )


def picked(tile, high, ok):
    row = lax.broadcasted_iota(jnp.int32, tile.shape, 0)
    start = jnp.where(high, 2, 0)
    use = (row >= start) & (row < start + 2) & ok
    return jnp.where(use, tile, 0.0)


def face_of(x, high, size):
    return jnp.where(high, x[-size:], x[:size])


def facing(face, high, rows):
    gap = jnp.zeros((rows - face.shape[0], face.shape[1]), F32)
    return jnp.where(
        high, jnp.concatenate([face, gap], 0), jnp.concatenate([gap, face], 0)
    )


def contraction(x, high, size, nx):
    ix = lax.axis_index("gx")
    count = x.shape[0] // size
    total = None
    for i in range(count):
        upper = 0.0 if i == count - 1 else float(K1[7, i])
        lower = 0.0 if i == 0 else float(K1[0, i])
        scale = jnp.where(high, upper, lower).astype(F32)
        if i == 0:
            scale = jnp.where(ix == 0, 0.0, scale)
        if i == count - 1:
            scale = jnp.where(ix == nx - 1, 0.0, scale)
        term = scale * x[i * size : (i + 1) * size]
        total = term if total is None else total + term
    return total


def forcing_kernel(
    adj_hbm,
    flow_hbm,
    grads_hbm,
    sponge_hbm,
    mass_hbm,
    dy_hbm,
    dz_hbm,
    pick_hbm,
    field,
    drag,
    slots,
    adj,
    flow,
    grads,
    sponge,
    mass,
    dy,
    dz,
    pick,
    sems,
):
    copies = [
        pltpu.make_async_copy(src, dst, sems.at[k])
        for k, (src, dst) in enumerate(
            (
                (adj_hbm, adj),
                (dz_hbm, dz),
                (mass_hbm, mass),
                (sponge_hbm, sponge),
                (dy_hbm, dy),
                (flow_hbm, flow),
                (grads_hbm, grads),
                (pick_hbm, pick),
            )
        )
    ]
    for copy in copies:
        copy.start()
    slots[...] = jnp.zeros(slots.shape, F32)
    copies[0].wait()
    a = adj[...]
    _, sx, sy, sz = a.shape
    rows = sx * sy
    copies[1].wait()
    grad_z = mul_right(a.reshape(3 * rows, sz), dz[...]).reshape(3, rows, sz)
    for copy in copies[2:]:
        copy.wait()
    m = mass[...]
    s_local = m * (inverse_step + sponge[...].reshape(rows, sz))
    s_asm = twin_z(twin_y(s_local.reshape(sx, sy, sz)).reshape(rows, sz))
    drag[...] = s_asm
    fl = [flow[j].astype(F32).reshape(rows, sz) for j in range(3)]
    flat = a.reshape(3, rows, sz)
    blocks = []
    for c in range(3):
        grad_y = mul_left(dy[...], flat[c])
        planes = [a[c, i] for i in range(sx)]
        grad_x = []
        for i in range(sx):
            total = float(D1[i, 0]) * planes[0]
            for k in range(1, sx):
                total = total + float(D1[i, k]) * planes[k]
            grad_x.append(total)
        grad_x = jnp.concatenate(grad_x, 0)
        local = inverse_step * flat[c]
        local = local + fl[0] * grad_x + fl[1] * grad_y + fl[2] * grad_z[c]
        for j in range(3):
            local = local - grads[3 * c + j].astype(F32).reshape(rows, sz) * flat[j]
        local = m * local
        out = twin_z(twin_y(local.reshape(sx, sy, sz)).reshape(rows, sz))
        field[c] = out
        blocks.append(out)
    blocks.append(s_asm)
    x_high, z_high = member("gx"), member("gz")
    mx, mz = 1 - as_number(x_high), 1 - as_number(z_high)
    for c, block in enumerate(blocks):
        face = face_of(block, x_high, sy)
        slots[slot_of(1 - mx, mz), c * sy : (c + 1) * sy] = face
        slots[slot_of(mx, 1 - mz), c * 8 : (c + 1) * 8] = turned(pick[...], block)
        slots[slot_of(1 - mx, 1 - mz), c * 8 : (c + 1) * 8] = turned(
            pick[...], facing(face, x_high, rows)
        )


def join(blocks, got, place, x_high, z_high, x_ok, z_ok, sy):
    mx, mz = 1 - as_number(x_high), 1 - as_number(z_high)
    rows = blocks[0].shape[0]
    sz = blocks[0].shape[1]
    count = len(blocks)
    tiles = []
    for c in range(count):
        tile = picked(got[slot_of(mx, 1 - mz), c * 8 : (c + 1) * 8], z_high, z_ok)
        corner = picked(
            got[slot_of(1 - mx, 1 - mz), c * 8 : (c + 1) * 8], z_high, z_ok & x_ok
        )
        tiles.append(tile + corner)
    add = spread(tiles, place)
    out, cross = [], []
    for c in range(count):
        face = got[slot_of(1 - mx, mz), c * sy : (c + 1) * sy]
        face = jnp.where(x_ok, face, 0.0)
        part = add[c * rows : (c + 1) * rows]
        out.append(
            blocks[c] + facing(face, jnp.logical_not(x_high), rows) + part[:, :sz]
        )
        cross.append(part[:, sz:])
    return out, cross


def second_kernel(
    nx, field, drag, got, pick, place, field_out, drag_out, cross_out, slots
):
    rows = drag.shape[0]
    sy = rows // NODES
    x_high, z_high = member("gx"), member("gz")
    blocks = [field[0], field[1], field[2], drag[...]]
    blocks, cross = join(blocks, got, place[...], x_high, z_high, True, True, sy)
    slots[...] = jnp.zeros(slots.shape, F32)
    x_high, z_high = jnp.logical_not(x_high), jnp.logical_not(z_high)
    mx, mz = 1 - as_number(x_high), 1 - as_number(z_high)
    bends = []
    for c, block in enumerate(blocks):
        face = face_of(block, x_high, sy)
        slots[slot_of(1 - mx, mz), c * sy : (c + 1) * sy] = face
        slots[slot_of(mx, 1 - mz), c * 8 : (c + 1) * 8] = turned(pick[...], block)
        slots[slot_of(1 - mx, 1 - mz), c * 8 : (c + 1) * 8] = turned(
            pick[...], facing(face, x_high, rows)
        )
        if c < 3:
            field_out[c] = block
            cross_out[c] = cross[c]
            bend = contraction(block, x_high, sy, nx) + face_of(cross[c], x_high, sy)
            slots[slot_of(1 - mx, mz), (4 + c) * sy : (5 + c) * sy] = bend
            bends.append(bend)
        else:
            drag_out[...] = block
    bends.append(jnp.zeros((rows - 3 * sy, drag.shape[1]), F32))
    slots[slot_of(1 - mx, 1 - mz), 32:40] = turned(
        pick[...], jnp.concatenate(bends, 0)
    )


def third_kernel(
    nx,
    ny,
    nz,
    field,
    drag,
    cross,
    got,
    place,
    field_out,
    drag_out,
    cross_out,
    bend_out,
    slots,
):
    rows, sz = drag.shape
    sx = NODES
    sy = rows // sx
    x_high, z_high = jnp.logical_not(member("gx")), jnp.logical_not(member("gz"))
    x_ok = has_neighbour("gx", x_high, nx)
    z_ok = has_neighbour("gz", z_high, nz)
    mx, mz = 1 - as_number(x_high), 1 - as_number(z_high)
    blocks = [field[0], field[1], field[2], drag[...]]
    blocks, add = join(blocks, got, place[...], x_high, z_high, x_ok, z_ok, sy)
    tile = picked(got[slot_of(1 - mx, 1 - mz), 32:40], z_high, z_ok & x_ok)
    bend_add = spread([tile], place[...])
    partner = slot_of(1 - mx, mz)
    drag_out[...] = blocks[3]
    slots[...] = jnp.zeros(slots.shape, F32)
    x_high = jnp.logical_not(x_high)
    mx = 1 - as_number(x_high)
    j = lax.axis_index("gy")
    above = mx * ny + jnp.minimum(j + 1, ny - 1)
    below = mx * ny + jnp.maximum(j - 1, 0)
    beside = (1 - mx) * ny + j
    beside_above = (1 - mx) * ny + jnp.minimum(j + 1, ny - 1)
    beside_below = (1 - mx) * ny + jnp.maximum(j - 1, 0)
    top, bottom = sy - 1, 0
    for c in range(3):
        field_out[c] = blocks[c]
        cross_out[c] = cross[c] + add[c]
        bend = jnp.where(x_ok, got[partner, (4 + c) * sy : (5 + c) * sy], 0.0)
        bend = bend + bend_add[c * sy : (c + 1) * sy, :sz]
        bend_out[c] = bend
        own = contraction(blocks[c], x_high, sy, nx)
        slots[beside, c * sy : (c + 1) * sy] = own
        slots[beside_above, 48 + c : 49 + c] = own[top:]
        slots[beside_below, 48 + c : 49 + c] = own[:1]

        def row(ref, y):
            return ref[c, pl.ds(y, sx, stride=sy), :]

        up = row(cross_out, top)
        for k in range(7):
            up = up + float(K1[7, k]) * row(field_out, sy - 8 + k)
        down = row(cross_out, bottom)
        for k in range(1, 8):
            down = down + float(K1[0, k]) * row(field_out, k)
        slots[above, c * 16 : c * 16 + 8] = row(field_out, top)
        slots[above, c * 16 + 8 : c * 16 + 16] = up
        slots[above, 56 + c : 57 + c] = bend[top:]
        slots[below, c * 16 : c * 16 + 8] = row(field_out, bottom)
        slots[below, c * 16 + 8 : c * 16 + 16] = down
        slots[below, 56 + c : 57 + c] = bend[:1]
    slots[above, 48:56] = drag_out[pl.ds(top, sx, stride=sy), :]
    slots[below, 48:56] = drag_out[pl.ds(bottom, sx, stride=sy), :]


def keep_mask(shape, sy, counts):
    row = lax.broadcasted_iota(jnp.int32, shape, 0)
    z = lax.broadcasted_iota(jnp.int32, shape, 1)
    shift = sy.bit_length() - 1
    x = lax.shift_right_logical(row, shift)
    y = row & (sy - 1)
    sx = shape[0] // sy
    mask = None
    for axis, spot, size in (("gx", x, sx), ("gy", y, sy), ("gz", z, shape[1])):
        here = spot + lax.axis_index(axis) * size
        inside = (here != 0) & (here != counts[axis] * size - 1)
        mask = inside if mask is None else mask & inside
    return mask


def line_pattern(values, shape):
    spot = lax.broadcasted_iota(jnp.int32, shape, 1) & (NODES - 1)
    out = jnp.full(shape, float(values[0]), F32)
    for k in range(1, NODES):
        out = jnp.where(spot == k, float(values[k]), out)
    return out


def moments_kernel(
    counts,
    sy,
    field,
    drag_in,
    cross,
    bend_odd,
    sponge,
    got,
    plane_asm,
    line_asm,
    plane_own,
    line_own,
    mass,
    share,
    plane_weight_asm,
    plane_weight,
    base,
    image,
    sums,
    ext,
    drag,
):
    rows, sz = drag.shape
    sx = rows // sy
    ny = counts["gy"]
    keep = keep_mask((rows, sz), sy, counts)
    x_high = member("gx")
    mx = 1 - as_number(x_high)
    j = lax.axis_index("gy")
    low_ok, high_ok = j > 0, j < ny - 1
    below = jnp.maximum(j - 1, 0)
    above = jnp.minimum(j + 1, ny - 1)
    low = jnp.where(low_ok, got[mx * ny + below], 0.0)
    high = jnp.where(high_ok, got[mx * ny + above], 0.0)
    beside_low = jnp.where(low_ok, got[(1 - mx) * ny + below, 48:56], 0.0)
    beside_high = jnp.where(high_ok, got[(1 - mx) * ny + above, 48:56], 0.0)
    bottom, top = pl.ds(0, sx, stride=sy), pl.ds(sy - 1, sx, stride=sy)
    drag[...] = drag_in[...]
    drag[bottom, :] = drag_in[bottom, :] + low[48:56]
    drag[top, :] = drag_in[top, :] + high[48:56]
    used = rows + 2 * sy
    gap = jnp.zeros((sy - 2, sz), F32)
    for c in range(3):
        at = 16 * c
        ext[c, :rows] = field[c]
        ext[c, bottom, :] = field[c, bottom, :] + low[at : at + 8]
        ext[c, top, :] = field[c, top, :] + high[at : at + 8]
        odd = bend_odd[c] + jnp.concatenate(
            [low[56 + c : 57 + c], gap, high[56 + c : 57 + c]], 0
        )
        even = got[(1 - mx) * ny + j, c * sy : (c + 1) * sy] + jnp.concatenate(
            [beside_low[c : c + 1], gap, beside_high[c : c + 1]], 0
        )
        ext[c, rows : rows + sy] = jnp.where(x_high, odd, even)
        ext[c, rows + sy : used] = jnp.where(x_high, even, odd)
        ext[c, used : used + 8] = low[at + 8 : at + 16]
        ext[c, used + 8 : used + 16] = high[at + 8 : at + 16]
        ext[c, used + 16 :] = jnp.zeros((rows - 2 * sy - 16, sz), F32)
    s_asm = drag[...]
    s_own = mass[...] * (inverse_step + sponge[...].reshape(rows, sz))
    line_weight = line_pattern(W1, (1, sz))
    line_weight_asm = line_pattern(assembled_weights(NODES), (1, sz))
    total = [jnp.zeros((1, sz), F32) for _ in range(4)]
    for c in range(3):
        whole = ext[c]
        v = jnp.where(keep, whole[:rows], 0.0)
        plane = mul_left(plane_asm[...], jnp.concatenate([v, whole[rows:]], 0))
        line = mul_right(v, line_asm[...]) + cross[c]
        stiff = plane * line_weight_asm + line * plane_weight_asm[...]
        u = jnp.where(keep, s_asm * v + viscosity * stiff, 0.0)
        stiff = (
            mul_left(plane_own[...], u) * line_weight
            + mul_right(u, line_own[...]) * plane_weight[...]
        )
        own = s_own * u + viscosity * stiff
        base[c] = v
        image[c] = u
        sv = share[...] * v
        su = share[...] * u
        for k, term in enumerate((sv * v, sv * u, su * u, u * own)):
            total[k] = total[k] + jnp.sum(term, axis=0, keepdims=True)
    spot = lax.broadcasted_iota(jnp.int32, (1, sz), 1)
    out = jnp.zeros((1, sz), F32)
    for k in range(4):
        out = jnp.where(spot == k, jnp.sum(total[k], axis=1, keepdims=True), out)
    sums[...] = jnp.broadcast_to(out, sums.shape)


def combine_kernel(base, image, sums, out):
    total = jnp.sum(sums[...], axis=0, keepdims=True)
    m0, m1, m2, m3 = (total[:, k : k + 1] for k in range(4))
    alpha = m0 / m1
    norm = m0 - 2.0 * alpha * m1 + alpha * alpha * m2
    grow = 1.0 + norm / m0
    bend = grow * grow * m1 - 2.0 * grow * alpha * m2 + alpha * alpha * m3
    alpha2 = norm / bend
    one = alpha + alpha2 * grow
    two = alpha * alpha2
    for c in range(3):
        out[c] = one * base[c] - two * image[c]


VMEM = pl.BlockSpec(memory_space=pltpu.VMEM)
HBM = pl.BlockSpec(memory_space=pltpu.HBM)


def call(kernel, operands, outs, fetch=False, scratch=()):
    shapes = [jax.ShapeDtypeStruct(s, F32) for s in outs]
    size = sum(4 * int(np.prod(s)) for s in outs) + sum(
        o.dtype.itemsize * o.size for o in operands
    )
    if fetch:
        operands = [pltpu.with_memory_space_constraint(o, pltpu.HBM) for o in operands]
    return pl.pallas_call(
        kernel,
        out_shape=shapes,
        in_specs=[HBM if fetch else VMEM] * len(operands),
        out_specs=[VMEM] * len(outs),
        scratch_shapes=[pltpu.VMEM(o.shape, o.dtype) for o in operands]
        + [pltpu.SemaphoreType.DMA((len(operands),))]
        if fetch
        else [pltpu.VMEM(s, F32) for s in scratch],
        compiler_params=pltpu.CompilerParams(vmem_limit_bytes=16 * 1024 * 1024),
        cost_estimate=pl.CostEstimate(
            flops=1_000_000, bytes_accessed=size, transcendentals=0
        ),
    )(*operands)


def pairs_of(count, start):
    return [((start + 2 * m) % count, (start + 2 * m + 1) % count) for m in range(count // 2)]


def groups_of(x_pairs, z_pairs, width):
    return [[x * width + z for x in xs for z in zs] for xs in x_pairs for zs in z_pairs]


def body(adjoint_state, base_flow, base_grads, sponge):
    _, sx, sy, sz = adjoint_state.shape
    rows = sx * sy
    size = 2 * rows
    used = rows + 2 * sy
    counts = {axis: lax.axis_size(axis) for axis in ("gx", "gy", "gz")}
    wx, wy, wz = W1, np.tile(W1, sy // NODES), np.tile(W1, sz // NODES)
    ax, ay = assembled_weights(sx), assembled_weights(sy)

    def f32(x):
        return jnp.asarray(x.astype(np.float32))

    def over_plane(x, y):
        return f32(np.broadcast_to(np.kron(x, y)[:, None], (rows, sz)))

    mass = f32(np.kron(wx, wy)[:, None] * wz[None, :])
    ends = np.ones(NODES)
    ends[0] = ends[-1] = 0.5
    share = f32(
        np.kron(ends, np.tile(ends, sy // NODES))[:, None]
        * np.tile(ends, sz // NODES)[None, :]
    )
    dy = jnp.asarray(left_operand(block_diag(D1, rows // NODES)))
    dz = jnp.asarray(right_operand(block_diag(D1, sz // NODES).T))
    pick = np.zeros((8, sz))
    pick[0, sz - 1] = 1.0
    pick[1, sz - 8 : sz - 1] = K1[7, :7]
    pick[2, 0] = 1.0
    pick[3, 1:8] = K1[0, 1:]
    pick = f32(pick)
    place = np.zeros((8, 2 * sz))
    place[0, 0] = place[1, sz] = place[2, sz - 1] = place[3, 2 * sz - 1] = 1.0
    place = jnp.asarray(np.tile(place, (3, 1)).astype(np.float32).astype(BF16))
    nx, ny, nz = counts["gx"], counts["gy"], counts["gz"]

    def exchange(slots, start):
        groups = groups_of(pairs_of(nx, start), pairs_of(nz, start), nz)
        return lax.all_to_all(
            slots, ("gx", "gz"), 0, 0, tiled=True, axis_index_groups=groups
        )

    block, plane = (3, rows, sz), (rows, sz)
    field, drag, slots = call(
        forcing_kernel,
        (adjoint_state, base_flow, base_grads, sponge, mass, dy, dz, pick),
        [block, plane, (4, 64, sz)],
        fetch=True,
    )
    got = exchange(slots, 0)
    field, drag, cross, slots = call(
        functools.partial(second_kernel, nx),
        (field, drag, got, pick, place),
        [block, plane, block, (4, 7 * sy, sz)],
    )
    got = exchange(slots, 1)
    field, drag, cross, bend, slots = call(
        functools.partial(third_kernel, nx, ny, nz),
        (field, drag, cross, got, place),
        [block, plane, block, (3, sy, sz), (2 * ny, 64, sz)],
    )
    every = [tuple(range(ny))]
    got = lax.all_to_all(
        slots,
        ("gx", "gy"),
        0,
        0,
        tiled=True,
        axis_index_groups=groups_of(pairs_of(nx, 0), every, ny),
    )

    plane_asm = np.zeros((rows, size))
    plane_asm[:, :rows] = np.kron(assembled_stiffness(sx), np.diag(ay)) + np.kron(
        np.diag(ax), assembled_stiffness(sy)
    )
    for y in range(sy):
        plane_asm[y, rows + y] = ay[y]
        plane_asm[rows - sy + y, rows + sy + y] = ay[y]
    for x in range(sx):
        plane_asm[x * sy, used + x] = ax[x]
        plane_asm[x * sy + sy - 1, used + sx + x] = ax[x]
    plane_own = np.kron(K1, np.diag(wy)) + np.kron(
        np.diag(wx), block_diag(K1, sy // NODES)
    )
    slots = counts["gz"]
    base, image, sums = call(
        functools.partial(moments_kernel, counts, sy),
        (
            field,
            drag,
            cross,
            bend,
            sponge,
            got,
            jnp.asarray(left_operand(plane_asm)),
            jnp.asarray(right_operand(assembled_stiffness(sz).T)),
            jnp.asarray(left_operand(plane_own)),
            jnp.asarray(right_operand(block_diag(K1, sz // NODES).T)),
            mass,
            share,
            over_plane(ax, ay),
            over_plane(wx, wy),
        ),
        [block, block, (slots, sz)],
        scratch=[(3, size, sz), plane],
    )
    sums = lax.all_to_all(sums, "gz", 0, 0, tiled=True)
    sums = jnp.sum(sums, axis=0, keepdims=True)
    slots = counts["gx"] * counts["gy"]
    sums = jnp.broadcast_to(sums, (slots, sz))
    sums = lax.all_to_all(sums, ("gx", "gy"), 0, 0, tiled=True)
    (out,) = call(combine_kernel, (base, image, sums), [(3, rows, sz)])
    return out.reshape(3, sx, sy, sz)


def solution(mesh):
    placed = (
        P(None, "gx", "gy", "gz"),
        P(None, "gx", "gy", "gz"),
        P(None, "gx", "gy", "gz"),
        P("gx", "gy", "gz"),
    )
    return jax.shard_map(
        body, mesh=mesh, in_specs=placed, out_specs=P(None, "gx", "gy", "gz"), check_vma=False
    )
```

```python
import functools

import jax
import jax.numpy as jnp
import numpy as np
from jax import lax
from jax.experimental import pallas as pl
from jax.experimental.pallas import tpu as pltpu
from jax.sharding import PartitionSpec as P

inverse_step = 2.0
viscosity = 0.05
F32 = jnp.float32
BF16 = jnp.bfloat16
NODES = 8


def gll_tables():
    degree = 7
    interior = np.array(
        [
            -0.8717401485096066,
            -0.5917001814331423,
            -0.2092992179024789,
            0.2092992179024789,
            0.5917001814331423,
            0.8717401485096066,
        ]
    )
    points = np.concatenate([[-1.0], interior, [1.0]])
    previous = np.ones(8)
    current = points * 1.0
    for degree_now in range(1, degree):
        following = ((2 * degree_now + 1) * points * current - degree_now * previous) / (
            degree_now + 1
        )
        previous = current
        current = following
    weights = 2.0 / (degree * (degree + 1) * current**2)
    matrix = np.zeros((8, 8))
    for row_idx in range(8):
        for col_idx in range(8):
            if row_idx != col_idx:
                matrix[row_idx, col_idx] = current[row_idx] / (
                    current[col_idx] * (points[row_idx] - points[col_idx])
                )
    matrix[0, 0] = -degree * (degree + 1) / 4.0
    matrix[7, 7] = degree * (degree + 1) / 4.0
    return (weights, matrix)


W1, D1 = gll_tables()
W1 = W1.astype(np.float32).astype(np.float64)
D1 = D1.astype(np.float32).astype(np.float64)
K1 = D1.T @ (W1[:, None] * D1)


def block_diag(small, count):
    return np.kron(np.eye(count), small)


def twin_matrix(length):
    out = np.eye(length)
    for i in range(NODES - 1, length - 1, NODES):
        out[i, i + 1] = 1.0
        out[i + 1, i] = 1.0
    return out


def assembled_stiffness(length):
    out = twin_matrix(length) @ block_diag(K1, length // NODES)
    out[0, 0] += K1[7, 7]
    out[-1, -1] += K1[0, 0]
    return out


def assembled_weights(length):
    out = np.tile(W1, length // NODES)
    out[0::NODES] *= 2.0
    out[NODES - 1 :: NODES] *= 2.0
    return out


def halves(matrix):
    high = matrix.astype(np.float32).astype(BF16)
    low = (matrix - high.astype(np.float64)).astype(np.float32).astype(BF16)
    return np.asarray(high), np.asarray(low)


def left_operand(matrix):
    high, low = halves(matrix)
    zero = np.zeros_like(low)
    return np.concatenate(
        [np.concatenate([high, high], 1), np.concatenate([low, zero], 1)], 0
    )


def right_operand(matrix):
    high, low = halves(matrix)
    zero = np.zeros_like(low)
    return np.concatenate(
        [np.concatenate([high, low], 1), np.concatenate([high, zero], 1)], 0
    )


def split(x):
    high = x.astype(BF16)
    low = (x - high.astype(F32)).astype(BF16)
    return high, low


def mul_left(operand, x):
    rows = operand.shape[0] // 2
    high, low = split(x)
    out = jnp.dot(operand, jnp.concatenate([high, low], 0), preferred_element_type=F32)
    return out[:rows] + out[rows:]


def mul_right(x, operand):
    cols = operand.shape[1] // 2
    high, low = split(x)
    out = jnp.dot(jnp.concatenate([high, low], 1), operand, preferred_element_type=F32)
    return out[:, :cols] + out[:, cols:]


def twin_z(x):
    length = x.shape[-1]
    lane = lax.broadcasted_iota(jnp.int32, x.shape, 1)
    after = pltpu.roll(x, length - 1, 1)
    before = pltpu.roll(x, 1, 1)
    spot = lane & (NODES - 1)
    upper = (spot == NODES - 1) & (lane != length - 1)
    lower = (spot == 0) & (lane != 0)
    return x + jnp.where(upper, after, 0.0) + jnp.where(lower, before, 0.0)


def twin_y(x):
    first, second = x[:, :8], x[:, 8:]
    row = lax.broadcasted_iota(jnp.int32, first.shape, 1)
    one = first + jnp.where(row == 7, second[:, 0:1], 0.0)
    two = second + jnp.where(row == 0, first[:, 7:8], 0.0)
    return jnp.concatenate([one, two], 1)


def member(axis):
    return (lax.axis_index(axis) & 1) == 0


def has_neighbour(axis, high, count):
    here = lax.axis_index(axis)
    return jnp.where(high, here < count - 1, here > 0)


def slot_of(x, z):
    return 2 * x + z


def as_number(flag):
    return jnp.where(flag, 1, 0)


def turned(pick, tile):
    count = pick.shape[0] // 2
    out = lax.dot_general(
        pick,
        jnp.concatenate(split(tile), 1),
        (((1,), (1,)), ((), ())),
        preferred_element_type=F32,
    )
    return out[:count] + out[count:]


def spread(tiles, place):
    both = jnp.concatenate(tiles, 1)
    high = both.astype(BF16)
    rest = both - high.astype(F32)
    mid = rest.astype(BF16)
    low = (rest - mid.astype(F32)).astype(BF16)
    parts = jnp.concatenate([high, mid, low], 0)
    return lax.dot_general(
        parts, place, (((0,), (0,)), ((), ())), preferred_element_type=F32
    )


def picked(tile, high, ok):
    row = lax.broadcasted_iota(jnp.int32, tile.shape, 0)
    start = jnp.where(high, 2, 0)
    use = (row >= start) & (row < start + 2) & ok
    return jnp.where(use, tile, 0.0)


def face_of(x, high, size):
    return jnp.where(high, x[-size:], x[:size])


def corner_at(packed, c, x_high, size, rows):
    start = jnp.where(x_high, rows - size, 0)
    moved = pltpu.roll(packed, lax.rem(start + rows - c * size, rows), 1)
    lane = lax.broadcasted_iota(jnp.int32, packed.shape, 1)
    return jnp.where((lane >= start) & (lane < start + size), moved, 0.0)


def facing(face, high, rows):
    gap = jnp.zeros((rows - face.shape[0], face.shape[1]), F32)
    return jnp.where(
        high, jnp.concatenate([face, gap], 0), jnp.concatenate([gap, face], 0)
    )


def contraction(x, high, size, nx):
    ix = lax.axis_index("gx")
    count = x.shape[0] // size
    total = None
    for i in range(count):
        upper = 0.0 if i == count - 1 else float(K1[7, i])
        lower = 0.0 if i == 0 else float(K1[0, i])
        scale = jnp.where(high, upper, lower).astype(F32)
        if i == 0:
            scale = jnp.where(ix == 0, 0.0, scale)
        if i == count - 1:
            scale = jnp.where(ix == nx - 1, 0.0, scale)
        term = scale * x[i * size : (i + 1) * size]
        total = term if total is None else total + term
    return total


def forcing_kernel(
    adj_hbm,
    flow_hbm,
    grads_hbm,
    sponge_hbm,
    mass_hbm,
    dy_hbm,
    dz_hbm,
    pick_hbm,
    field,
    drag,
    slots,
    adj,
    flow,
    grads,
    sponge,
    mass,
    dy,
    dz,
    pick,
    sems,
):
    copies = [
        pltpu.make_async_copy(src, dst, sems.at[k])
        for k, (src, dst) in enumerate(
            (
                (adj_hbm, adj),
                (dz_hbm, dz),
                (mass_hbm, mass),
                (sponge_hbm, sponge),
                (dy_hbm, dy),
                (flow_hbm, flow),
                (grads_hbm, grads),
                (pick_hbm, pick),
            )
        )
    ]
    for copy in copies:
        copy.start()
    slots[...] = jnp.zeros(slots.shape, F32)
    copies[0].wait()
    a = adj[...]
    _, sx, sy, sz = a.shape
    rows = sx * sy
    copies[1].wait()
    grad_z = mul_right(a.reshape(3 * rows, sz), dz[...]).reshape(3, rows, sz)
    for copy in copies[2:]:
        copy.wait()
    m = mass[...]
    s_local = m * (inverse_step + sponge[...].reshape(rows, sz))
    s_asm = twin_z(twin_y(s_local.reshape(sx, sy, sz)).reshape(rows, sz))
    drag[...] = s_asm
    fl = [flow[j].astype(F32).reshape(rows, sz) for j in range(3)]
    flat = a.reshape(3, rows, sz)
    blocks = []
    for c in range(3):
        grad_y = mul_left(dy[...], flat[c])
        planes = [a[c, i] for i in range(sx)]
        grad_x = []
        for i in range(sx):
            total = float(D1[i, 0]) * planes[0]
            for k in range(1, sx):
                total = total + float(D1[i, k]) * planes[k]
            grad_x.append(total)
        grad_x = jnp.concatenate(grad_x, 0)
        local = inverse_step * flat[c]
        local = local + fl[0] * grad_x + fl[1] * grad_y + fl[2] * grad_z[c]
        for j in range(3):
            local = local - grads[3 * c + j].astype(F32).reshape(rows, sz) * flat[j]
        local = m * local
        out = twin_z(twin_y(local.reshape(sx, sy, sz)).reshape(rows, sz))
        field[c] = out
        blocks.append(out)
    blocks.append(s_asm)
    x_high, z_high = member("gx"), member("gz")
    mx, mz = 1 - as_number(x_high), 1 - as_number(z_high)
    faces = []
    for c, block in enumerate(blocks):
        face = face_of(block, x_high, sy)
        slots[slot_of(1 - mx, mz), c * sy : (c + 1) * sy] = face
        slots[slot_of(mx, 1 - mz), c * 8 : (c + 1) * 8] = turned(pick[...], block)
        faces.append(face)
    faces.append(jnp.zeros((rows - 4 * sy, sz), F32))
    slots[slot_of(1 - mx, 1 - mz), 0:8] = turned(pick[...], jnp.concatenate(faces, 0))


def join(blocks, got, place, x_high, z_high, x_ok, z_ok, sy, bends=False):
    mx, mz = 1 - as_number(x_high), 1 - as_number(z_high)
    rows = blocks[0].shape[0]
    sz = blocks[0].shape[1]
    count = len(blocks)
    tiles = []
    packed = picked(got[slot_of(1 - mx, 1 - mz), 0:8], z_high, z_ok & x_ok)
    for c in range(count):
        tile = picked(got[slot_of(mx, 1 - mz), c * 8 : (c + 1) * 8], z_high, z_ok)
        tiles.append(tile + corner_at(packed, c, x_high, sy, rows))
    if bends:
        tiles.append(pltpu.roll(packed, rows - count * sy, 1))
    add = spread(tiles, place)
    out, cross = [], []
    for c in range(count):
        face = got[slot_of(1 - mx, mz), c * sy : (c + 1) * sy]
        face = jnp.where(x_ok, face, 0.0)
        part = add[c * rows : (c + 1) * rows]
        out.append(
            blocks[c] + facing(face, jnp.logical_not(x_high), rows) + part[:, :sz]
        )
        cross.append(part[:, sz:])
    return out, cross, add[count * rows :, :sz]


def second_kernel(
    nx, field, drag, got, pick, place, field_out, drag_out, cross_out, slots
):
    rows = drag.shape[0]
    sy = rows // NODES
    x_high, z_high = member("gx"), member("gz")
    blocks = [field[0], field[1], field[2], drag[...]]
    blocks, cross, _ = join(blocks, got, place[...], x_high, z_high, True, True, sy)
    slots[...] = jnp.zeros(slots.shape, F32)
    x_high, z_high = jnp.logical_not(x_high), jnp.logical_not(z_high)
    mx, mz = 1 - as_number(x_high), 1 - as_number(z_high)
    faces, bends = [], []
    for c, block in enumerate(blocks):
        face = face_of(block, x_high, sy)
        slots[slot_of(1 - mx, mz), c * sy : (c + 1) * sy] = face
        slots[slot_of(mx, 1 - mz), c * 8 : (c + 1) * 8] = turned(pick[...], block)
        faces.append(face)
        if c < 3:
            field_out[c] = block
            cross_out[c] = cross[c]
            bend = contraction(block, x_high, sy, nx) + face_of(cross[c], x_high, sy)
            slots[slot_of(1 - mx, mz), (4 + c) * sy : (5 + c) * sy] = bend
            bends.append(bend)
        else:
            drag_out[...] = block
    gap = jnp.zeros((rows - 7 * sy, drag.shape[1]), F32)
    slots[slot_of(1 - mx, 1 - mz), 0:8] = turned(
        pick[...], jnp.concatenate(faces + bends + [gap], 0)
    )


def third_kernel(
    nx,
    ny,
    nz,
    field,
    drag,
    cross,
    got,
    place,
    field_out,
    drag_out,
    cross_out,
    bend_out,
    slots,
):
    rows, sz = drag.shape
    sx = NODES
    sy = rows // sx
    x_high, z_high = jnp.logical_not(member("gx")), jnp.logical_not(member("gz"))
    x_ok = has_neighbour("gx", x_high, nx)
    z_ok = has_neighbour("gz", z_high, nz)
    mx, mz = 1 - as_number(x_high), 1 - as_number(z_high)
    blocks = [field[0], field[1], field[2], drag[...]]
    blocks, add, bend_add = join(
        blocks, got, place[...], x_high, z_high, x_ok, z_ok, sy, bends=True
    )
    partner = slot_of(1 - mx, mz)
    drag_out[...] = blocks[3]
    slots[...] = jnp.zeros(slots.shape, F32)
    x_high = jnp.logical_not(x_high)
    mx = 1 - as_number(x_high)
    j = lax.axis_index("gy")
    above = mx * ny + jnp.minimum(j + 1, ny - 1)
    below = mx * ny + jnp.maximum(j - 1, 0)
    beside = (1 - mx) * ny + j
    beside_above = (1 - mx) * ny + jnp.minimum(j + 1, ny - 1)
    beside_below = (1 - mx) * ny + jnp.maximum(j - 1, 0)
    top, bottom = sy - 1, 0
    for c in range(3):
        field_out[c] = blocks[c]
        cross_out[c] = cross[c] + add[c]
        bend = jnp.where(x_ok, got[partner, (4 + c) * sy : (5 + c) * sy], 0.0)
        bend = bend + bend_add[c * sy : (c + 1) * sy]
        bend_out[c] = bend
        own = contraction(blocks[c], x_high, sy, nx)
        slots[beside, c * sy : (c + 1) * sy] = own
        slots[beside_above, 48 + c : 49 + c] = own[top:]
        slots[beside_below, 48 + c : 49 + c] = own[:1]

        def row(ref, y):
            return ref[c, pl.ds(y, sx, stride=sy), :]

        up = row(cross_out, top)
        for k in range(7):
            up = up + float(K1[7, k]) * row(field_out, sy - 8 + k)
        down = row(cross_out, bottom)
        for k in range(1, 8):
            down = down + float(K1[0, k]) * row(field_out, k)
        slots[above, c * 16 : c * 16 + 8] = row(field_out, top)
        slots[above, c * 16 + 8 : c * 16 + 16] = up
        slots[above, 56 + c : 57 + c] = bend[top:]
        slots[below, c * 16 : c * 16 + 8] = row(field_out, bottom)
        slots[below, c * 16 + 8 : c * 16 + 16] = down
        slots[below, 56 + c : 57 + c] = bend[:1]
    slots[above, 48:56] = drag_out[pl.ds(top, sx, stride=sy), :]
    slots[below, 48:56] = drag_out[pl.ds(bottom, sx, stride=sy), :]


def keep_mask(shape, sy, counts):
    row = lax.broadcasted_iota(jnp.int32, shape, 0)
    z = lax.broadcasted_iota(jnp.int32, shape, 1)
    shift = sy.bit_length() - 1
    x = lax.shift_right_logical(row, shift)
    y = row & (sy - 1)
    sx = shape[0] // sy
    mask = None
    for axis, spot, size in (("gx", x, sx), ("gy", y, sy), ("gz", z, shape[1])):
        here = spot + lax.axis_index(axis) * size
        inside = (here != 0) & (here != counts[axis] * size - 1)
        mask = inside if mask is None else mask & inside
    return mask


def line_pattern(values, shape):
    spot = lax.broadcasted_iota(jnp.int32, shape, 1) & (NODES - 1)
    out = jnp.full(shape, float(values[0]), F32)
    for k in range(1, NODES):
        out = jnp.where(spot == k, float(values[k]), out)
    return out


def moments_kernel(
    counts,
    sy,
    field,
    drag_in,
    cross,
    bend_odd,
    sponge,
    got,
    plane_asm,
    line_asm,
    plane_own,
    line_own,
    mass,
    share,
    plane_weight_asm,
    plane_weight,
    base,
    image,
    sums,
    ext,
    drag,
):
    rows, sz = drag.shape
    sx = rows // sy
    ny = counts["gy"]
    keep = keep_mask((rows, sz), sy, counts)
    x_high = member("gx")
    mx = 1 - as_number(x_high)
    j = lax.axis_index("gy")
    low_ok, high_ok = j > 0, j < ny - 1
    below = jnp.maximum(j - 1, 0)
    above = jnp.minimum(j + 1, ny - 1)
    low = jnp.where(low_ok, got[mx * ny + below], 0.0)
    high = jnp.where(high_ok, got[mx * ny + above], 0.0)
    beside_low = jnp.where(low_ok, got[(1 - mx) * ny + below, 48:56], 0.0)
    beside_high = jnp.where(high_ok, got[(1 - mx) * ny + above, 48:56], 0.0)
    bottom, top = pl.ds(0, sx, stride=sy), pl.ds(sy - 1, sx, stride=sy)
    drag[...] = drag_in[...]
    drag[bottom, :] = drag_in[bottom, :] + low[48:56]
    drag[top, :] = drag_in[top, :] + high[48:56]
    used = rows + 2 * sy
    gap = jnp.zeros((sy - 2, sz), F32)
    for c in range(3):
        at = 16 * c
        ext[c, :rows] = field[c]
        ext[c, bottom, :] = field[c, bottom, :] + low[at : at + 8]
        ext[c, top, :] = field[c, top, :] + high[at : at + 8]
        odd = bend_odd[c] + jnp.concatenate(
            [low[56 + c : 57 + c], gap, high[56 + c : 57 + c]], 0
        )
        even = got[(1 - mx) * ny + j, c * sy : (c + 1) * sy] + jnp.concatenate(
            [beside_low[c : c + 1], gap, beside_high[c : c + 1]], 0
        )
        ext[c, rows : rows + sy] = jnp.where(x_high, odd, even)
        ext[c, rows + sy : used] = jnp.where(x_high, even, odd)
        ext[c, used : used + 8] = low[at + 8 : at + 16]
        ext[c, used + 8 : used + 16] = high[at + 8 : at + 16]
        ext[c, used + 16 :] = jnp.zeros((rows - 2 * sy - 16, sz), F32)
    s_asm = drag[...]
    s_own = mass[...] * (inverse_step + sponge[...].reshape(rows, sz))
    line_weight = line_pattern(W1, (1, sz))
    line_weight_asm = line_pattern(assembled_weights(NODES), (1, sz))
    total = [jnp.zeros((1, sz), F32) for _ in range(4)]
    for c in range(3):
        whole = ext[c]
        v = jnp.where(keep, whole[:rows], 0.0)
        plane = mul_left(plane_asm[...], jnp.concatenate([v, whole[rows:]], 0))
        line = mul_right(v, line_asm[...]) + cross[c]
        stiff = plane * line_weight_asm + line * plane_weight_asm[...]
        u = jnp.where(keep, s_asm * v + viscosity * stiff, 0.0)
        stiff = (
            mul_left(plane_own[...], u) * line_weight
            + mul_right(u, line_own[...]) * plane_weight[...]
        )
        own = s_own * u + viscosity * stiff
        base[c] = v
        image[c] = u
        sv = share[...] * v
        su = share[...] * u
        for k, term in enumerate((sv * v, sv * u, su * u, u * own)):
            total[k] = total[k] + jnp.sum(term, axis=0, keepdims=True)
    spot = lax.broadcasted_iota(jnp.int32, (1, sz), 1)
    out = jnp.zeros((1, sz), F32)
    for k in range(4):
        out = jnp.where(spot == k, jnp.sum(total[k], axis=1, keepdims=True), out)
    sums[...] = jnp.broadcast_to(out, sums.shape)


def combine_kernel(base, image, sums, out):
    total = jnp.sum(sums[...], axis=0, keepdims=True)
    m0, m1, m2, m3 = (total[:, k : k + 1] for k in range(4))
    alpha = m0 / m1
    norm = m0 - 2.0 * alpha * m1 + alpha * alpha * m2
    grow = 1.0 + norm / m0
    bend = grow * grow * m1 - 2.0 * grow * alpha * m2 + alpha * alpha * m3
    alpha2 = norm / bend
    one = alpha + alpha2 * grow
    two = alpha * alpha2
    for c in range(3):
        out[c] = one * base[c] - two * image[c]


VMEM = pl.BlockSpec(memory_space=pltpu.VMEM)
HBM = pl.BlockSpec(memory_space=pltpu.HBM)


def call(kernel, operands, outs, fetch=False, scratch=()):
    shapes = [jax.ShapeDtypeStruct(s, F32) for s in outs]
    size = sum(4 * int(np.prod(s)) for s in outs) + sum(
        o.dtype.itemsize * o.size for o in operands
    )
    if fetch:
        operands = [pltpu.with_memory_space_constraint(o, pltpu.HBM) for o in operands]
    return pl.pallas_call(
        kernel,
        out_shape=shapes,
        in_specs=[HBM if fetch else VMEM] * len(operands),
        out_specs=[VMEM] * len(outs),
        scratch_shapes=[pltpu.VMEM(o.shape, o.dtype) for o in operands]
        + [pltpu.SemaphoreType.DMA((len(operands),))]
        if fetch
        else [pltpu.VMEM(s, F32) for s in scratch],
        compiler_params=pltpu.CompilerParams(vmem_limit_bytes=16 * 1024 * 1024),
        cost_estimate=pl.CostEstimate(
            flops=1_000_000, bytes_accessed=size, transcendentals=0
        ),
    )(*operands)


def pairs_of(count, start):
    return [((start + 2 * m) % count, (start + 2 * m + 1) % count) for m in range(count // 2)]


def groups_of(x_pairs, z_pairs, width):
    return [[x * width + z for x in xs for z in zs] for xs in x_pairs for zs in z_pairs]


def body(adjoint_state, base_flow, base_grads, sponge):
    _, sx, sy, sz = adjoint_state.shape
    rows = sx * sy
    size = 2 * rows
    used = rows + 2 * sy
    counts = {axis: lax.axis_size(axis) for axis in ("gx", "gy", "gz")}
    wx, wy, wz = W1, np.tile(W1, sy // NODES), np.tile(W1, sz // NODES)
    ax, ay = assembled_weights(sx), assembled_weights(sy)

    def f32(x):
        return jnp.asarray(x.astype(np.float32))

    def over_plane(x, y):
        return f32(np.broadcast_to(np.kron(x, y)[:, None], (rows, sz)))

    mass = f32(np.kron(wx, wy)[:, None] * wz[None, :])
    ends = np.ones(NODES)
    ends[0] = ends[-1] = 0.5
    share = f32(
        np.kron(ends, np.tile(ends, sy // NODES))[:, None]
        * np.tile(ends, sz // NODES)[None, :]
    )
    dy = jnp.asarray(left_operand(block_diag(D1, rows // NODES)))
    dz = jnp.asarray(right_operand(block_diag(D1, sz // NODES).T))
    pick = np.zeros((8, sz))
    pick[0, sz - 1] = 1.0
    pick[1, sz - 8 : sz - 1] = K1[7, :7]
    pick[2, 0] = 1.0
    pick[3, 1:8] = K1[0, 1:]
    pick = jnp.asarray(left_operand(pick))
    place = np.zeros((8, 2 * sz))
    place[0, 0] = place[1, sz] = place[2, sz - 1] = place[3, 2 * sz - 1] = 1.0
    place = jnp.asarray(np.tile(place, (3, 1)).astype(np.float32).astype(BF16))
    nx, ny, nz = counts["gx"], counts["gy"], counts["gz"]

    def exchange(slots, start):
        groups = groups_of(pairs_of(nx, start), pairs_of(nz, start), nz)
        return lax.all_to_all(
            slots, ("gx", "gz"), 0, 0, tiled=True, axis_index_groups=groups
        )

    block, plane = (3, rows, sz), (rows, sz)
    field, drag, slots = call(
        forcing_kernel,
        (adjoint_state, base_flow, base_grads, sponge, mass, dy, dz, pick),
        [block, plane, (4, 64, sz)],
        fetch=True,
    )
    got = exchange(slots, 0)
    field, drag, cross, slots = call(
        functools.partial(second_kernel, nx),
        (field, drag, got, pick, place),
        [block, plane, block, (4, 7 * sy, sz)],
    )
    got = exchange(slots, 1)
    field, drag, cross, bend, slots = call(
        functools.partial(third_kernel, nx, ny, nz),
        (field, drag, cross, got, place),
        [block, plane, block, (3, sy, sz), (2 * ny, 64, sz)],
    )
    every = [tuple(range(ny))]
    got = lax.all_to_all(
        slots,
        ("gx", "gy"),
        0,
        0,
        tiled=True,
        axis_index_groups=groups_of(pairs_of(nx, 0), every, ny),
    )

    plane_asm = np.zeros((rows, size))
    plane_asm[:, :rows] = np.kron(assembled_stiffness(sx), np.diag(ay)) + np.kron(
        np.diag(ax), assembled_stiffness(sy)
    )
    for y in range(sy):
        plane_asm[y, rows + y] = ay[y]
        plane_asm[rows - sy + y, rows + sy + y] = ay[y]
    for x in range(sx):
        plane_asm[x * sy, used + x] = ax[x]
        plane_asm[x * sy + sy - 1, used + sx + x] = ax[x]
    plane_own = np.kron(K1, np.diag(wy)) + np.kron(
        np.diag(wx), block_diag(K1, sy // NODES)
    )
    slots = counts["gz"]
    base, image, sums = call(
        functools.partial(moments_kernel, counts, sy),
        (
            field,
            drag,
            cross,
            bend,
            sponge,
            got,
            jnp.asarray(left_operand(plane_asm)),
            jnp.asarray(right_operand(assembled_stiffness(sz).T)),
            jnp.asarray(left_operand(plane_own)),
            jnp.asarray(right_operand(block_diag(K1, sz // NODES).T)),
            mass,
            share,
            over_plane(ax, ay),
            over_plane(wx, wy),
        ),
        [block, block, (slots, sz)],
        scratch=[(3, size, sz), plane],
    )
    sums = lax.all_to_all(sums, "gz", 0, 0, tiled=True)
    sums = jnp.sum(sums, axis=0, keepdims=True)
    slots = counts["gx"] * counts["gy"]
    sums = jnp.broadcast_to(sums, (slots, sz))
    sums = lax.all_to_all(sums, ("gx", "gy"), 0, 0, tiled=True)
    (out,) = call(combine_kernel, (base, image, sums), [(3, rows, sz)])
    return out.reshape(3, sx, sy, sz)


def solution(mesh):
    placed = (
        P(None, "gx", "gy", "gz"),
        P(None, "gx", "gy", "gz"),
        P(None, "gx", "gy", "gz"),
        P("gx", "gy", "gz"),
    )
    return jax.shard_map(
        body, mesh=mesh, in_specs=placed, out_specs=P(None, "gx", "gy", "gz"), check_vma=False
    )
```

```python
import functools

import jax
import jax.numpy as jnp
import numpy as np
from jax import lax
from jax.experimental import pallas as pl
from jax.experimental.pallas import tpu as pltpu
from jax.sharding import PartitionSpec as P

inverse_step = 2.0
viscosity = 0.05
F32 = jnp.float32
BF16 = jnp.bfloat16
NODES = 8


def gll_tables():
    degree = 7
    interior = np.array(
        [
            -0.8717401485096066,
            -0.5917001814331423,
            -0.2092992179024789,
            0.2092992179024789,
            0.5917001814331423,
            0.8717401485096066,
        ]
    )
    points = np.concatenate([[-1.0], interior, [1.0]])
    previous = np.ones(8)
    current = points * 1.0
    for degree_now in range(1, degree):
        following = ((2 * degree_now + 1) * points * current - degree_now * previous) / (
            degree_now + 1
        )
        previous = current
        current = following
    weights = 2.0 / (degree * (degree + 1) * current**2)
    matrix = np.zeros((8, 8))
    for row_idx in range(8):
        for col_idx in range(8):
            if row_idx != col_idx:
                matrix[row_idx, col_idx] = current[row_idx] / (
                    current[col_idx] * (points[row_idx] - points[col_idx])
                )
    matrix[0, 0] = -degree * (degree + 1) / 4.0
    matrix[7, 7] = degree * (degree + 1) / 4.0
    return (weights, matrix)


W1, D1 = gll_tables()
W1 = W1.astype(np.float32).astype(np.float64)
D1 = D1.astype(np.float32).astype(np.float64)
K1 = D1.T @ (W1[:, None] * D1)


def block_diag(small, count):
    return np.kron(np.eye(count), small)


def twin_matrix(length):
    out = np.eye(length)
    for i in range(NODES - 1, length - 1, NODES):
        out[i, i + 1] = 1.0
        out[i + 1, i] = 1.0
    return out


def assembled_stiffness(length):
    out = twin_matrix(length) @ block_diag(K1, length // NODES)
    out[0, 0] += K1[7, 7]
    out[-1, -1] += K1[0, 0]
    return out


def assembled_weights(length):
    out = np.tile(W1, length // NODES)
    out[0::NODES] *= 2.0
    out[NODES - 1 :: NODES] *= 2.0
    return out


def halves(matrix):
    high = matrix.astype(np.float32).astype(BF16)
    low = (matrix - high.astype(np.float64)).astype(np.float32).astype(BF16)
    return np.asarray(high), np.asarray(low)


def left_operand(matrix):
    high, low = halves(matrix)
    zero = np.zeros_like(low)
    return np.concatenate(
        [np.concatenate([high, high], 1), np.concatenate([low, zero], 1)], 0
    )


def right_operand(matrix):
    high, low = halves(matrix)
    zero = np.zeros_like(low)
    return np.concatenate(
        [np.concatenate([high, low], 1), np.concatenate([high, zero], 1)], 0
    )


def split(x):
    high = x.astype(BF16)
    low = (x - high.astype(F32)).astype(BF16)
    return high, low


def mul_left(operand, x):
    rows = operand.shape[0] // 2
    high, low = split(x)
    out = jnp.dot(operand, jnp.concatenate([high, low], 0), preferred_element_type=F32)
    return out[:rows] + out[rows:]


def mul_right(x, operand):
    cols = operand.shape[1] // 2
    high, low = split(x)
    out = jnp.dot(jnp.concatenate([high, low], 1), operand, preferred_element_type=F32)
    return out[:, :cols] + out[:, cols:]


def twin_z(x):
    length = x.shape[-1]
    lane = lax.broadcasted_iota(jnp.int32, x.shape, 1)
    after = pltpu.roll(x, length - 1, 1)
    before = pltpu.roll(x, 1, 1)
    spot = lane & (NODES - 1)
    upper = (spot == NODES - 1) & (lane != length - 1)
    lower = (spot == 0) & (lane != 0)
    return x + jnp.where(upper, after, 0.0) + jnp.where(lower, before, 0.0)


def twin_y(x):
    first, second = x[:, :8], x[:, 8:]
    row = lax.broadcasted_iota(jnp.int32, first.shape, 1)
    one = first + jnp.where(row == 7, second[:, 0:1], 0.0)
    two = second + jnp.where(row == 0, first[:, 7:8], 0.0)
    return jnp.concatenate([one, two], 1)


def member(axis):
    return (lax.axis_index(axis) & 1) == 0


def has_neighbour(axis, high, count):
    here = lax.axis_index(axis)
    return jnp.where(high, here < count - 1, here > 0)


def slot_of(x, z):
    return 2 * x + z


def as_number(flag):
    return jnp.where(flag, 1, 0)


def turned(pick, tile):
    count = pick.shape[0] // 2
    out = lax.dot_general(
        pick,
        jnp.concatenate(split(tile), 1),
        (((1,), (1,)), ((), ())),
        preferred_element_type=F32,
    )
    return out[:count] + out[count:]


def spread(tiles, place):
    both = jnp.concatenate(tiles, 1)
    high = both.astype(BF16)
    rest = both - high.astype(F32)
    mid = rest.astype(BF16)
    low = (rest - mid.astype(F32)).astype(BF16)
    parts = jnp.concatenate([high, mid, low], 0)
    return lax.dot_general(
        parts, place, (((0,), (0,)), ((), ())), preferred_element_type=F32
    )


def picked(tile, high, ok):
    row = lax.broadcasted_iota(jnp.int32, tile.shape, 0)
    start = jnp.where(high, 2, 0)
    use = (row >= start) & (row < start + 2) & ok
    return jnp.where(use, tile, 0.0)


def face_of(x, high, size):
    return jnp.where(high, x[-size:], x[:size])


def corner_at(packed, c, x_high, size, rows):
    start = jnp.where(x_high, rows - size, 0)
    moved = pltpu.roll(packed, lax.rem(start + rows - c * size, rows), 1)
    lane = lax.broadcasted_iota(jnp.int32, packed.shape, 1)
    return jnp.where((lane >= start) & (lane < start + size), moved, 0.0)


def facing(face, high, rows):
    gap = jnp.zeros((rows - face.shape[0], face.shape[1]), F32)
    return jnp.where(
        high, jnp.concatenate([face, gap], 0), jnp.concatenate([gap, face], 0)
    )


def contraction(x, high, size, nx):
    ix = lax.axis_index("gx")
    count = x.shape[0] // size
    total = None
    for i in range(count):
        upper = 0.0 if i == count - 1 else float(K1[7, i])
        lower = 0.0 if i == 0 else float(K1[0, i])
        scale = jnp.where(high, upper, lower).astype(F32)
        if i == 0:
            scale = jnp.where(ix == 0, 0.0, scale)
        if i == count - 1:
            scale = jnp.where(ix == nx - 1, 0.0, scale)
        term = scale * x[i * size : (i + 1) * size]
        total = term if total is None else total + term
    return total


def forcing_kernel(
    adj_hbm,
    flow_hbm,
    grads_hbm,
    sponge_hbm,
    mass_hbm,
    dy_hbm,
    dz_hbm,
    pick_hbm,
    field,
    drag,
    slots,
    adj,
    flow,
    grads,
    sponge,
    mass,
    dy,
    dz,
    pick,
    sems,
):
    copies = [
        pltpu.make_async_copy(src, dst, sems.at[k])
        for k, (src, dst) in enumerate(
            (
                (adj_hbm, adj),
                (dz_hbm, dz),
                (mass_hbm, mass),
                (sponge_hbm, sponge),
                (dy_hbm, dy),
                (flow_hbm, flow),
                (grads_hbm, grads),
                (pick_hbm, pick),
            )
        )
    ]
    for copy in copies:
        copy.start()
    slots[...] = jnp.zeros(slots.shape, F32)
    copies[0].wait()
    a = adj[...]
    _, sx, sy, sz = a.shape
    rows = sx * sy
    copies[1].wait()
    grad_z = mul_right(a.reshape(3 * rows, sz), dz[...]).reshape(3, rows, sz)
    for copy in copies[2:]:
        copy.wait()
    m = mass[...]
    s_local = m * (inverse_step + sponge[...].reshape(rows, sz))
    s_asm = twin_z(twin_y(s_local.reshape(sx, sy, sz)).reshape(rows, sz))
    drag[...] = s_asm
    fl = [flow[j].astype(F32).reshape(rows, sz) for j in range(3)]
    flat = a.reshape(3, rows, sz)
    blocks = []
    for c in range(3):
        grad_y = mul_left(dy[...], flat[c])
        planes = [a[c, i] for i in range(sx)]
        grad_x = []
        for i in range(sx):
            total = float(D1[i, 0]) * planes[0]
            for k in range(1, sx):
                total = total + float(D1[i, k]) * planes[k]
            grad_x.append(total)
        grad_x = jnp.concatenate(grad_x, 0)
        local = inverse_step * flat[c]
        local = local + fl[0] * grad_x + fl[1] * grad_y + fl[2] * grad_z[c]
        for j in range(3):
            local = local - grads[3 * c + j].astype(F32).reshape(rows, sz) * flat[j]
        local = m * local
        out = twin_z(twin_y(local.reshape(sx, sy, sz)).reshape(rows, sz))
        field[c] = out
        blocks.append(out)
    blocks.append(s_asm)
    x_high, z_high = member("gx"), member("gz")
    mx, mz = 1 - as_number(x_high), 1 - as_number(z_high)
    faces = []
    for c, block in enumerate(blocks):
        face = face_of(block, x_high, sy)
        slots[slot_of(1 - mx, mz), c * sy : (c + 1) * sy] = face
        slots[slot_of(mx, 1 - mz), c * 8 : (c + 1) * 8] = turned(pick[...], block)
        faces.append(face)
    faces.append(jnp.zeros((rows - 4 * sy, sz), F32))
    slots[slot_of(1 - mx, 1 - mz), 0:8] = turned(pick[...], jnp.concatenate(faces, 0))


def join(blocks, got, place, x_high, z_high, x_ok, z_ok, sy, bends=False):
    mx, mz = 1 - as_number(x_high), 1 - as_number(z_high)
    rows = blocks[0].shape[0]
    sz = blocks[0].shape[1]
    count = len(blocks)
    tiles = []
    packed = picked(got[slot_of(1 - mx, 1 - mz), 0:8], z_high, z_ok & x_ok)
    for c in range(count):
        tile = picked(got[slot_of(mx, 1 - mz), c * 8 : (c + 1) * 8], z_high, z_ok)
        tiles.append(tile + corner_at(packed, c, x_high, sy, rows))
    if bends:
        tiles.append(pltpu.roll(packed, rows - count * sy, 1))
    add = spread(tiles, place)
    out, cross = [], []
    for c in range(count):
        face = got[slot_of(1 - mx, mz), c * sy : (c + 1) * sy]
        face = jnp.where(x_ok, face, 0.0)
        part = add[c * rows : (c + 1) * rows]
        out.append(
            blocks[c] + facing(face, jnp.logical_not(x_high), rows) + part[:, :sz]
        )
        cross.append(part[:, sz:])
    return out, cross, add[count * rows :, :sz]


def second_kernel(
    nx, field, drag, got, pick, place, field_out, drag_out, cross_out, slots
):
    rows = drag.shape[0]
    sy = rows // NODES
    x_high, z_high = member("gx"), member("gz")
    blocks = [field[0], field[1], field[2], drag[...]]
    blocks, cross, _ = join(blocks, got, place[...], x_high, z_high, True, True, sy)
    slots[...] = jnp.zeros(slots.shape, F32)
    x_high, z_high = jnp.logical_not(x_high), jnp.logical_not(z_high)
    mx, mz = 1 - as_number(x_high), 1 - as_number(z_high)
    faces, bends = [], []
    for c, block in enumerate(blocks):
        face = face_of(block, x_high, sy)
        slots[slot_of(1 - mx, mz), c * sy : (c + 1) * sy] = face
        slots[slot_of(mx, 1 - mz), c * 8 : (c + 1) * 8] = turned(pick[...], block)
        faces.append(face)
        if c < 3:
            field_out[c] = block
            cross_out[c] = cross[c]
            bend = contraction(block, x_high, sy, nx) + face_of(cross[c], x_high, sy)
            slots[slot_of(1 - mx, mz), (4 + c) * sy : (5 + c) * sy] = bend
            bends.append(bend)
        else:
            drag_out[...] = block
    gap = jnp.zeros((rows - 7 * sy, drag.shape[1]), F32)
    slots[slot_of(1 - mx, 1 - mz), 0:8] = turned(
        pick[...], jnp.concatenate(faces + bends + [gap], 0)
    )


def third_kernel(
    nx,
    ny,
    nz,
    field,
    drag,
    cross,
    got,
    place,
    field_out,
    drag_out,
    cross_out,
    bend_out,
    slots,
):
    rows, sz = drag.shape
    sx = NODES
    sy = rows // sx
    x_high, z_high = jnp.logical_not(member("gx")), jnp.logical_not(member("gz"))
    x_ok = has_neighbour("gx", x_high, nx)
    z_ok = has_neighbour("gz", z_high, nz)
    mx, mz = 1 - as_number(x_high), 1 - as_number(z_high)
    blocks = [field[0], field[1], field[2], drag[...]]
    blocks, add, bend_add = join(
        blocks, got, place[...], x_high, z_high, x_ok, z_ok, sy, bends=True
    )
    partner = slot_of(1 - mx, mz)
    drag_out[...] = blocks[3]
    slots[...] = jnp.zeros(slots.shape, F32)
    x_high = jnp.logical_not(x_high)
    mx = 1 - as_number(x_high)
    j = lax.axis_index("gy")
    above = mx * ny + jnp.minimum(j + 1, ny - 1)
    below = mx * ny + jnp.maximum(j - 1, 0)
    beside = (1 - mx) * ny + j
    beside_above = (1 - mx) * ny + jnp.minimum(j + 1, ny - 1)
    beside_below = (1 - mx) * ny + jnp.maximum(j - 1, 0)
    top, bottom = sy - 1, 0
    for c in range(3):
        field_out[c] = blocks[c]
        cross_out[c] = cross[c] + add[c]
        bend = jnp.where(x_ok, got[partner, (4 + c) * sy : (5 + c) * sy], 0.0)
        bend = bend + bend_add[c * sy : (c + 1) * sy]
        bend_out[c] = bend
        own = contraction(blocks[c], x_high, sy, nx)
        slots[beside, c * sy : (c + 1) * sy] = own
        slots[beside_above, 48 + c : 49 + c] = own[top:]
        slots[beside_below, 48 + c : 49 + c] = own[:1]

        def row(ref, y):
            return ref[c, pl.ds(y, sx, stride=sy), :]

        up = row(cross_out, top)
        for k in range(7):
            up = up + float(K1[7, k]) * row(field_out, sy - 8 + k)
        down = row(cross_out, bottom)
        for k in range(1, 8):
            down = down + float(K1[0, k]) * row(field_out, k)
        slots[above, c * 16 : c * 16 + 8] = row(field_out, top)
        slots[above, c * 16 + 8 : c * 16 + 16] = up
        slots[above, 56 + c : 57 + c] = bend[top:]
        slots[below, c * 16 : c * 16 + 8] = row(field_out, bottom)
        slots[below, c * 16 + 8 : c * 16 + 16] = down
        slots[below, 56 + c : 57 + c] = bend[:1]
    slots[above, 48:56] = drag_out[pl.ds(top, sx, stride=sy), :]
    slots[below, 48:56] = drag_out[pl.ds(bottom, sx, stride=sy), :]


def keep_mask(shape, sy, counts):
    row = lax.broadcasted_iota(jnp.int32, shape, 0)
    z = lax.broadcasted_iota(jnp.int32, shape, 1)
    shift = sy.bit_length() - 1
    x = lax.shift_right_logical(row, shift)
    y = row & (sy - 1)
    sx = shape[0] // sy
    mask = None
    for axis, spot, size in (("gx", x, sx), ("gy", y, sy), ("gz", z, shape[1])):
        here = spot + lax.axis_index(axis) * size
        inside = (here != 0) & (here != counts[axis] * size - 1)
        mask = inside if mask is None else mask & inside
    return mask


def line_pattern(values, shape):
    spot = lax.broadcasted_iota(jnp.int32, shape, 1) & (NODES - 1)
    out = jnp.full(shape, float(values[0]), F32)
    for k in range(1, NODES):
        out = jnp.where(spot == k, float(values[k]), out)
    return out


def moments_kernel(
    counts,
    sy,
    field,
    drag_in,
    cross,
    bend_odd,
    sponge,
    got,
    plane_asm,
    line_asm,
    plane_own,
    line_own,
    mass,
    share,
    plane_weight_asm,
    plane_weight,
    base,
    image,
    sums,
    ext,
    drag,
):
    rows, sz = drag.shape
    sx = rows // sy
    ny = counts["gy"]
    keep = keep_mask((rows, sz), sy, counts)
    x_high = member("gx")
    mx = 1 - as_number(x_high)
    j = lax.axis_index("gy")
    low_ok, high_ok = j > 0, j < ny - 1
    below = jnp.maximum(j - 1, 0)
    above = jnp.minimum(j + 1, ny - 1)
    low = jnp.where(low_ok, got[mx * ny + below], 0.0)
    high = jnp.where(high_ok, got[mx * ny + above], 0.0)
    beside_low = jnp.where(low_ok, got[(1 - mx) * ny + below, 48:56], 0.0)
    beside_high = jnp.where(high_ok, got[(1 - mx) * ny + above, 48:56], 0.0)
    bottom, top = pl.ds(0, sx, stride=sy), pl.ds(sy - 1, sx, stride=sy)
    drag[...] = drag_in[...]
    drag[bottom, :] = drag_in[bottom, :] + low[48:56]
    drag[top, :] = drag_in[top, :] + high[48:56]
    used = rows + 2 * sy
    gap = jnp.zeros((sy - 2, sz), F32)
    for c in range(3):
        at = 16 * c
        ext[c, :rows] = field[c]
        ext[c, bottom, :] = field[c, bottom, :] + low[at : at + 8]
        ext[c, top, :] = field[c, top, :] + high[at : at + 8]
        odd = bend_odd[c] + jnp.concatenate(
            [low[56 + c : 57 + c], gap, high[56 + c : 57 + c]], 0
        )
        even = got[(1 - mx) * ny + j, c * sy : (c + 1) * sy] + jnp.concatenate(
            [beside_low[c : c + 1], gap, beside_high[c : c + 1]], 0
        )
        ext[c, rows : rows + sy] = jnp.where(x_high, odd, even)
        ext[c, rows + sy : used] = jnp.where(x_high, even, odd)
        ext[c, used : used + 8] = low[at + 8 : at + 16]
        ext[c, used + 8 : used + 16] = high[at + 8 : at + 16]
        ext[c, used + 16 :] = jnp.zeros((rows - 2 * sy - 16, sz), F32)
    s_asm = drag[...]
    s_own = mass[...] * (inverse_step + sponge[...].reshape(rows, sz))
    line_weight = line_pattern(W1, (1, sz))
    line_weight_asm = line_pattern(assembled_weights(NODES), (1, sz))
    total = [jnp.zeros((1, sz), F32) for _ in range(4)]
    for c in range(3):
        whole = ext[c]
        v = jnp.where(keep, whole[:rows], 0.0)
        plane = mul_left(plane_asm[...], jnp.concatenate([v, whole[rows:]], 0))
        line = mul_right(v, line_asm[...]) + cross[c]
        stiff = plane * line_weight_asm + line * plane_weight_asm[...]
        u = jnp.where(keep, s_asm * v + viscosity * stiff, 0.0)
        stiff = (
            mul_left(plane_own[...], u) * line_weight
            + mul_right(u, line_own[...]) * plane_weight[...]
        )
        own = s_own * u + viscosity * stiff
        base[c] = v
        image[c] = u
        sv = share[...] * v
        su = share[...] * u
        for k, term in enumerate((sv * v, sv * u, su * u, u * own)):
            total[k] = total[k] + jnp.sum(term, axis=0, keepdims=True)
    spot = lax.broadcasted_iota(jnp.int32, (1, sz), 1)
    out = jnp.zeros((1, sz), F32)
    for k in range(4):
        out = jnp.where(spot == k, jnp.sum(total[k], axis=1, keepdims=True), out)
    sums[...] = jnp.broadcast_to(out, sums.shape)


def combine_kernel(base, image, sums, out):
    total = jnp.sum(sums[...], axis=0, keepdims=True)
    m0, m1, m2, m3 = (total[:, k : k + 1] for k in range(4))
    alpha = m0 / m1
    norm = m0 - 2.0 * alpha * m1 + alpha * alpha * m2
    grow = 1.0 + norm / m0
    bend = grow * grow * m1 - 2.0 * grow * alpha * m2 + alpha * alpha * m3
    alpha2 = norm / bend
    one = alpha + alpha2 * grow
    two = alpha * alpha2
    for c in range(3):
        out[c] = one * base[c] - two * image[c]


VMEM = pl.BlockSpec(memory_space=pltpu.VMEM)
HBM = pl.BlockSpec(memory_space=pltpu.HBM)


def call(kernel, operands, outs, fetch=False, scratch=()):
    shapes = [jax.ShapeDtypeStruct(s, F32) for s in outs]
    size = sum(4 * int(np.prod(s)) for s in outs) + sum(
        o.dtype.itemsize * o.size for o in operands
    )
    if fetch:
        operands = [pltpu.with_memory_space_constraint(o, pltpu.HBM) for o in operands]
    return pl.pallas_call(
        kernel,
        out_shape=shapes,
        in_specs=[HBM if fetch else VMEM] * len(operands),
        out_specs=[VMEM] * len(outs),
        scratch_shapes=[pltpu.VMEM(o.shape, o.dtype) for o in operands]
        + [pltpu.SemaphoreType.DMA((len(operands),))]
        if fetch
        else [pltpu.VMEM(s, F32) for s in scratch],
        compiler_params=pltpu.CompilerParams(vmem_limit_bytes=16 * 1024 * 1024),
        cost_estimate=pl.CostEstimate(
            flops=1_000_000, bytes_accessed=size, transcendentals=0
        ),
    )(*operands)


def pairs_of(count, start):
    return [((start + 2 * m) % count, (start + 2 * m + 1) % count) for m in range(count // 2)]


def groups_of(x_pairs, z_pairs, width):
    return [[x * width + z for x in xs for z in zs] for xs in x_pairs for zs in z_pairs]


def body(adjoint_state, base_flow, base_grads, sponge):
    _, sx, sy, sz = adjoint_state.shape
    rows = sx * sy
    size = 2 * rows
    used = rows + 2 * sy
    counts = {axis: lax.axis_size(axis) for axis in ("gx", "gy", "gz")}
    wx, wy, wz = W1, np.tile(W1, sy // NODES), np.tile(W1, sz // NODES)
    ax, ay = assembled_weights(sx), assembled_weights(sy)

    def f32(x):
        return jnp.asarray(x.astype(np.float32))

    def over_plane(x, y):
        return f32(np.broadcast_to(np.kron(x, y)[:, None], (rows, sz)))

    mass = f32(np.kron(wx, wy)[:, None] * wz[None, :])
    ends = np.ones(NODES)
    ends[0] = ends[-1] = 0.5
    share = f32(
        np.kron(ends, np.tile(ends, sy // NODES))[:, None]
        * np.tile(ends, sz // NODES)[None, :]
    )
    dy = jnp.asarray(left_operand(block_diag(D1, rows // NODES)))
    dz = jnp.asarray(right_operand(block_diag(D1, sz // NODES).T))
    pick = np.zeros((8, sz))
    pick[0, sz - 1] = 1.0
    pick[1, sz - 8 : sz - 1] = K1[7, :7]
    pick[2, 0] = 1.0
    pick[3, 1:8] = K1[0, 1:]
    pick = jnp.asarray(left_operand(pick))
    place = np.zeros((8, 2 * sz))
    place[0, 0] = place[1, sz] = place[2, sz - 1] = place[3, 2 * sz - 1] = 1.0
    place = jnp.asarray(np.tile(place, (3, 1)).astype(np.float32).astype(BF16))
    nx, ny, nz = counts["gx"], counts["gy"], counts["gz"]

    def exchange(slots, start):
        groups = groups_of(pairs_of(nx, start), pairs_of(nz, start), nz)
        return lax.all_to_all(
            slots, ("gx", "gz"), 0, 0, tiled=True, axis_index_groups=groups
        )

    block, plane = (3, rows, sz), (rows, sz)
    field, drag, slots = call(
        forcing_kernel,
        (adjoint_state, base_flow, base_grads, sponge, mass, dy, dz, pick),
        [block, plane, (4, 64, sz)],
        fetch=True,
    )
    got = exchange(slots, 0)
    field, drag, cross, slots = call(
        functools.partial(second_kernel, nx),
        (field, drag, got, pick, place),
        [block, plane, block, (4, 7 * sy, sz)],
    )
    got = exchange(slots, 1)
    field, drag, cross, bend, slots = call(
        functools.partial(third_kernel, nx, ny, nz),
        (field, drag, cross, got, place),
        [block, plane, block, (3, sy, sz), (2 * ny, 64, sz)],
    )
    every = [tuple(range(ny))]
    got = lax.all_to_all(
        slots,
        ("gx", "gy"),
        0,
        0,
        tiled=True,
        axis_index_groups=groups_of(pairs_of(nx, 0), every, ny),
    )

    plane_asm = np.zeros((rows, size))
    plane_asm[:, :rows] = np.kron(assembled_stiffness(sx), np.diag(ay)) + np.kron(
        np.diag(ax), assembled_stiffness(sy)
    )
    for y in range(sy):
        plane_asm[y, rows + y] = ay[y]
        plane_asm[rows - sy + y, rows + sy + y] = ay[y]
    for x in range(sx):
        plane_asm[x * sy, used + x] = ax[x]
        plane_asm[x * sy + sy - 1, used + sx + x] = ax[x]
    plane_own = np.kron(K1, np.diag(wy)) + np.kron(
        np.diag(wx), block_diag(K1, sy // NODES)
    )
    near = min(4, nz)
    runs = [tuple(range(k, k + near)) for k in range(0, nz, near)]
    first = groups_of(every, runs, nz)
    strides = [tuple(range(k, nz, near)) for k in range(near)]
    second = groups_of([tuple(range(nx))], strides, nz)
    base, image, sums = call(
        functools.partial(moments_kernel, counts, sy),
        (
            field,
            drag,
            cross,
            bend,
            sponge,
            got,
            jnp.asarray(left_operand(plane_asm)),
            jnp.asarray(right_operand(assembled_stiffness(sz).T)),
            jnp.asarray(left_operand(plane_own)),
            jnp.asarray(right_operand(block_diag(K1, sz // NODES).T)),
            mass,
            share,
            over_plane(ax, ay),
            over_plane(wx, wy),
        ),
        [block, block, (len(first[0]), sz)],
        scratch=[(3, size, sz), plane],
    )
    sums = lax.all_to_all(
        sums, ("gy", "gz"), 0, 0, tiled=True, axis_index_groups=first
    )
    sums = jnp.sum(sums, axis=0, keepdims=True)
    sums = jnp.broadcast_to(sums, (len(second[0]), sz))
    sums = lax.all_to_all(
        sums, ("gx", "gz"), 0, 0, tiled=True, axis_index_groups=second
    )
    (out,) = call(combine_kernel, (base, image, sums), [(3, rows, sz)])
    return out.reshape(3, sx, sy, sz)


def solution(mesh):
    placed = (
        P(None, "gx", "gy", "gz"),
        P(None, "gx", "gy", "gz"),
        P(None, "gx", "gy", "gz"),
        P("gx", "gy", "gz"),
    )
    return jax.shard_map(
        body, mesh=mesh, in_specs=placed, out_specs=P(None, "gx", "gy", "gz"), check_vma=False
    )
```

```python
import functools

import jax
import jax.numpy as jnp
import numpy as np
from jax import lax
from jax.experimental import pallas as pl
from jax.experimental.pallas import tpu as pltpu
from jax.sharding import PartitionSpec as P

inverse_step = 2.0
viscosity = 0.05
F32 = jnp.float32
BF16 = jnp.bfloat16
NODES = 8


def gll_tables():
    degree = 7
    interior = np.array(
        [
            -0.8717401485096066,
            -0.5917001814331423,
            -0.2092992179024789,
            0.2092992179024789,
            0.5917001814331423,
            0.8717401485096066,
        ]
    )
    points = np.concatenate([[-1.0], interior, [1.0]])
    previous = np.ones(8)
    current = points * 1.0
    for degree_now in range(1, degree):
        following = ((2 * degree_now + 1) * points * current - degree_now * previous) / (
            degree_now + 1
        )
        previous = current
        current = following
    weights = 2.0 / (degree * (degree + 1) * current**2)
    matrix = np.zeros((8, 8))
    for row_idx in range(8):
        for col_idx in range(8):
            if row_idx != col_idx:
                matrix[row_idx, col_idx] = current[row_idx] / (
                    current[col_idx] * (points[row_idx] - points[col_idx])
                )
    matrix[0, 0] = -degree * (degree + 1) / 4.0
    matrix[7, 7] = degree * (degree + 1) / 4.0
    return (weights, matrix)


W1, D1 = gll_tables()
W1 = W1.astype(np.float32).astype(np.float64)
D1 = D1.astype(np.float32).astype(np.float64)
K1 = D1.T @ (W1[:, None] * D1)


def block_diag(small, count):
    return np.kron(np.eye(count), small)


def twin_matrix(length):
    out = np.eye(length)
    for i in range(NODES - 1, length - 1, NODES):
        out[i, i + 1] = 1.0
        out[i + 1, i] = 1.0
    return out


def assembled_stiffness(length):
    out = twin_matrix(length) @ block_diag(K1, length // NODES)
    out[0, 0] += K1[7, 7]
    out[-1, -1] += K1[0, 0]
    return out


def assembled_weights(length):
    out = np.tile(W1, length // NODES)
    out[0::NODES] *= 2.0
    out[NODES - 1 :: NODES] *= 2.0
    return out


def halves(matrix):
    high = matrix.astype(np.float32).astype(BF16)
    low = (matrix - high.astype(np.float64)).astype(np.float32).astype(BF16)
    return np.asarray(high), np.asarray(low)


def left_operand(matrix):
    high, low = halves(matrix)
    zero = np.zeros_like(low)
    return np.concatenate(
        [np.concatenate([high, high], 1), np.concatenate([low, zero], 1)], 0
    )


def right_operand(matrix):
    high, low = halves(matrix)
    zero = np.zeros_like(low)
    return np.concatenate(
        [np.concatenate([high, low], 1), np.concatenate([high, zero], 1)], 0
    )


def split(x):
    high = x.astype(BF16)
    low = (x - high.astype(F32)).astype(BF16)
    return high, low


def mul_left(operand, x):
    rows = operand.shape[0] // 2
    high, low = split(x)
    out = jnp.dot(operand, jnp.concatenate([high, low], 0), preferred_element_type=F32)
    return out[:rows] + out[rows:]


def mul_right(x, operand):
    cols = operand.shape[1] // 2
    high, low = split(x)
    out = jnp.dot(jnp.concatenate([high, low], 1), operand, preferred_element_type=F32)
    return out[:, :cols] + out[:, cols:]


def twin_z(x):
    length = x.shape[-1]
    lane = lax.broadcasted_iota(jnp.int32, x.shape, 1)
    after = pltpu.roll(x, length - 1, 1)
    before = pltpu.roll(x, 1, 1)
    spot = lane & (NODES - 1)
    upper = (spot == NODES - 1) & (lane != length - 1)
    lower = (spot == 0) & (lane != 0)
    return x + jnp.where(upper, after, 0.0) + jnp.where(lower, before, 0.0)


def twin_y(x):
    first, second = x[:, :8], x[:, 8:]
    row = lax.broadcasted_iota(jnp.int32, first.shape, 1)
    one = first + jnp.where(row == 7, second[:, 0:1], 0.0)
    two = second + jnp.where(row == 0, first[:, 7:8], 0.0)
    return jnp.concatenate([one, two], 1)


def member(axis):
    return (lax.axis_index(axis) & 1) == 0


def has_neighbour(axis, high, count):
    here = lax.axis_index(axis)
    return jnp.where(high, here < count - 1, here > 0)


def slot_of(x, z):
    return 2 * x + z


def as_number(flag):
    return jnp.where(flag, 1, 0)


def turned(pick, tile):
    count = pick.shape[0] // 2
    out = lax.dot_general(
        pick,
        jnp.concatenate(split(tile), 1),
        (((1,), (1,)), ((), ())),
        preferred_element_type=F32,
    )
    return out[:count] + out[count:]


def spread(tiles, place):
    both = jnp.concatenate(tiles, 1)
    high = both.astype(BF16)
    rest = both - high.astype(F32)
    mid = rest.astype(BF16)
    low = (rest - mid.astype(F32)).astype(BF16)
    parts = jnp.concatenate([high, mid, low], 0)
    return lax.dot_general(
        parts, place, (((0,), (0,)), ((), ())), preferred_element_type=F32
    )


def picked(tile, high, ok):
    row = lax.broadcasted_iota(jnp.int32, tile.shape, 0)
    start = jnp.where(high, 2, 0)
    use = (row >= start) & (row < start + 2) & ok
    return jnp.where(use, tile, 0.0)


def face_of(x, high, size):
    return jnp.where(high, x[-size:], x[:size])


def corner_at(packed, c, x_high, size, rows):
    start = jnp.where(x_high, rows - size, 0)
    moved = pltpu.roll(packed, lax.rem(start + rows - c * size, rows), 1)
    lane = lax.broadcasted_iota(jnp.int32, packed.shape, 1)
    return jnp.where((lane >= start) & (lane < start + size), moved, 0.0)


def facing(face, high, rows):
    gap = jnp.zeros((rows - face.shape[0], face.shape[1]), F32)
    return jnp.where(
        high, jnp.concatenate([face, gap], 0), jnp.concatenate([gap, face], 0)
    )


def contraction(x, high, size, nx):
    ix = lax.axis_index("gx")
    count = x.shape[0] // size
    total = None
    for i in range(count):
        upper = 0.0 if i == count - 1 else float(K1[7, i])
        lower = 0.0 if i == 0 else float(K1[0, i])
        scale = jnp.where(high, upper, lower).astype(F32)
        if i == 0:
            scale = jnp.where(ix == 0, 0.0, scale)
        if i == count - 1:
            scale = jnp.where(ix == nx - 1, 0.0, scale)
        term = scale * x[i * size : (i + 1) * size]
        total = term if total is None else total + term
    return total


def forcing_kernel(
    adj_hbm,
    flow_hbm,
    grads_hbm,
    sponge_hbm,
    mass_hbm,
    dy_hbm,
    dz_hbm,
    pick_hbm,
    field,
    drag,
    slots,
    adj,
    flow,
    grads,
    sponge,
    mass,
    dy,
    dz,
    pick,
    sems,
):
    copies = [
        pltpu.make_async_copy(src, dst, sems.at[k])
        for k, (src, dst) in enumerate(
            (
                (adj_hbm, adj),
                (dz_hbm, dz),
                (grads_hbm, grads),
                (flow_hbm, flow),
                (dy_hbm, dy),
                (sponge_hbm, sponge),
                (mass_hbm, mass),
                (pick_hbm, pick),
            )
        )
    ]
    for copy in copies:
        copy.start()
    slots[...] = jnp.zeros(slots.shape, F32)
    copies[0].wait()
    a = adj[...]
    _, sx, sy, sz = a.shape
    rows = sx * sy
    copies[1].wait()
    grad_z = mul_right(a.reshape(3 * rows, sz), dz[...]).reshape(3, rows, sz)
    for copy in copies[2:]:
        copy.wait()
    m = mass[...]
    s_local = m * (inverse_step + sponge[...].reshape(rows, sz))
    s_asm = twin_z(twin_y(s_local.reshape(sx, sy, sz)).reshape(rows, sz))
    drag[...] = s_asm
    fl = [flow[j].astype(F32).reshape(rows, sz) for j in range(3)]
    flat = a.reshape(3, rows, sz)
    blocks = []
    for c in range(3):
        grad_y = mul_left(dy[...], flat[c])
        planes = [a[c, i] for i in range(sx)]
        grad_x = []
        for i in range(sx):
            total = float(D1[i, 0]) * planes[0]
            for k in range(1, sx):
                total = total + float(D1[i, k]) * planes[k]
            grad_x.append(total)
        grad_x = jnp.concatenate(grad_x, 0)
        local = inverse_step * flat[c]
        local = local + fl[0] * grad_x + fl[1] * grad_y + fl[2] * grad_z[c]
        for j in range(3):
            local = local - grads[3 * c + j].astype(F32).reshape(rows, sz) * flat[j]
        local = m * local
        out = twin_z(twin_y(local.reshape(sx, sy, sz)).reshape(rows, sz))
        field[c] = out
        blocks.append(out)
    blocks.append(s_asm)
    x_high, z_high = member("gx"), member("gz")
    mx, mz = 1 - as_number(x_high), 1 - as_number(z_high)
    faces = []
    for c, block in enumerate(blocks):
        face = face_of(block, x_high, sy)
        slots[slot_of(1 - mx, mz), c * sy : (c + 1) * sy] = face
        slots[slot_of(mx, 1 - mz), c * 8 : (c + 1) * 8] = turned(pick[...], block)
        faces.append(face)
    faces.append(jnp.zeros((rows - 4 * sy, sz), F32))
    slots[slot_of(1 - mx, 1 - mz), 0:8] = turned(pick[...], jnp.concatenate(faces, 0))


def join(blocks, got, place, x_high, z_high, x_ok, z_ok, sy, bends=False):
    mx, mz = 1 - as_number(x_high), 1 - as_number(z_high)
    rows = blocks[0].shape[0]
    sz = blocks[0].shape[1]
    count = len(blocks)
    tiles = []
    packed = picked(got[slot_of(1 - mx, 1 - mz), 0:8], z_high, z_ok & x_ok)
    for c in range(count):
        tile = picked(got[slot_of(mx, 1 - mz), c * 8 : (c + 1) * 8], z_high, z_ok)
        tiles.append(tile + corner_at(packed, c, x_high, sy, rows))
    if bends:
        tiles.append(pltpu.roll(packed, rows - count * sy, 1))
    add = spread(tiles, place)
    out, cross = [], []
    for c in range(count):
        face = got[slot_of(1 - mx, mz), c * sy : (c + 1) * sy]
        face = jnp.where(x_ok, face, 0.0)
        part = add[c * rows : (c + 1) * rows]
        out.append(
            blocks[c] + facing(face, jnp.logical_not(x_high), rows) + part[:, :sz]
        )
        cross.append(part[:, sz:])
    return out, cross, add[count * rows :, :sz]


def second_kernel(
    nx, field, drag, got, pick, place, field_out, drag_out, cross_out, slots
):
    rows = drag.shape[0]
    sy = rows // NODES
    x_high, z_high = member("gx"), member("gz")
    blocks = [field[0], field[1], field[2], drag[...]]
    blocks, cross, _ = join(blocks, got, place[...], x_high, z_high, True, True, sy)
    slots[...] = jnp.zeros(slots.shape, F32)
    x_high, z_high = jnp.logical_not(x_high), jnp.logical_not(z_high)
    mx, mz = 1 - as_number(x_high), 1 - as_number(z_high)
    faces, bends = [], []
    for c, block in enumerate(blocks):
        face = face_of(block, x_high, sy)
        slots[slot_of(1 - mx, mz), c * sy : (c + 1) * sy] = face
        slots[slot_of(mx, 1 - mz), c * 8 : (c + 1) * 8] = turned(pick[...], block)
        faces.append(face)
        if c < 3:
            field_out[c] = block
            cross_out[c] = cross[c]
            bend = contraction(block, x_high, sy, nx) + face_of(cross[c], x_high, sy)
            slots[slot_of(1 - mx, mz), (4 + c) * sy : (5 + c) * sy] = bend
            bends.append(bend)
        else:
            drag_out[...] = block
    gap = jnp.zeros((rows - 7 * sy, drag.shape[1]), F32)
    slots[slot_of(1 - mx, 1 - mz), 0:8] = turned(
        pick[...], jnp.concatenate(faces + bends + [gap], 0)
    )


def third_kernel(
    nx,
    ny,
    nz,
    field,
    drag,
    cross,
    got,
    place,
    field_out,
    drag_out,
    cross_out,
    bend_out,
    slots,
):
    rows, sz = drag.shape
    sx = NODES
    sy = rows // sx
    x_high, z_high = jnp.logical_not(member("gx")), jnp.logical_not(member("gz"))
    x_ok = has_neighbour("gx", x_high, nx)
    z_ok = has_neighbour("gz", z_high, nz)
    mx, mz = 1 - as_number(x_high), 1 - as_number(z_high)
    blocks = [field[0], field[1], field[2], drag[...]]
    blocks, add, bend_add = join(
        blocks, got, place[...], x_high, z_high, x_ok, z_ok, sy, bends=True
    )
    partner = slot_of(1 - mx, mz)
    drag_out[...] = blocks[3]
    slots[...] = jnp.zeros(slots.shape, F32)
    x_high = jnp.logical_not(x_high)
    mx = 1 - as_number(x_high)
    j = lax.axis_index("gy")
    above = mx * ny + jnp.minimum(j + 1, ny - 1)
    below = mx * ny + jnp.maximum(j - 1, 0)
    beside = (1 - mx) * ny + j
    beside_above = (1 - mx) * ny + jnp.minimum(j + 1, ny - 1)
    beside_below = (1 - mx) * ny + jnp.maximum(j - 1, 0)
    top, bottom = sy - 1, 0
    for c in range(3):
        field_out[c] = blocks[c]
        cross_out[c] = cross[c] + add[c]
        bend = jnp.where(x_ok, got[partner, (4 + c) * sy : (5 + c) * sy], 0.0)
        bend = bend + bend_add[c * sy : (c + 1) * sy]
        bend_out[c] = bend
        own = contraction(blocks[c], x_high, sy, nx)
        slots[beside, c * sy : (c + 1) * sy] = own
        slots[beside_above, 48 + c : 49 + c] = own[top:]
        slots[beside_below, 48 + c : 49 + c] = own[:1]

        def row(ref, y):
            return ref[c, pl.ds(y, sx, stride=sy), :]

        up = row(cross_out, top)
        for k in range(7):
            up = up + float(K1[7, k]) * row(field_out, sy - 8 + k)
        down = row(cross_out, bottom)
        for k in range(1, 8):
            down = down + float(K1[0, k]) * row(field_out, k)
        slots[above, c * 16 : c * 16 + 8] = row(field_out, top)
        slots[above, c * 16 + 8 : c * 16 + 16] = up
        slots[above, 56 + c : 57 + c] = bend[top:]
        slots[below, c * 16 : c * 16 + 8] = row(field_out, bottom)
        slots[below, c * 16 + 8 : c * 16 + 16] = down
        slots[below, 56 + c : 57 + c] = bend[:1]
    slots[above, 48:56] = drag_out[pl.ds(top, sx, stride=sy), :]
    slots[below, 48:56] = drag_out[pl.ds(bottom, sx, stride=sy), :]


def keep_mask(shape, sy, counts):
    row = lax.broadcasted_iota(jnp.int32, shape, 0)
    z = lax.broadcasted_iota(jnp.int32, shape, 1)
    shift = sy.bit_length() - 1
    x = lax.shift_right_logical(row, shift)
    y = row & (sy - 1)
    sx = shape[0] // sy
    mask = None
    for axis, spot, size in (("gx", x, sx), ("gy", y, sy), ("gz", z, shape[1])):
        here = spot + lax.axis_index(axis) * size
        inside = (here != 0) & (here != counts[axis] * size - 1)
        mask = inside if mask is None else mask & inside
    return mask


def line_pattern(values, shape):
    spot = lax.broadcasted_iota(jnp.int32, shape, 1) & (NODES - 1)
    out = jnp.full(shape, float(values[0]), F32)
    for k in range(1, NODES):
        out = jnp.where(spot == k, float(values[k]), out)
    return out


def moments_kernel(
    counts,
    sy,
    field,
    drag_in,
    cross,
    bend_odd,
    sponge,
    got,
    plane_asm,
    line_asm,
    plane_own,
    line_own,
    mass,
    share,
    plane_weight_asm,
    plane_weight,
    base,
    image,
    sums,
    ext,
    drag,
):
    rows, sz = drag.shape
    sx = rows // sy
    ny = counts["gy"]
    keep = keep_mask((rows, sz), sy, counts)
    x_high = member("gx")
    mx = 1 - as_number(x_high)
    j = lax.axis_index("gy")
    low_ok, high_ok = j > 0, j < ny - 1
    below = jnp.maximum(j - 1, 0)
    above = jnp.minimum(j + 1, ny - 1)
    low = jnp.where(low_ok, got[mx * ny + below], 0.0)
    high = jnp.where(high_ok, got[mx * ny + above], 0.0)
    beside_low = jnp.where(low_ok, got[(1 - mx) * ny + below, 48:56], 0.0)
    beside_high = jnp.where(high_ok, got[(1 - mx) * ny + above, 48:56], 0.0)
    bottom, top = pl.ds(0, sx, stride=sy), pl.ds(sy - 1, sx, stride=sy)
    drag[...] = drag_in[...]
    drag[bottom, :] = drag_in[bottom, :] + low[48:56]
    drag[top, :] = drag_in[top, :] + high[48:56]
    used = rows + 2 * sy
    gap = jnp.zeros((sy - 2, sz), F32)
    for c in range(3):
        at = 16 * c
        ext[c, :rows] = field[c]
        ext[c, bottom, :] = field[c, bottom, :] + low[at : at + 8]
        ext[c, top, :] = field[c, top, :] + high[at : at + 8]
        odd = bend_odd[c] + jnp.concatenate(
            [low[56 + c : 57 + c], gap, high[56 + c : 57 + c]], 0
        )
        even = got[(1 - mx) * ny + j, c * sy : (c + 1) * sy] + jnp.concatenate(
            [beside_low[c : c + 1], gap, beside_high[c : c + 1]], 0
        )
        ext[c, rows : rows + sy] = jnp.where(x_high, odd, even)
        ext[c, rows + sy : used] = jnp.where(x_high, even, odd)
        ext[c, used : used + 8] = low[at + 8 : at + 16]
        ext[c, used + 8 : used + 16] = high[at + 8 : at + 16]
        ext[c, used + 16 :] = jnp.zeros((rows - 2 * sy - 16, sz), F32)
    s_asm = drag[...]
    s_own = mass[...] * (inverse_step + sponge[...].reshape(rows, sz))
    line_weight = line_pattern(W1, (1, sz))
    line_weight_asm = line_pattern(assembled_weights(NODES), (1, sz))
    total = [jnp.zeros((1, sz), F32) for _ in range(4)]
    vs = [jnp.where(keep, ext[c, :rows], 0.0) for c in range(3)]
    wide = jnp.concatenate(
        [jnp.concatenate([vs[c], ext[c, rows:]], 0) for c in range(3)], 1
    )
    planes = mul_left(plane_asm[...], wide)
    us = []
    for c in range(3):
        v = vs[c]
        line = mul_right(v, line_asm[...]) + cross[c]
        stiff = planes[:, c * sz : (c + 1) * sz] * line_weight_asm
        stiff = stiff + line * plane_weight_asm[...]
        u = jnp.where(keep, s_asm * v + viscosity * stiff, 0.0)
        us.append(u)
    planes = mul_left(plane_own[...], jnp.concatenate(us, 1))
    for c in range(3):
        v, u = vs[c], us[c]
        stiff = (
            planes[:, c * sz : (c + 1) * sz] * line_weight
            + mul_right(u, line_own[...]) * plane_weight[...]
        )
        own = s_own * u + viscosity * stiff
        base[c] = v
        image[c] = u
        sv = share[...] * v
        su = share[...] * u
        for k, term in enumerate((sv * v, sv * u, su * u, u * own)):
            total[k] = total[k] + jnp.sum(term, axis=0, keepdims=True)
    spot = lax.broadcasted_iota(jnp.int32, (1, sz), 1)
    out = jnp.zeros((1, sz), F32)
    for k in range(4):
        out = jnp.where(spot == k, jnp.sum(total[k], axis=1, keepdims=True), out)
    sums[...] = jnp.broadcast_to(out, sums.shape)


def combine_kernel(base, image, sums, out):
    total = jnp.sum(sums[...], axis=0, keepdims=True)
    m0, m1, m2, m3 = (total[:, k : k + 1] for k in range(4))
    alpha = m0 / m1
    norm = m0 - 2.0 * alpha * m1 + alpha * alpha * m2
    grow = 1.0 + norm / m0
    bend = grow * grow * m1 - 2.0 * grow * alpha * m2 + alpha * alpha * m3
    alpha2 = norm / bend
    one = alpha + alpha2 * grow
    two = alpha * alpha2
    for c in range(3):
        out[c] = one * base[c] - two * image[c]


VMEM = pl.BlockSpec(memory_space=pltpu.VMEM)
HBM = pl.BlockSpec(memory_space=pltpu.HBM)


def call(kernel, operands, outs, fetch=False, scratch=()):
    shapes = [jax.ShapeDtypeStruct(s, F32) for s in outs]
    size = sum(4 * int(np.prod(s)) for s in outs) + sum(
        o.dtype.itemsize * o.size for o in operands
    )
    if fetch:
        operands = [pltpu.with_memory_space_constraint(o, pltpu.HBM) for o in operands]
    return pl.pallas_call(
        kernel,
        out_shape=shapes,
        in_specs=[HBM if fetch else VMEM] * len(operands),
        out_specs=[VMEM] * len(outs),
        scratch_shapes=[pltpu.VMEM(o.shape, o.dtype) for o in operands]
        + [pltpu.SemaphoreType.DMA((len(operands),))]
        if fetch
        else [pltpu.VMEM(s, F32) for s in scratch],
        compiler_params=pltpu.CompilerParams(vmem_limit_bytes=16 * 1024 * 1024),
        cost_estimate=pl.CostEstimate(
            flops=1_000_000, bytes_accessed=size, transcendentals=0
        ),
    )(*operands)


def pairs_of(count, start):
    return [((start + 2 * m) % count, (start + 2 * m + 1) % count) for m in range(count // 2)]


def groups_of(x_pairs, z_pairs, width):
    return [[x * width + z for x in xs for z in zs] for xs in x_pairs for zs in z_pairs]


def body(adjoint_state, base_flow, base_grads, sponge):
    _, sx, sy, sz = adjoint_state.shape
    rows = sx * sy
    size = 2 * rows
    used = rows + 2 * sy
    counts = {axis: lax.axis_size(axis) for axis in ("gx", "gy", "gz")}
    wx, wy, wz = W1, np.tile(W1, sy // NODES), np.tile(W1, sz // NODES)
    ax, ay = assembled_weights(sx), assembled_weights(sy)

    def f32(x):
        return jnp.asarray(x.astype(np.float32))

    def over_plane(x, y):
        return f32(np.broadcast_to(np.kron(x, y)[:, None], (rows, sz)))

    mass = f32(np.kron(wx, wy)[:, None] * wz[None, :])
    ends = np.ones(NODES)
    ends[0] = ends[-1] = 0.5
    share = f32(
        np.kron(ends, np.tile(ends, sy // NODES))[:, None]
        * np.tile(ends, sz // NODES)[None, :]
    )
    dy = jnp.asarray(left_operand(block_diag(D1, rows // NODES)))
    dz = jnp.asarray(right_operand(block_diag(D1, sz // NODES).T))
    pick = np.zeros((8, sz))
    pick[0, sz - 1] = 1.0
    pick[1, sz - 8 : sz - 1] = K1[7, :7]
    pick[2, 0] = 1.0
    pick[3, 1:8] = K1[0, 1:]
    pick = jnp.asarray(left_operand(pick))
    place = np.zeros((8, 2 * sz))
    place[0, 0] = place[1, sz] = place[2, sz - 1] = place[3, 2 * sz - 1] = 1.0
    place = jnp.asarray(np.tile(place, (3, 1)).astype(np.float32).astype(BF16))
    nx, ny, nz = counts["gx"], counts["gy"], counts["gz"]

    def exchange(slots, start):
        groups = groups_of(pairs_of(nx, start), pairs_of(nz, start), nz)
        return lax.all_to_all(
            slots, ("gx", "gz"), 0, 0, tiled=True, axis_index_groups=groups
        )

    block, plane = (3, rows, sz), (rows, sz)
    field, drag, slots = call(
        forcing_kernel,
        (adjoint_state, base_flow, base_grads, sponge, mass, dy, dz, pick),
        [block, plane, (4, 64, sz)],
        fetch=True,
    )
    got = exchange(slots, 0)
    field, drag, cross, slots = call(
        functools.partial(second_kernel, nx),
        (field, drag, got, pick, place),
        [block, plane, block, (4, 7 * sy, sz)],
    )
    got = exchange(slots, 1)
    field, drag, cross, bend, slots = call(
        functools.partial(third_kernel, nx, ny, nz),
        (field, drag, cross, got, place),
        [block, plane, block, (3, sy, sz), (2 * ny, 64, sz)],
    )
    every = [tuple(range(ny))]
    got = lax.all_to_all(
        slots,
        ("gx", "gy"),
        0,
        0,
        tiled=True,
        axis_index_groups=groups_of(pairs_of(nx, 0), every, ny),
    )

    plane_asm = np.zeros((rows, size))
    plane_asm[:, :rows] = np.kron(assembled_stiffness(sx), np.diag(ay)) + np.kron(
        np.diag(ax), assembled_stiffness(sy)
    )
    for y in range(sy):
        plane_asm[y, rows + y] = ay[y]
        plane_asm[rows - sy + y, rows + sy + y] = ay[y]
    for x in range(sx):
        plane_asm[x * sy, used + x] = ax[x]
        plane_asm[x * sy + sy - 1, used + sx + x] = ax[x]
    plane_own = np.kron(K1, np.diag(wy)) + np.kron(
        np.diag(wx), block_diag(K1, sy // NODES)
    )
    slots = counts["gz"]
    base, image, sums = call(
        functools.partial(moments_kernel, counts, sy),
        (
            field,
            drag,
            cross,
            bend,
            sponge,
            got,
            jnp.asarray(left_operand(plane_asm)),
            jnp.asarray(right_operand(assembled_stiffness(sz).T)),
            jnp.asarray(left_operand(plane_own)),
            jnp.asarray(right_operand(block_diag(K1, sz // NODES).T)),
            mass,
            share,
            over_plane(ax, ay),
            over_plane(wx, wy),
        ),
        [block, block, (slots, sz)],
        scratch=[(3, size, sz), plane],
    )
    sums = lax.all_to_all(sums, "gz", 0, 0, tiled=True)
    sums = jnp.sum(sums, axis=0, keepdims=True)
    slots = counts["gx"] * counts["gy"]
    sums = jnp.broadcast_to(sums, (slots, sz))
    sums = lax.all_to_all(sums, ("gx", "gy"), 0, 0, tiled=True)
    (out,) = call(combine_kernel, (base, image, sums), [(3, rows, sz)])
    return out.reshape(3, sx, sy, sz)


def solution(mesh):
    placed = (
        P(None, "gx", "gy", "gz"),
        P(None, "gx", "gy", "gz"),
        P(None, "gx", "gy", "gz"),
        P("gx", "gy", "gz"),
    )
    return jax.shard_map(
        body, mesh=mesh, in_specs=placed, out_specs=P(None, "gx", "gy", "gz"), check_vma=False
    )
```

```python
import functools

import jax
import jax.numpy as jnp
import numpy as np
from jax import lax
from jax.experimental import pallas as pl
from jax.experimental.pallas import tpu as pltpu
from jax.sharding import PartitionSpec as P

inverse_step = 2.0
viscosity = 0.05
F32 = jnp.float32
BF16 = jnp.bfloat16
NODES = 8


def gll_tables():
    degree = 7
    interior = np.array(
        [
            -0.8717401485096066,
            -0.5917001814331423,
            -0.2092992179024789,
            0.2092992179024789,
            0.5917001814331423,
            0.8717401485096066,
        ]
    )
    points = np.concatenate([[-1.0], interior, [1.0]])
    previous = np.ones(8)
    current = points * 1.0
    for degree_now in range(1, degree):
        following = ((2 * degree_now + 1) * points * current - degree_now * previous) / (
            degree_now + 1
        )
        previous = current
        current = following
    weights = 2.0 / (degree * (degree + 1) * current**2)
    matrix = np.zeros((8, 8))
    for row_idx in range(8):
        for col_idx in range(8):
            if row_idx != col_idx:
                matrix[row_idx, col_idx] = current[row_idx] / (
                    current[col_idx] * (points[row_idx] - points[col_idx])
                )
    matrix[0, 0] = -degree * (degree + 1) / 4.0
    matrix[7, 7] = degree * (degree + 1) / 4.0
    return (weights, matrix)


W1, D1 = gll_tables()
W1 = W1.astype(np.float32).astype(np.float64)
D1 = D1.astype(np.float32).astype(np.float64)
K1 = D1.T @ (W1[:, None] * D1)


def block_diag(small, count):
    return np.kron(np.eye(count), small)


def twin_matrix(length):
    out = np.eye(length)
    for i in range(NODES - 1, length - 1, NODES):
        out[i, i + 1] = 1.0
        out[i + 1, i] = 1.0
    return out


def assembled_stiffness(length):
    out = twin_matrix(length) @ block_diag(K1, length // NODES)
    out[0, 0] += K1[7, 7]
    out[-1, -1] += K1[0, 0]
    return out


def assembled_weights(length):
    out = np.tile(W1, length // NODES)
    out[0::NODES] *= 2.0
    out[NODES - 1 :: NODES] *= 2.0
    return out


def halves(matrix):
    high = matrix.astype(np.float32).astype(BF16)
    low = (matrix - high.astype(np.float64)).astype(np.float32).astype(BF16)
    return np.asarray(high), np.asarray(low)


def left_operand(matrix):
    high, low = halves(matrix)
    zero = np.zeros_like(low)
    return np.concatenate(
        [np.concatenate([high, high], 1), np.concatenate([low, zero], 1)], 0
    )


def right_operand(matrix):
    high, low = halves(matrix)
    zero = np.zeros_like(low)
    return np.concatenate(
        [np.concatenate([high, low], 1), np.concatenate([high, zero], 1)], 0
    )


def split(x):
    high = x.astype(BF16)
    low = (x - high.astype(F32)).astype(BF16)
    return high, low


def mul_left(operand, x):
    rows = operand.shape[0] // 2
    high, low = split(x)
    out = jnp.dot(operand, jnp.concatenate([high, low], 0), preferred_element_type=F32)
    return out[:rows] + out[rows:]


def mul_right(x, operand):
    cols = operand.shape[1] // 2
    high, low = split(x)
    out = jnp.dot(jnp.concatenate([high, low], 1), operand, preferred_element_type=F32)
    return out[:, :cols] + out[:, cols:]


def twin_z(x):
    length = x.shape[-1]
    lane = lax.broadcasted_iota(jnp.int32, x.shape, 1)
    after = pltpu.roll(x, length - 1, 1)
    before = pltpu.roll(x, 1, 1)
    spot = lane & (NODES - 1)
    upper = (spot == NODES - 1) & (lane != length - 1)
    lower = (spot == 0) & (lane != 0)
    return x + jnp.where(upper, after, 0.0) + jnp.where(lower, before, 0.0)


def twin_y(x):
    first, second = x[:, :8], x[:, 8:]
    row = lax.broadcasted_iota(jnp.int32, first.shape, 1)
    one = first + jnp.where(row == 7, second[:, 0:1], 0.0)
    two = second + jnp.where(row == 0, first[:, 7:8], 0.0)
    return jnp.concatenate([one, two], 1)


def member(axis):
    return (lax.axis_index(axis) & 1) == 0


def has_neighbour(axis, high, count):
    here = lax.axis_index(axis)
    return jnp.where(high, here < count - 1, here > 0)


def slot_of(x, z):
    return 2 * x + z


def as_number(flag):
    return jnp.where(flag, 1, 0)


def turned(pick, tile):
    count = pick.shape[0] // 2
    out = lax.dot_general(
        pick,
        jnp.concatenate(split(tile), 1),
        (((1,), (1,)), ((), ())),
        preferred_element_type=F32,
    )
    return out[:count] + out[count:]


def spread(tiles, place):
    both = jnp.concatenate(tiles, 1)
    high = both.astype(BF16)
    rest = both - high.astype(F32)
    mid = rest.astype(BF16)
    low = (rest - mid.astype(F32)).astype(BF16)
    parts = jnp.concatenate([high, mid, low], 0)
    return lax.dot_general(
        parts, place, (((0,), (0,)), ((), ())), preferred_element_type=F32
    )


def picked(tile, high, ok):
    row = lax.broadcasted_iota(jnp.int32, tile.shape, 0)
    start = jnp.where(high, 2, 0)
    use = (row >= start) & (row < start + 2) & ok
    return jnp.where(use, tile, 0.0)


def face_of(x, high, size):
    return jnp.where(high, x[-size:], x[:size])


def corner_at(packed, c, x_high, size, rows):
    start = jnp.where(x_high, rows - size, 0)
    moved = pltpu.roll(packed, lax.rem(start + rows - c * size, rows), 1)
    lane = lax.broadcasted_iota(jnp.int32, packed.shape, 1)
    return jnp.where((lane >= start) & (lane < start + size), moved, 0.0)


def facing(face, high, rows):
    gap = jnp.zeros((rows - face.shape[0], face.shape[1]), F32)
    return jnp.where(
        high, jnp.concatenate([face, gap], 0), jnp.concatenate([gap, face], 0)
    )


def contraction(x, high, size, nx):
    ix = lax.axis_index("gx")
    count = x.shape[0] // size
    total = None
    for i in range(count):
        upper = 0.0 if i == count - 1 else float(K1[7, i])
        lower = 0.0 if i == 0 else float(K1[0, i])
        scale = jnp.where(high, upper, lower).astype(F32)
        if i == 0:
            scale = jnp.where(ix == 0, 0.0, scale)
        if i == count - 1:
            scale = jnp.where(ix == nx - 1, 0.0, scale)
        term = scale * x[i * size : (i + 1) * size]
        total = term if total is None else total + term
    return total


def forcing_kernel(
    adj_hbm,
    flow_hbm,
    grads_hbm,
    sponge_hbm,
    mass_hbm,
    dy_hbm,
    dz_hbm,
    pick_hbm,
    field,
    drag,
    slots,
    adj,
    flow,
    grads,
    sponge,
    mass,
    dy,
    dz,
    pick,
    sems,
):
    copies = [
        pltpu.make_async_copy(src, dst, sems.at[k])
        for k, (src, dst) in enumerate(
            (
                (adj_hbm, adj),
                (dz_hbm, dz),
                (grads_hbm, grads),
                (flow_hbm, flow),
                (dy_hbm, dy),
                (sponge_hbm, sponge),
                (mass_hbm, mass),
                (pick_hbm, pick),
            )
        )
    ]
    for copy in copies:
        copy.start()
    slots[...] = jnp.zeros(slots.shape, F32)
    copies[0].wait()
    a = adj[...]
    _, sx, sy, sz = a.shape
    rows = sx * sy
    copies[1].wait()
    grad_z = mul_right(a.reshape(3 * rows, sz), dz[...]).reshape(3, rows, sz)
    for copy in copies[2:]:
        copy.wait()
    m = mass[...]
    s_local = m * (inverse_step + sponge[...].reshape(rows, sz))
    s_asm = twin_z(twin_y(s_local.reshape(sx, sy, sz)).reshape(rows, sz))
    drag[...] = s_asm
    fl = [flow[j].astype(F32).reshape(rows, sz) for j in range(3)]
    flat = a.reshape(3, rows, sz)
    blocks = []
    for c in range(3):
        grad_y = mul_left(dy[...], flat[c])
        planes = [a[c, i] for i in range(sx)]
        grad_x = []
        for i in range(sx):
            total = float(D1[i, 0]) * planes[0]
            for k in range(1, sx):
                total = total + float(D1[i, k]) * planes[k]
            grad_x.append(total)
        grad_x = jnp.concatenate(grad_x, 0)
        local = inverse_step * flat[c]
        local = local + fl[0] * grad_x + fl[1] * grad_y + fl[2] * grad_z[c]
        for j in range(3):
            local = local - grads[3 * c + j].astype(F32).reshape(rows, sz) * flat[j]
        local = m * local
        out = twin_z(twin_y(local.reshape(sx, sy, sz)).reshape(rows, sz))
        field[c] = out
        blocks.append(out)
    blocks.append(s_asm)
    x_high, z_high = member("gx"), member("gz")
    mx, mz = 1 - as_number(x_high), 1 - as_number(z_high)
    faces = []
    for c, block in enumerate(blocks):
        face = face_of(block, x_high, sy)
        slots[slot_of(1 - mx, mz), c * sy : (c + 1) * sy] = face
        slots[slot_of(mx, 1 - mz), c * 8 : (c + 1) * 8] = turned(pick[...], block)
        faces.append(face)
    faces.append(jnp.zeros((rows - 4 * sy, sz), F32))
    slots[slot_of(1 - mx, 1 - mz), 0:8] = turned(pick[...], jnp.concatenate(faces, 0))


def join(blocks, got, place, x_high, z_high, x_ok, z_ok, sy, bends=False):
    mx, mz = 1 - as_number(x_high), 1 - as_number(z_high)
    rows = blocks[0].shape[0]
    sz = blocks[0].shape[1]
    count = len(blocks)
    tiles = []
    packed = picked(got[slot_of(1 - mx, 1 - mz), 0:8], z_high, z_ok & x_ok)
    for c in range(count):
        tile = picked(got[slot_of(mx, 1 - mz), c * 8 : (c + 1) * 8], z_high, z_ok)
        tiles.append(tile + corner_at(packed, c, x_high, sy, rows))
    if bends:
        tiles.append(pltpu.roll(packed, rows - count * sy, 1))
    add = spread(tiles, place)
    out, cross = [], []
    for c in range(count):
        face = got[slot_of(1 - mx, mz), c * sy : (c + 1) * sy]
        face = jnp.where(x_ok, face, 0.0)
        part = add[c * rows : (c + 1) * rows]
        out.append(
            blocks[c] + facing(face, jnp.logical_not(x_high), rows) + part[:, :sz]
        )
        cross.append(part[:, sz:])
    return out, cross, add[count * rows :, :sz]


def second_kernel(
    nx, field, drag, got, pick, place, field_out, drag_out, cross_out, slots
):
    rows = drag.shape[0]
    sy = rows // NODES
    x_high, z_high = member("gx"), member("gz")
    blocks = [field[0], field[1], field[2], drag[...]]
    blocks, cross, _ = join(blocks, got, place[...], x_high, z_high, True, True, sy)
    slots[...] = jnp.zeros(slots.shape, F32)
    x_high, z_high = jnp.logical_not(x_high), jnp.logical_not(z_high)
    mx, mz = 1 - as_number(x_high), 1 - as_number(z_high)
    faces, bends = [], []
    for c, block in enumerate(blocks):
        face = face_of(block, x_high, sy)
        slots[slot_of(1 - mx, mz), c * sy : (c + 1) * sy] = face
        slots[slot_of(mx, 1 - mz), c * 8 : (c + 1) * 8] = turned(pick[...], block)
        faces.append(face)
        if c < 3:
            field_out[c] = block
            cross_out[c] = cross[c]
            bend = contraction(block, x_high, sy, nx) + face_of(cross[c], x_high, sy)
            slots[slot_of(1 - mx, mz), (4 + c) * sy : (5 + c) * sy] = bend
            bends.append(bend)
        else:
            drag_out[...] = block
    gap = jnp.zeros((rows - 7 * sy, drag.shape[1]), F32)
    slots[slot_of(1 - mx, 1 - mz), 0:8] = turned(
        pick[...], jnp.concatenate(faces + bends + [gap], 0)
    )


def third_kernel(
    nx,
    ny,
    nz,
    field,
    drag,
    cross,
    got,
    place,
    field_out,
    drag_out,
    cross_out,
    bend_out,
    slots,
):
    rows, sz = drag.shape
    sx = NODES
    sy = rows // sx
    x_high, z_high = jnp.logical_not(member("gx")), jnp.logical_not(member("gz"))
    x_ok = has_neighbour("gx", x_high, nx)
    z_ok = has_neighbour("gz", z_high, nz)
    mx, mz = 1 - as_number(x_high), 1 - as_number(z_high)
    blocks = [field[0], field[1], field[2], drag[...]]
    blocks, add, bend_add = join(
        blocks, got, place[...], x_high, z_high, x_ok, z_ok, sy, bends=True
    )
    partner = slot_of(1 - mx, mz)
    drag_out[...] = blocks[3]
    slots[...] = jnp.zeros(slots.shape, F32)
    x_high = jnp.logical_not(x_high)
    mx = 1 - as_number(x_high)
    j = lax.axis_index("gy")
    above = mx * ny + jnp.minimum(j + 1, ny - 1)
    below = mx * ny + jnp.maximum(j - 1, 0)
    beside = (1 - mx) * ny + j
    beside_above = (1 - mx) * ny + jnp.minimum(j + 1, ny - 1)
    beside_below = (1 - mx) * ny + jnp.maximum(j - 1, 0)
    top, bottom = sy - 1, 0
    for c in range(3):
        field_out[c] = blocks[c]
        cross_out[c] = cross[c] + add[c]
        bend = jnp.where(x_ok, got[partner, (4 + c) * sy : (5 + c) * sy], 0.0)
        bend = bend + bend_add[c * sy : (c + 1) * sy]
        bend_out[c] = bend
        own = contraction(blocks[c], x_high, sy, nx)
        slots[beside, c * sy : (c + 1) * sy] = own
        slots[beside_above, 48 + c : 49 + c] = own[top:]
        slots[beside_below, 48 + c : 49 + c] = own[:1]

        def row(ref, y):
            return ref[c, pl.ds(y, sx, stride=sy), :]

        up = row(cross_out, top)
        for k in range(7):
            up = up + float(K1[7, k]) * row(field_out, sy - 8 + k)
        down = row(cross_out, bottom)
        for k in range(1, 8):
            down = down + float(K1[0, k]) * row(field_out, k)
        slots[above, c * 16 : c * 16 + 8] = row(field_out, top)
        slots[above, c * 16 + 8 : c * 16 + 16] = up
        slots[above, 56 + c : 57 + c] = bend[top:]
        slots[below, c * 16 : c * 16 + 8] = row(field_out, bottom)
        slots[below, c * 16 + 8 : c * 16 + 16] = down
        slots[below, 56 + c : 57 + c] = bend[:1]
    slots[above, 48:56] = drag_out[pl.ds(top, sx, stride=sy), :]
    slots[below, 48:56] = drag_out[pl.ds(bottom, sx, stride=sy), :]


def keep_mask(shape, sy, counts):
    row = lax.broadcasted_iota(jnp.int32, shape, 0)
    z = lax.broadcasted_iota(jnp.int32, shape, 1)
    shift = sy.bit_length() - 1
    x = lax.shift_right_logical(row, shift)
    y = row & (sy - 1)
    sx = shape[0] // sy
    mask = None
    for axis, spot, size in (("gx", x, sx), ("gy", y, sy), ("gz", z, shape[1])):
        here = spot + lax.axis_index(axis) * size
        inside = (here != 0) & (here != counts[axis] * size - 1)
        mask = inside if mask is None else mask & inside
    return mask


def line_pattern(values, shape):
    spot = lax.broadcasted_iota(jnp.int32, shape, 1) & (NODES - 1)
    out = jnp.full(shape, float(values[0]), F32)
    for k in range(1, NODES):
        out = jnp.where(spot == k, float(values[k]), out)
    return out


def moments_kernel(
    counts,
    sy,
    field,
    drag_in,
    cross,
    bend_odd,
    sponge,
    got,
    plane_asm,
    line_asm,
    plane_own,
    line_own,
    mass,
    share,
    plane_weight_asm,
    plane_weight,
    base,
    image,
    sums,
    ext,
    drag,
):
    rows, sz = drag.shape
    sx = rows // sy
    ny = counts["gy"]
    keep = keep_mask((rows, sz), sy, counts)
    x_high = member("gx")
    mx = 1 - as_number(x_high)
    j = lax.axis_index("gy")
    low_ok, high_ok = j > 0, j < ny - 1
    below = jnp.maximum(j - 1, 0)
    above = jnp.minimum(j + 1, ny - 1)
    low = jnp.where(low_ok, got[mx * ny + below], 0.0)
    high = jnp.where(high_ok, got[mx * ny + above], 0.0)
    beside_low = jnp.where(low_ok, got[(1 - mx) * ny + below, 48:56], 0.0)
    beside_high = jnp.where(high_ok, got[(1 - mx) * ny + above, 48:56], 0.0)
    bottom, top = pl.ds(0, sx, stride=sy), pl.ds(sy - 1, sx, stride=sy)
    drag[...] = drag_in[...]
    drag[bottom, :] = drag_in[bottom, :] + low[48:56]
    drag[top, :] = drag_in[top, :] + high[48:56]
    used = rows + 2 * sy
    gap = jnp.zeros((sy - 2, sz), F32)
    for c in range(3):
        at = 16 * c
        ext[c, :rows] = field[c]
        ext[c, bottom, :] = field[c, bottom, :] + low[at : at + 8]
        ext[c, top, :] = field[c, top, :] + high[at : at + 8]
        odd = bend_odd[c] + jnp.concatenate(
            [low[56 + c : 57 + c], gap, high[56 + c : 57 + c]], 0
        )
        even = got[(1 - mx) * ny + j, c * sy : (c + 1) * sy] + jnp.concatenate(
            [beside_low[c : c + 1], gap, beside_high[c : c + 1]], 0
        )
        ext[c, rows : rows + sy] = jnp.where(x_high, odd, even)
        ext[c, rows + sy : used] = jnp.where(x_high, even, odd)
        ext[c, used : used + 8] = low[at + 8 : at + 16]
        ext[c, used + 8 : used + 16] = high[at + 8 : at + 16]
        ext[c, used + 16 :] = jnp.zeros((rows - 2 * sy - 16, sz), F32)
    s_asm = drag[...]
    s_own = mass[...] * (inverse_step + sponge[...].reshape(rows, sz))
    line_weight = line_pattern(W1, (1, sz))
    line_weight_asm = line_pattern(assembled_weights(NODES), (1, sz))
    total = [jnp.zeros((1, sz), F32) for _ in range(4)]
    vs = [jnp.where(keep, ext[c, :rows], 0.0) for c in range(3)]
    wide = jnp.concatenate(
        [jnp.concatenate([vs[c], ext[c, rows:]], 0) for c in range(3)], 1
    )
    planes = mul_left(plane_asm[...], wide)
    us = []
    for c in range(3):
        v = vs[c]
        line = mul_right(v, line_asm[...]) + cross[c]
        stiff = planes[:, c * sz : (c + 1) * sz] * line_weight_asm
        stiff = stiff + line * plane_weight_asm[...]
        u = jnp.where(keep, s_asm * v + viscosity * stiff, 0.0)
        us.append(u)
    planes = mul_left(plane_own[...], jnp.concatenate(us, 1))
    for c in range(3):
        v, u = vs[c], us[c]
        stiff = (
            planes[:, c * sz : (c + 1) * sz] * line_weight
            + mul_right(u, line_own[...]) * plane_weight[...]
        )
        own = s_own * u + viscosity * stiff
        base[c] = v
        image[c] = u
        sv = share[...] * v
        su = share[...] * u
        for k, term in enumerate((sv * v, sv * u, su * u, u * own)):
            total[k] = total[k] + jnp.sum(term, axis=0, keepdims=True)
    spot = lax.broadcasted_iota(jnp.int32, (1, sz), 1)
    out = jnp.zeros((1, sz), F32)
    for k in range(4):
        out = jnp.where(spot == k, jnp.sum(total[k], axis=1, keepdims=True), out)
    sums[...] = jnp.broadcast_to(out, sums.shape)


def combine_kernel(base, image, sums, out):
    total = jnp.sum(sums[...], axis=0, keepdims=True)
    m0, m1, m2, m3 = (total[:, k : k + 1] for k in range(4))
    alpha = m0 / m1
    norm = m0 - 2.0 * alpha * m1 + alpha * alpha * m2
    grow = 1.0 + norm / m0
    bend = grow * grow * m1 - 2.0 * grow * alpha * m2 + alpha * alpha * m3
    alpha2 = norm / bend
    one = alpha + alpha2 * grow
    two = alpha * alpha2
    for c in range(3):
        out[c] = one * base[c] - two * image[c]


VMEM = pl.BlockSpec(memory_space=pltpu.VMEM)
HBM = pl.BlockSpec(memory_space=pltpu.HBM)


def call(kernel, operands, outs, fetch=False, scratch=()):
    shapes = [jax.ShapeDtypeStruct(s, F32) for s in outs]
    size = sum(4 * int(np.prod(s)) for s in outs) + sum(
        o.dtype.itemsize * o.size for o in operands
    )
    if fetch:
        operands = [pltpu.with_memory_space_constraint(o, pltpu.HBM) for o in operands]
    return pl.pallas_call(
        kernel,
        out_shape=shapes,
        in_specs=[HBM if fetch else VMEM] * len(operands),
        out_specs=[VMEM] * len(outs),
        scratch_shapes=[pltpu.VMEM(o.shape, o.dtype) for o in operands]
        + [pltpu.SemaphoreType.DMA((len(operands),))]
        if fetch
        else [pltpu.VMEM(s, F32) for s in scratch],
        compiler_params=pltpu.CompilerParams(vmem_limit_bytes=16 * 1024 * 1024),
        cost_estimate=pl.CostEstimate(
            flops=1_000_000, bytes_accessed=size, transcendentals=0
        ),
    )(*operands)


def pairs_of(count, start):
    return [((start + 2 * m) % count, (start + 2 * m + 1) % count) for m in range(count // 2)]


def groups_of(x_pairs, z_pairs, width):
    return [[x * width + z for x in xs for z in zs] for xs in x_pairs for zs in z_pairs]


def body(adjoint_state, base_flow, base_grads, sponge):
    _, sx, sy, sz = adjoint_state.shape
    rows = sx * sy
    size = 2 * rows
    used = rows + 2 * sy
    counts = {axis: lax.axis_size(axis) for axis in ("gx", "gy", "gz")}
    wx, wy, wz = W1, np.tile(W1, sy // NODES), np.tile(W1, sz // NODES)
    ax, ay = assembled_weights(sx), assembled_weights(sy)

    def f32(x):
        return jnp.asarray(x.astype(np.float32))

    def over_plane(x, y):
        return f32(np.broadcast_to(np.kron(x, y)[:, None], (rows, sz)))

    mass = f32(np.kron(wx, wy)[:, None] * wz[None, :])
    ends = np.ones(NODES)
    ends[0] = ends[-1] = 0.5
    share = f32(
        np.kron(ends, np.tile(ends, sy // NODES))[:, None]
        * np.tile(ends, sz // NODES)[None, :]
    )
    dy = jnp.asarray(left_operand(block_diag(D1, rows // NODES)))
    dz = jnp.asarray(right_operand(block_diag(D1, sz // NODES).T))
    pick = np.zeros((8, sz))
    pick[0, sz - 1] = 1.0
    pick[1, sz - 8 : sz - 1] = K1[7, :7]
    pick[2, 0] = 1.0
    pick[3, 1:8] = K1[0, 1:]
    pick = jnp.asarray(left_operand(pick))
    place = np.zeros((8, 2 * sz))
    place[0, 0] = place[1, sz] = place[2, sz - 1] = place[3, 2 * sz - 1] = 1.0
    place = jnp.asarray(np.tile(place, (3, 1)).astype(np.float32).astype(BF16))
    nx, ny, nz = counts["gx"], counts["gy"], counts["gz"]

    def exchange(slots, start):
        groups = groups_of(pairs_of(nx, start), pairs_of(nz, start), nz)
        return lax.all_to_all(
            slots, ("gx", "gz"), 0, 0, tiled=True, axis_index_groups=groups
        )

    block, plane = (3, rows, sz), (rows, sz)
    field, drag, slots = call(
        forcing_kernel,
        (adjoint_state, base_flow, base_grads, sponge, mass, dy, dz, pick),
        [block, plane, (4, 64, sz)],
        fetch=True,
    )
    got = exchange(slots, 0)
    field, drag, cross, slots = call(
        functools.partial(second_kernel, nx),
        (field, drag, got, pick, place),
        [block, plane, block, (4, 7 * sy, sz)],
    )
    got = exchange(slots, 1)
    field, drag, cross, bend, slots = call(
        functools.partial(third_kernel, nx, ny, nz),
        (field, drag, cross, got, place),
        [block, plane, block, (3, sy, sz), (2 * ny, 64, sz)],
    )
    every = [tuple(range(ny))]
    got = lax.all_to_all(
        slots,
        ("gx", "gy"),
        0,
        0,
        tiled=True,
        axis_index_groups=groups_of(pairs_of(nx, 0), every, ny),
    )

    plane_asm = np.zeros((rows, size))
    plane_asm[:, :rows] = np.kron(assembled_stiffness(sx), np.diag(ay)) + np.kron(
        np.diag(ax), assembled_stiffness(sy)
    )
    for y in range(sy):
        plane_asm[y, rows + y] = ay[y]
        plane_asm[rows - sy + y, rows + sy + y] = ay[y]
    for x in range(sx):
        plane_asm[x * sy, used + x] = ax[x]
        plane_asm[x * sy + sy - 1, used + sx + x] = ax[x]
    plane_own = np.kron(K1, np.diag(wy)) + np.kron(
        np.diag(wx), block_diag(K1, sy // NODES)
    )
    slots = nx * ny
    base, image, sums = call(
        functools.partial(moments_kernel, counts, sy),
        (
            field,
            drag,
            cross,
            bend,
            sponge,
            got,
            jnp.asarray(left_operand(plane_asm)),
            jnp.asarray(right_operand(assembled_stiffness(sz).T)),
            jnp.asarray(left_operand(plane_own)),
            jnp.asarray(right_operand(block_diag(K1, sz // NODES).T)),
            mass,
            share,
            over_plane(ax, ay),
            over_plane(wx, wy),
        ),
        [block, block, (slots, sz)],
        scratch=[(3, size, sz), plane],
    )
    sums = lax.all_to_all(sums, ("gx", "gy"), 0, 0, tiled=True)
    sums = jnp.sum(sums, axis=0, keepdims=True)
    sums = jnp.broadcast_to(sums, (nz, sz))
    sums = lax.all_to_all(sums, "gz", 0, 0, tiled=True)
    (out,) = call(combine_kernel, (base, image, sums), [(3, rows, sz)])
    return out.reshape(3, sx, sy, sz)


def solution(mesh):
    placed = (
        P(None, "gx", "gy", "gz"),
        P(None, "gx", "gy", "gz"),
        P(None, "gx", "gy", "gz"),
        P("gx", "gy", "gz"),
    )
    return jax.shard_map(
        body, mesh=mesh, in_specs=placed, out_specs=P(None, "gx", "gy", "gz"), check_vma=False
    )
```

```python
import functools

import jax
import jax.numpy as jnp
import numpy as np
from jax import lax
from jax.experimental import pallas as pl
from jax.experimental.pallas import tpu as pltpu
from jax.sharding import PartitionSpec as P

inverse_step = 2.0
viscosity = 0.05
F32 = jnp.float32
BF16 = jnp.bfloat16
NODES = 8


def gll_tables():
    degree = 7
    interior = np.array(
        [
            -0.8717401485096066,
            -0.5917001814331423,
            -0.2092992179024789,
            0.2092992179024789,
            0.5917001814331423,
            0.8717401485096066,
        ]
    )
    points = np.concatenate([[-1.0], interior, [1.0]])
    previous = np.ones(8)
    current = points * 1.0
    for degree_now in range(1, degree):
        following = ((2 * degree_now + 1) * points * current - degree_now * previous) / (
            degree_now + 1
        )
        previous = current
        current = following
    weights = 2.0 / (degree * (degree + 1) * current**2)
    matrix = np.zeros((8, 8))
    for row_idx in range(8):
        for col_idx in range(8):
            if row_idx != col_idx:
                matrix[row_idx, col_idx] = current[row_idx] / (
                    current[col_idx] * (points[row_idx] - points[col_idx])
                )
    matrix[0, 0] = -degree * (degree + 1) / 4.0
    matrix[7, 7] = degree * (degree + 1) / 4.0
    return (weights, matrix)


W1, D1 = gll_tables()
W1 = W1.astype(np.float32).astype(np.float64)
D1 = D1.astype(np.float32).astype(np.float64)
K1 = D1.T @ (W1[:, None] * D1)


def block_diag(small, count):
    return np.kron(np.eye(count), small)


def twin_matrix(length):
    out = np.eye(length)
    for i in range(NODES - 1, length - 1, NODES):
        out[i, i + 1] = 1.0
        out[i + 1, i] = 1.0
    return out


def assembled_stiffness(length):
    out = twin_matrix(length) @ block_diag(K1, length // NODES)
    out[0, 0] += K1[7, 7]
    out[-1, -1] += K1[0, 0]
    return out


def assembled_weights(length):
    out = np.tile(W1, length // NODES)
    out[0::NODES] *= 2.0
    out[NODES - 1 :: NODES] *= 2.0
    return out


def halves(matrix):
    high = matrix.astype(np.float32).astype(BF16)
    low = (matrix - high.astype(np.float64)).astype(np.float32).astype(BF16)
    return np.asarray(high), np.asarray(low)


def left_operand(matrix):
    high, low = halves(matrix)
    zero = np.zeros_like(low)
    return np.concatenate(
        [np.concatenate([high, high], 1), np.concatenate([low, zero], 1)], 0
    )


def right_operand(matrix):
    high, low = halves(matrix)
    zero = np.zeros_like(low)
    return np.concatenate(
        [np.concatenate([high, low], 1), np.concatenate([high, zero], 1)], 0
    )


def split(x):
    high = x.astype(BF16)
    low = (x - high.astype(F32)).astype(BF16)
    return high, low


def mul_left(operand, x):
    rows = operand.shape[0] // 2
    high, low = split(x)
    out = jnp.dot(operand, jnp.concatenate([high, low], 0), preferred_element_type=F32)
    return out[:rows] + out[rows:]


def mul_right(x, operand):
    cols = operand.shape[1] // 2
    high, low = split(x)
    out = jnp.dot(jnp.concatenate([high, low], 1), operand, preferred_element_type=F32)
    return out[:, :cols] + out[:, cols:]


def twin_z(x):
    length = x.shape[-1]
    lane = lax.broadcasted_iota(jnp.int32, x.shape, 1)
    after = pltpu.roll(x, length - 1, 1)
    before = pltpu.roll(x, 1, 1)
    spot = lane & (NODES - 1)
    upper = (spot == NODES - 1) & (lane != length - 1)
    lower = (spot == 0) & (lane != 0)
    return x + jnp.where(upper, after, 0.0) + jnp.where(lower, before, 0.0)


def twin_y(x):
    first, second = x[:, :8], x[:, 8:]
    row = lax.broadcasted_iota(jnp.int32, first.shape, 1)
    one = first + jnp.where(row == 7, second[:, 0:1], 0.0)
    two = second + jnp.where(row == 0, first[:, 7:8], 0.0)
    return jnp.concatenate([one, two], 1)


def member(axis):
    return (lax.axis_index(axis) & 1) == 0


def has_neighbour(axis, high, count):
    here = lax.axis_index(axis)
    return jnp.where(high, here < count - 1, here > 0)


def slot_of(x, z):
    return 2 * x + z


def as_number(flag):
    return jnp.where(flag, 1, 0)


def turned(pick, tile):
    count = pick.shape[0] // 2
    out = lax.dot_general(
        pick,
        jnp.concatenate(split(tile), 1),
        (((1,), (1,)), ((), ())),
        preferred_element_type=F32,
    )
    return out[:count] + out[count:]


def spread(tiles, place):
    both = jnp.concatenate(tiles, 1)
    high = both.astype(BF16)
    rest = both - high.astype(F32)
    mid = rest.astype(BF16)
    low = (rest - mid.astype(F32)).astype(BF16)
    parts = jnp.concatenate([high, mid, low], 0)
    return lax.dot_general(
        parts, place, (((0,), (0,)), ((), ())), preferred_element_type=F32
    )


def picked(tile, high, ok):
    row = lax.broadcasted_iota(jnp.int32, tile.shape, 0)
    start = jnp.where(high, 2, 0)
    use = (row >= start) & (row < start + 2) & ok
    return jnp.where(use, tile, 0.0)


def face_of(x, high, size):
    return jnp.where(high, x[-size:], x[:size])


def corner_at(packed, c, x_high, size, rows):
    start = jnp.where(x_high, rows - size, 0)
    moved = pltpu.roll(packed, lax.rem(start + rows - c * size, rows), 1)
    lane = lax.broadcasted_iota(jnp.int32, packed.shape, 1)
    return jnp.where((lane >= start) & (lane < start + size), moved, 0.0)


def facing(face, high, rows):
    gap = jnp.zeros((rows - face.shape[0], face.shape[1]), F32)
    return jnp.where(
        high, jnp.concatenate([face, gap], 0), jnp.concatenate([gap, face], 0)
    )


def contraction(x, high, size, nx):
    ix = lax.axis_index("gx")
    count = x.shape[0] // size
    total = None
    for i in range(count):
        upper = 0.0 if i == count - 1 else float(K1[7, i])
        lower = 0.0 if i == 0 else float(K1[0, i])
        scale = jnp.where(high, upper, lower).astype(F32)
        if i == 0:
            scale = jnp.where(ix == 0, 0.0, scale)
        if i == count - 1:
            scale = jnp.where(ix == nx - 1, 0.0, scale)
        term = scale * x[i * size : (i + 1) * size]
        total = term if total is None else total + term
    return total


def forcing_kernel(
    adj_hbm,
    flow_hbm,
    grads_hbm,
    sponge_hbm,
    mass_hbm,
    dy_hbm,
    dz_hbm,
    pick_hbm,
    field,
    drag,
    slots,
    adj,
    flow,
    grads,
    sponge,
    mass,
    dy,
    dz,
    pick,
    sems,
):
    copies = [
        pltpu.make_async_copy(src, dst, sems.at[k])
        for k, (src, dst) in enumerate(
            (
                (adj_hbm, adj),
                (dz_hbm, dz),
                (grads_hbm, grads),
                (flow_hbm, flow),
                (dy_hbm, dy),
                (sponge_hbm, sponge),
                (mass_hbm, mass),
                (pick_hbm, pick),
            )
        )
    ]
    for copy in copies:
        copy.start()
    slots[...] = jnp.zeros(slots.shape, F32)
    copies[0].wait()
    a = adj[...]
    _, sx, sy, sz = a.shape
    rows = sx * sy
    copies[1].wait()
    grad_z = mul_right(a.reshape(3 * rows, sz), dz[...]).reshape(3, rows, sz)
    for copy in copies[2:]:
        copy.wait()
    m = mass[...]
    s_local = m * (inverse_step + sponge[...].reshape(rows, sz))
    s_asm = twin_z(twin_y(s_local.reshape(sx, sy, sz)).reshape(rows, sz))
    drag[...] = s_asm
    fl = [flow[j].astype(F32).reshape(rows, sz) for j in range(3)]
    flat = a.reshape(3, rows, sz)
    blocks = []
    for c in range(3):
        grad_y = mul_left(dy[...], flat[c])
        planes = [a[c, i] for i in range(sx)]
        grad_x = []
        for i in range(sx):
            total = float(D1[i, 0]) * planes[0]
            for k in range(1, sx):
                total = total + float(D1[i, k]) * planes[k]
            grad_x.append(total)
        grad_x = jnp.concatenate(grad_x, 0)
        local = inverse_step * flat[c]
        local = local + fl[0] * grad_x + fl[1] * grad_y + fl[2] * grad_z[c]
        for j in range(3):
            local = local - grads[3 * c + j].astype(F32).reshape(rows, sz) * flat[j]
        local = m * local
        out = twin_z(twin_y(local.reshape(sx, sy, sz)).reshape(rows, sz))
        field[c] = out
        blocks.append(out)
    blocks.append(s_asm)
    x_high, z_high = member("gx"), member("gz")
    mx, mz = 1 - as_number(x_high), 1 - as_number(z_high)
    faces = []
    for c, block in enumerate(blocks):
        face = face_of(block, x_high, sy)
        slots[slot_of(1 - mx, mz), c * sy : (c + 1) * sy] = face
        slots[slot_of(mx, 1 - mz), c * 8 : (c + 1) * 8] = turned(pick[...], block)
        faces.append(face)
    faces.append(jnp.zeros((rows - 4 * sy, sz), F32))
    slots[slot_of(1 - mx, 1 - mz), 0:8] = turned(pick[...], jnp.concatenate(faces, 0))


def join(blocks, got, place, x_high, z_high, x_ok, z_ok, sy, bends=False):
    mx, mz = 1 - as_number(x_high), 1 - as_number(z_high)
    rows = blocks[0].shape[0]
    sz = blocks[0].shape[1]
    count = len(blocks)
    tiles = []
    packed = picked(got[slot_of(1 - mx, 1 - mz), 0:8], z_high, z_ok & x_ok)
    for c in range(count):
        tile = picked(got[slot_of(mx, 1 - mz), c * 8 : (c + 1) * 8], z_high, z_ok)
        tiles.append(tile + corner_at(packed, c, x_high, sy, rows))
    if bends:
        tiles.append(pltpu.roll(packed, rows - count * sy, 1))
    add = spread(tiles, place)
    out, cross = [], []
    for c in range(count):
        face = got[slot_of(1 - mx, mz), c * sy : (c + 1) * sy]
        face = jnp.where(x_ok, face, 0.0)
        part = add[c * rows : (c + 1) * rows]
        out.append(
            blocks[c] + facing(face, jnp.logical_not(x_high), rows) + part[:, :sz]
        )
        cross.append(part[:, sz:])
    return out, cross, add[count * rows :, :sz]


def second_kernel(
    nx, field, drag, got, pick, place, field_out, drag_out, cross_out, slots
):
    rows = drag.shape[0]
    sy = rows // NODES
    x_high, z_high = member("gx"), member("gz")
    blocks = [field[0], field[1], field[2], drag[...]]
    blocks, cross, _ = join(blocks, got, place[...], x_high, z_high, True, True, sy)
    slots[...] = jnp.zeros(slots.shape, F32)
    x_high, z_high = jnp.logical_not(x_high), jnp.logical_not(z_high)
    mx, mz = 1 - as_number(x_high), 1 - as_number(z_high)
    faces, bends = [], []
    for c, block in enumerate(blocks):
        face = face_of(block, x_high, sy)
        slots[slot_of(1 - mx, mz), c * sy : (c + 1) * sy] = face
        slots[slot_of(mx, 1 - mz), c * 8 : (c + 1) * 8] = turned(pick[...], block)
        faces.append(face)
        if c < 3:
            field_out[c] = block
            cross_out[c] = cross[c]
            bend = contraction(block, x_high, sy, nx) + face_of(cross[c], x_high, sy)
            slots[slot_of(1 - mx, mz), (4 + c) * sy : (5 + c) * sy] = bend
            bends.append(bend)
        else:
            drag_out[...] = block
    gap = jnp.zeros((rows - 7 * sy, drag.shape[1]), F32)
    slots[slot_of(1 - mx, 1 - mz), 0:8] = turned(
        pick[...], jnp.concatenate(faces + bends + [gap], 0)
    )


def third_kernel(
    nx,
    ny,
    nz,
    field,
    drag,
    cross,
    got,
    place,
    field_out,
    drag_out,
    cross_out,
    bend_out,
    slots,
):
    rows, sz = drag.shape
    sx = NODES
    sy = rows // sx
    x_high, z_high = jnp.logical_not(member("gx")), jnp.logical_not(member("gz"))
    x_ok = has_neighbour("gx", x_high, nx)
    z_ok = has_neighbour("gz", z_high, nz)
    mx, mz = 1 - as_number(x_high), 1 - as_number(z_high)
    blocks = [field[0], field[1], field[2], drag[...]]
    blocks, add, bend_add = join(
        blocks, got, place[...], x_high, z_high, x_ok, z_ok, sy, bends=True
    )
    partner = slot_of(1 - mx, mz)
    drag_out[...] = blocks[3]
    slots[...] = jnp.zeros(slots.shape, F32)
    x_high = jnp.logical_not(x_high)
    mx = 1 - as_number(x_high)
    j = lax.axis_index("gy")
    above = mx * ny + jnp.minimum(j + 1, ny - 1)
    below = mx * ny + jnp.maximum(j - 1, 0)
    beside = (1 - mx) * ny + j
    beside_above = (1 - mx) * ny + jnp.minimum(j + 1, ny - 1)
    beside_below = (1 - mx) * ny + jnp.maximum(j - 1, 0)
    top, bottom = sy - 1, 0
    side = lax.broadcasted_iota(jnp.int32, (sx, sz), 0) == jnp.where(x_high, 0, sx - 1)
    for c in range(3):
        field_out[c] = blocks[c]
        cross_out[c] = cross[c] + add[c]
        bend = jnp.where(x_ok, got[partner, (4 + c) * sy : (5 + c) * sy], 0.0)
        bend = bend + bend_add[c * sy : (c + 1) * sy]
        bend_out[c] = bend
        own = contraction(blocks[c], x_high, sy, nx)
        slots[beside, c * sy : (c + 1) * sy] = own
        slots[beside_above, 48 + c : 49 + c] = own[top:]
        slots[beside_below, 48 + c : 49 + c] = own[:1]

        def row(ref, y):
            return ref[c, pl.ds(y, sx, stride=sy), :]

        up = row(cross_out, top)
        for k in range(7):
            up = up + float(K1[7, k]) * row(field_out, sy - 8 + k)
        down = row(cross_out, bottom)
        for k in range(1, 8):
            down = down + float(K1[0, k]) * row(field_out, k)
        up = up + jnp.where(side, bend[top:], 0.0)
        down = down + jnp.where(side, bend[:1], 0.0)
        slots[above, c * 16 : c * 16 + 8] = row(field_out, top)
        slots[above, c * 16 + 8 : c * 16 + 16] = up
        slots[below, c * 16 : c * 16 + 8] = row(field_out, bottom)
        slots[below, c * 16 + 8 : c * 16 + 16] = down
    slots[above, 48:56] = drag_out[pl.ds(top, sx, stride=sy), :]
    slots[below, 48:56] = drag_out[pl.ds(bottom, sx, stride=sy), :]


def keep_mask(shape, sy, counts):
    row = lax.broadcasted_iota(jnp.int32, shape, 0)
    z = lax.broadcasted_iota(jnp.int32, shape, 1)
    shift = sy.bit_length() - 1
    x = lax.shift_right_logical(row, shift)
    y = row & (sy - 1)
    sx = shape[0] // sy
    mask = None
    for axis, spot, size in (("gx", x, sx), ("gy", y, sy), ("gz", z, shape[1])):
        here = spot + lax.axis_index(axis) * size
        inside = (here != 0) & (here != counts[axis] * size - 1)
        mask = inside if mask is None else mask & inside
    return mask


def line_pattern(values, shape):
    spot = lax.broadcasted_iota(jnp.int32, shape, 1) & (NODES - 1)
    out = jnp.full(shape, float(values[0]), F32)
    for k in range(1, NODES):
        out = jnp.where(spot == k, float(values[k]), out)
    return out


def moments_kernel(
    counts,
    sy,
    field,
    drag_in,
    cross,
    bend_odd,
    sponge,
    got,
    plane_asm,
    line_asm,
    plane_own,
    line_own,
    mass,
    share,
    plane_weight_asm,
    plane_weight,
    base,
    image,
    sums,
    ext,
    drag,
):
    rows, sz = drag.shape
    sx = rows // sy
    ny = counts["gy"]
    keep = keep_mask((rows, sz), sy, counts)
    x_high = member("gx")
    mx = 1 - as_number(x_high)
    j = lax.axis_index("gy")
    low_ok, high_ok = j > 0, j < ny - 1
    below = jnp.maximum(j - 1, 0)
    above = jnp.minimum(j + 1, ny - 1)
    low = jnp.where(low_ok, got[mx * ny + below], 0.0)
    high = jnp.where(high_ok, got[mx * ny + above], 0.0)
    beside_low = jnp.where(low_ok, got[(1 - mx) * ny + below, 48:56], 0.0)
    beside_high = jnp.where(high_ok, got[(1 - mx) * ny + above, 48:56], 0.0)
    bottom, top = pl.ds(0, sx, stride=sy), pl.ds(sy - 1, sx, stride=sy)
    drag[...] = drag_in[...]
    drag[bottom, :] = drag_in[bottom, :] + low[48:56]
    drag[top, :] = drag_in[top, :] + high[48:56]
    used = rows + 2 * sy
    gap = jnp.zeros((sy - 2, sz), F32)
    for c in range(3):
        at = 16 * c
        ext[c, :rows] = field[c]
        ext[c, bottom, :] = field[c, bottom, :] + low[at : at + 8]
        ext[c, top, :] = field[c, top, :] + high[at : at + 8]
        odd = bend_odd[c]
        even = got[(1 - mx) * ny + j, c * sy : (c + 1) * sy] + jnp.concatenate(
            [beside_low[c : c + 1], gap, beside_high[c : c + 1]], 0
        )
        ext[c, rows : rows + sy] = jnp.where(x_high, odd, even)
        ext[c, rows + sy : used] = jnp.where(x_high, even, odd)
        ext[c, used : used + 8] = low[at + 8 : at + 16]
        ext[c, used + 8 : used + 16] = high[at + 8 : at + 16]
        ext[c, used + 16 :] = jnp.zeros((rows - 2 * sy - 16, sz), F32)
    s_asm = drag[...]
    s_own = mass[...] * (inverse_step + sponge[...].reshape(rows, sz))
    line_weight = line_pattern(W1, (1, sz))
    line_weight_asm = line_pattern(assembled_weights(NODES), (1, sz))
    total = [jnp.zeros((1, sz), F32) for _ in range(4)]
    vs = [jnp.where(keep, ext[c, :rows], 0.0) for c in range(3)]
    wide = jnp.concatenate(
        [jnp.concatenate([vs[c], ext[c, rows:]], 0) for c in range(3)], 1
    )
    planes = mul_left(plane_asm[...], wide)
    us = []
    for c in range(3):
        v = vs[c]
        line = mul_right(v, line_asm[...]) + cross[c]
        stiff = planes[:, c * sz : (c + 1) * sz] * line_weight_asm
        stiff = stiff + line * plane_weight_asm[...]
        u = jnp.where(keep, s_asm * v + viscosity * stiff, 0.0)
        us.append(u)
    planes = mul_left(plane_own[...], jnp.concatenate(us, 1))
    for c in range(3):
        v, u = vs[c], us[c]
        stiff = (
            planes[:, c * sz : (c + 1) * sz] * line_weight
            + mul_right(u, line_own[...]) * plane_weight[...]
        )
        own = s_own * u + viscosity * stiff
        base[c] = v
        image[c] = u
        sv = share[...] * v
        su = share[...] * u
        for k, term in enumerate((sv * v, sv * u, su * u, u * own)):
            total[k] = total[k] + jnp.sum(term, axis=0, keepdims=True)
    spot = lax.broadcasted_iota(jnp.int32, (1, sz), 1)
    out = jnp.zeros((1, sz), F32)
    for k in range(4):
        out = jnp.where(spot == k, jnp.sum(total[k], axis=1, keepdims=True), out)
    sums[...] = jnp.broadcast_to(out, sums.shape)


def combine_kernel(base, image, sums, out):
    total = jnp.sum(sums[...], axis=0, keepdims=True)
    m0, m1, m2, m3 = (total[:, k : k + 1] for k in range(4))
    alpha = m0 / m1
    norm = m0 - 2.0 * alpha * m1 + alpha * alpha * m2
    grow = 1.0 + norm / m0
    bend = grow * grow * m1 - 2.0 * grow * alpha * m2 + alpha * alpha * m3
    alpha2 = norm / bend
    one = alpha + alpha2 * grow
    two = alpha * alpha2
    for c in range(3):
        out[c] = one * base[c] - two * image[c]


VMEM = pl.BlockSpec(memory_space=pltpu.VMEM)
HBM = pl.BlockSpec(memory_space=pltpu.HBM)


def call(kernel, operands, outs, fetch=False, scratch=()):
    shapes = [jax.ShapeDtypeStruct(s, F32) for s in outs]
    size = sum(4 * int(np.prod(s)) for s in outs) + sum(
        o.dtype.itemsize * o.size for o in operands
    )
    if fetch:
        operands = [pltpu.with_memory_space_constraint(o, pltpu.HBM) for o in operands]
    return pl.pallas_call(
        kernel,
        out_shape=shapes,
        in_specs=[HBM if fetch else VMEM] * len(operands),
        out_specs=[VMEM] * len(outs),
        scratch_shapes=[pltpu.VMEM(o.shape, o.dtype) for o in operands]
        + [pltpu.SemaphoreType.DMA((len(operands),))]
        if fetch
        else [pltpu.VMEM(s, F32) for s in scratch],
        compiler_params=pltpu.CompilerParams(vmem_limit_bytes=16 * 1024 * 1024),
        cost_estimate=pl.CostEstimate(
            flops=1_000_000, bytes_accessed=size, transcendentals=0
        ),
    )(*operands)


def pairs_of(count, start):
    return [((start + 2 * m) % count, (start + 2 * m + 1) % count) for m in range(count // 2)]


def groups_of(x_pairs, z_pairs, width):
    return [[x * width + z for x in xs for z in zs] for xs in x_pairs for zs in z_pairs]


def body(adjoint_state, base_flow, base_grads, sponge):
    _, sx, sy, sz = adjoint_state.shape
    rows = sx * sy
    size = 2 * rows
    used = rows + 2 * sy
    counts = {axis: lax.axis_size(axis) for axis in ("gx", "gy", "gz")}
    wx, wy, wz = W1, np.tile(W1, sy // NODES), np.tile(W1, sz // NODES)
    ax, ay = assembled_weights(sx), assembled_weights(sy)

    def f32(x):
        return jnp.asarray(x.astype(np.float32))

    def over_plane(x, y):
        return f32(np.broadcast_to(np.kron(x, y)[:, None], (rows, sz)))

    mass = f32(np.kron(wx, wy)[:, None] * wz[None, :])
    ends = np.ones(NODES)
    ends[0] = ends[-1] = 0.5
    share = f32(
        np.kron(ends, np.tile(ends, sy // NODES))[:, None]
        * np.tile(ends, sz // NODES)[None, :]
    )
    dy = jnp.asarray(left_operand(block_diag(D1, rows // NODES)))
    dz = jnp.asarray(right_operand(block_diag(D1, sz // NODES).T))
    pick = np.zeros((8, sz))
    pick[0, sz - 1] = 1.0
    pick[1, sz - 8 : sz - 1] = K1[7, :7]
    pick[2, 0] = 1.0
    pick[3, 1:8] = K1[0, 1:]
    pick = jnp.asarray(left_operand(pick))
    place = np.zeros((8, 2 * sz))
    place[0, 0] = place[1, sz] = place[2, sz - 1] = place[3, 2 * sz - 1] = 1.0
    place = jnp.asarray(np.tile(place, (3, 1)).astype(np.float32).astype(BF16))
    nx, ny, nz = counts["gx"], counts["gy"], counts["gz"]

    def exchange(slots, start):
        groups = groups_of(pairs_of(nx, start), pairs_of(nz, start), nz)
        return lax.all_to_all(
            slots, ("gx", "gz"), 0, 0, tiled=True, axis_index_groups=groups
        )

    block, plane = (3, rows, sz), (rows, sz)
    field, drag, slots = call(
        forcing_kernel,
        (adjoint_state, base_flow, base_grads, sponge, mass, dy, dz, pick),
        [block, plane, (4, 64, sz)],
        fetch=True,
    )
    got = exchange(slots, 0)
    field, drag, cross, slots = call(
        functools.partial(second_kernel, nx),
        (field, drag, got, pick, place),
        [block, plane, block, (4, 7 * sy, sz)],
    )
    got = exchange(slots, 1)
    field, drag, cross, bend, slots = call(
        functools.partial(third_kernel, nx, ny, nz),
        (field, drag, cross, got, place),
        [block, plane, block, (3, sy, sz), (2 * ny, 56, sz)],
    )
    every = [tuple(range(ny))]
    got = lax.all_to_all(
        slots,
        ("gx", "gy"),
        0,
        0,
        tiled=True,
        axis_index_groups=groups_of(pairs_of(nx, 0), every, ny),
    )

    plane_asm = np.zeros((rows, size))
    plane_asm[:, :rows] = np.kron(assembled_stiffness(sx), np.diag(ay)) + np.kron(
        np.diag(ax), assembled_stiffness(sy)
    )
    for y in range(sy):
        plane_asm[y, rows + y] = ay[y]
        plane_asm[rows - sy + y, rows + sy + y] = ay[y]
    for x in range(sx):
        plane_asm[x * sy, used + x] = ax[x]
        plane_asm[x * sy + sy - 1, used + sx + x] = ax[x]
    plane_own = np.kron(K1, np.diag(wy)) + np.kron(
        np.diag(wx), block_diag(K1, sy // NODES)
    )
    slots = counts["gz"]
    base, image, sums = call(
        functools.partial(moments_kernel, counts, sy),
        (
            field,
            drag,
            cross,
            bend,
            sponge,
            got,
            jnp.asarray(left_operand(plane_asm)),
            jnp.asarray(right_operand(assembled_stiffness(sz).T)),
            jnp.asarray(left_operand(plane_own)),
            jnp.asarray(right_operand(block_diag(K1, sz // NODES).T)),
            mass,
            share,
            over_plane(ax, ay),
            over_plane(wx, wy),
        ),
        [block, block, (slots, sz)],
        scratch=[(3, size, sz), plane],
    )
    sums = lax.all_to_all(sums, "gz", 0, 0, tiled=True)
    sums = jnp.sum(sums, axis=0, keepdims=True)
    slots = counts["gx"] * counts["gy"]
    sums = jnp.broadcast_to(sums, (slots, sz))
    sums = lax.all_to_all(sums, ("gx", "gy"), 0, 0, tiled=True)
    (out,) = call(combine_kernel, (base, image, sums), [(3, rows, sz)])
    return out.reshape(3, sx, sy, sz)


def solution(mesh):
    placed = (
        P(None, "gx", "gy", "gz"),
        P(None, "gx", "gy", "gz"),
        P(None, "gx", "gy", "gz"),
        P("gx", "gy", "gz"),
    )
    return jax.shard_map(
        body, mesh=mesh, in_specs=placed, out_specs=P(None, "gx", "gy", "gz"), check_vma=False
    )
```
